32 devices in a mesh: dp: 8 (over z, x), tensor: 4 (over y, core).
Axes of the slice: x: 2, y: 2, z: 4, core: 2. Of those that a mesh axis runs over, the one named last changes fastest.
Arguments:
- inputs: bfloat16 [16384, 768], P(('dp', 'tensor')), may hold values from -6 to 6
- segment_ids: int32 [16384], P('dp'), may hold values from 0 to 39, never falling along the last dimension, each value on 1 to 800 neighbouring positions
- keep_mask: int32 [16384], P('dp'), may hold values from 0 to 1, as said below
- timestep: int32 [8], P('dp'), may hold values from 0 to 1999
- w_qkv: bfloat16 [3, 768, 768], P(None, 'dp', 'tensor'), may hold values from -0.21875 to 0.21875
- b_query: float32 [768], P('tensor'), may hold values from -3 to 3
- b_value: float32 [768], P('tensor'), may hold values from -0.6 to 0.6
- w_out: bfloat16 [768, 768], P('tensor', 'dp'), may hold values from -1.75 to 1.75
- w_up: bfloat16 [768, 3072], P('dp', 'tensor'), may hold values from -0.21875 to 0.21875
- b_up: float32 [3072], P('tensor'), may hold values from -3 to 3
- w_down: bfloat16 [3072, 768], P('tensor', 'dp'), may hold values from -0.109375 to 0.109375
- time_weight: bfloat16 [128, 768], P(None, 'dp'), may hold values from -0.5 to 0.5
- gains: float32 [2, 768], replicated, may hold values from 0.1 to 1.9
- row_biases: float32 [5, 768], replicated, may hold values from -1.8 to 1.8
- d_out: bfloat16 [16384, 768], P(('dp', 'tensor')), may hold values from -6 to 6
Outputs:
- output: bfloat16 [16384, 768], P(('dp', 'tensor'))
- grad_input: float32 [16384, 768], P(('dp', 'tensor'))
- grad_qkv: float32 [3, 768, 768], P(None, 'dp', 'tensor')
- grad_query_bias: float32 [768], P('tensor')
- grad_value_bias: float32 [768], P('tensor')
- grad_out: float32 [768, 768], P('tensor', 'dp')
- grad_up: float32 [768, 3072], P('dp', 'tensor')
- grad_up_bias: float32 [3072], P('tensor')
- grad_down: float32 [3072, 768], P('tensor', 'dp')
- grad_time: float32 [128, 768], P(None, 'dp')
- grad_gains: float32 [2, 768], replicated
- grad_biases: float32 [5, 768], replicated
The draws below stay inside these ranges and needn't reach their ends.
Inputs may be any that keep to these rules, and one draw needn't show every extreme that they name: Within each sequence of 2048 tokens the zeros of keep_mask form a tail at its end, of 0 to 512 tokens. segment_ids never decrease along the tokens; one document has at most 800 tokens.
All inputs are finite; a program needn't handle non-finite values.
Results may differ from the reference program's by a relative error of at most 0.012.
Values may be sent and summed in bfloat16 or wider, within the bound.
No kernel may reach another device: no remote copies, remote signals or barrier semaphores. Data moves between devices by JAX's collectives and lax.ppermute only.
A program may use at most 192 MiB of HBM per device.

```python
import math
import jax
import jax.numpy as jnp
import numpy as np
from jax import lax

D = 768
HEADS = 12
HEAD = 64
FF = 3072
TE = 128
SEQ_LEN = 2048
DOC_MOST = 800
SEQS = 8
TOKENS = 16384


def draw_keep_mask(key, part):
    padding = jax.random.randint(key, (SEQS,), 0, SEQ_LEN // 4 + 1)
    places = jnp.arange(SEQ_LEN)
    kept_flags = places[None, :] < (SEQ_LEN - padding)[:, None]
    return kept_flags.astype(jnp.int32).reshape(SEQS * SEQ_LEN)


def place_ends(values, own_key, low, largest):
    spot = [jax.random.randint(jax.random.fold_in(own_key, axis), (), 0, length) for axis, length in enumerate(values.shape)]
    main_axis = values.shape.index(max(values.shape))
    neighbour = spot[:main_axis] + [(spot[main_axis] + 1) % values.shape[main_axis]] + spot[main_axis + 1:]
    return values.at[tuple(spot)].set(low).at[tuple(neighbour)].set(largest)


def shard_levels(rng, extent, shards, low, top_value):
    def one(axis_at, parts):
        heights = jax.random.uniform(jax.random.fold_in(jax.random.fold_in(rng, 6), axis_at), (parts,), jnp.float32, low / len(shards), top_value / len(shards))
        return jnp.repeat(jnp.exp(heights), extent[axis_at] // parts).reshape((-1,) + (1,) * (len(extent) - axis_at - 1))

    factor_of = one(*shards[0])
    for cut in shards[1:]:
        factor_of = factor_of * one(*cut)
    return factor_of


def split_up(amount, total, most, lean):
    portions = [(1 << 20) // math.isqrt(grade ** lean) + 1 for grade in range(2, amount + 1)]
    surplus, counts = total - most - (amount - 1), [1] * (amount - 1)
    while surplus > 0:
        movable = [i for i in range(amount - 1) if counts[i] < most]
        pool, remaining = sum([portions[i] for i in movable]), surplus
        for i in movable:
            addition = min(most - counts[i], max(1, remaining * portions[i] // pool), surplus)
            counts[i] = counts[i] + addition
            surplus = surplus - addition
    return np.array([most] + counts)


def uneven_parts(key, number_of, total, limit, lean):
    if number_of == 2:
        one = jax.random.randint(key, (), max(1, total - limit), min(limit, total - 1) + 1)
        return jnp.stack([one, total - one])
    sizes = jnp.asarray(split_up(number_of, total, limit, lean), jnp.int32)
    pairs = (number_of - 1) // 2
    giver, taker = sizes[1:1 + 2 * pairs:2], sizes[2:2 + 2 * pairs:2]
    margin = jnp.minimum(giver - 1, limit - taker)
    shifted = jax.random.randint(jax.random.fold_in(key, 1), (pairs,), 0, 1 << 20) % (margin + 1)
    sizes = sizes.at[1:1 + 2 * pairs:2].set(giver - shifted).at[2:2 + 2 * pairs:2].set(taker + shifted)
    return sizes[jax.random.permutation(jax.random.fold_in(key, 2), number_of)]


def noise(key, extent, width, limit, split=(), held_as=jnp.bfloat16):
    drawn = jax.random.normal(key, extent, jnp.float32) * width
    if len(split) > 0:
        drawn = shard_levels(key, extent, split, -0.22, 0.18) * drawn
    return jnp.clip(drawn, min=-limit, max=limit).astype(held_as)


def setup_inputs(seed: int = 0) -> dict:
    keys = jax.random.split(jax.random.key(seed), 16)
    inputs = noise(keys[0], (TOKENS, D), 1.0, 6.0, ((0, 32),))
    segment_ids = jnp.searchsorted(jnp.cumsum(uneven_parts(keys[1], TOKENS // (DOC_MOST // 2), TOKENS, DOC_MOST, 0)), jnp.arange(TOKENS), side="right").astype(jnp.int32)
    keep_mask = draw_keep_mask(jax.random.fold_in(keys[15], 71), 0)
    timestep = place_ends(jax.random.randint(keys[3], (SEQS,), 0, 2000), jax.random.fold_in(keys[3], 1), 0, 1999).astype(jnp.int32)
    w_qkv = noise(keys[4], (3, D, D), D ** -0.5, 0.21875, ((1, 8), (2, 4)))
    b_query = noise(keys[5], (D,), 0.5, 3.0, ((0, 4),), jnp.float32)
    b_value = noise(keys[6], (D,), 0.1, 0.6, ((0, 4),), jnp.float32)
    w_out = noise(keys[7], (D, D), (max(D // 64, 1)) ** -0.5, 1.75, ((0, 4), (1, 8)))
    w_up = noise(keys[8], (D, FF), D ** -0.5, 0.21875, ((0, 8), (1, 4)))
    b_up = noise(keys[9], (FF,), 0.5, 3.0, ((0, 4),), jnp.float32)
    w_down = noise(keys[10], (FF, D), FF ** -0.5, 0.109375, ((0, 4), (1, 8)))
    time_weight = noise(keys[11], (TE, D), TE ** -0.5, 0.5, ((1, 8),))
    gains = jnp.clip(1.0 + 0.18 * jax.random.normal(keys[12], (2, D), jnp.float32), 0.1, 1.9)
    row_biases = noise(keys[13], (5, D), 0.3, 1.8, (), jnp.float32)
    d_out = noise(keys[14], (TOKENS, D), 1.0, 6.0, ((0, 32),))
    return dict(inputs=inputs, segment_ids=segment_ids, keep_mask=keep_mask, timestep=timestep, w_qkv=w_qkv, b_query=b_query, b_value=b_value, w_out=w_out, w_up=w_up, b_up=b_up, w_down=w_down, time_weight=time_weight, gains=gains, row_biases=row_biases, d_out=d_out)


epsilon = 1e-05
masked = -1e+30
highest = lax.Precision.HIGHEST

@jax.custom_vjp
def low(v):
    return lax.optimization_barrier(v.astype(jnp.bfloat16)).astype(jnp.float32)

@jax.custom_vjp
def low_back(v):
    return v

def low_keep(v):
    return (low(v), None)

def low_pass(kept, grad):
    return (grad,)

def back_keep(v):
    return (v, None)

def back_low(kept, grad):
    return (low(grad),)
low.defvjp(low_keep, low_pass)
low_back.defvjp(back_keep, back_low)

def matmul(left, right):
    return jnp.dot(left, right, precision=highest, preferred_element_type=jnp.float32)

def layer_norm(values, norm_gain, norm_shift):
    average = lax.optimization_barrier(jnp.mean(values, axis=-1, keepdims=True))
    centered = values - average
    variance = lax.optimization_barrier(jnp.mean(centered * centered, axis=-1, keepdims=True))
    return centered * lax.rsqrt(variance + epsilon) * norm_gain + norm_shift

def sinusoid(timesteps, features):
    half_width = features // 2
    frequency = jnp.exp(-math.log(10000.0) * jnp.arange(half_width, dtype=jnp.float32) / half_width)
    angles = timesteps.astype(jnp.float32)[:, None] * frequency[None, :]
    return jnp.concatenate([jnp.cos(angles), jnp.sin(angles)], axis=1)

def attention(queries, key_rows, value_rows, segment, kept_tokens):
    length = segment.shape[0]
    query_heads = queries.reshape(length, HEADS, HEAD)
    key_heads = key_rows.reshape(length, HEADS, HEAD)
    value_heads = value_rows.reshape(length, HEADS, HEAD)
    scores = low_back(jnp.einsum('qhd,khd->hqk', query_heads, key_heads, precision=highest))
    places = jnp.arange(length)
    allowed = (segment[:, None] == segment[None, :]) & ((kept_tokens[None, :] > 0) | (places[:, None] == places[None, :]))
    scores = jnp.where(allowed[None], scores, masked)
    row_max = lax.optimization_barrier(jnp.max(scores, axis=-1, keepdims=True))
    weights = jnp.exp(scores - row_max)
    chances = low(weights / lax.optimization_barrier(jnp.sum(weights, axis=-1, keepdims=True)))
    context = jnp.einsum('hqk,khd->qhd', chances, value_heads, precision=highest)
    return context.reshape(length, D)

def layer(weights, inputs, segment, kept_tokens, timestep_one):
    w_qkv, b_query, b_value, w_out, w_up, b_up, w_down, time_weight, gains, row_biases = weights
    time_rows = low(sinusoid(timestep_one[None], TE))
    time_embed = matmul(time_rows, time_weight) + row_biases[4]
    stream_in = inputs + time_embed
    normed_one = low(layer_norm(stream_in, gains[0], row_biases[0]))
    query_scale = HEAD ** (-0.5)
    queries = low_back(low((matmul(normed_one, w_qkv[0]) + b_query) * query_scale))
    key_rows = low_back(low(matmul(normed_one, w_qkv[1])))
    value_rows = low_back(low(matmul(normed_one, w_qkv[2]) + b_value))
    context = low_back(low(attention(queries, key_rows, value_rows, segment, kept_tokens)))
    stream_mid = stream_in + low_back(matmul(context, w_out)) + row_biases[2]
    normed_two = low(layer_norm(stream_mid, gains[1], row_biases[1]))
    hidden_pre = low_back(matmul(normed_two, w_up) + b_up)
    hidden = low(jax.nn.gelu(hidden_pre, approximate=False))
    return stream_mid + low_back(matmul(hidden, w_down)) + row_biases[3]

def reference(inputs, segment_ids, keep_mask, timestep, w_qkv, b_query, b_value, w_out, w_up, b_up, w_down, time_weight, gains, row_biases, d_out):
    params = (w_qkv.astype(jnp.float32), b_query.astype(jnp.float32), b_value.astype(jnp.float32), w_out.astype(jnp.float32), w_up.astype(jnp.float32), b_up.astype(jnp.float32), w_down.astype(jnp.float32), time_weight.astype(jnp.float32), gains.astype(jnp.float32), row_biases.astype(jnp.float32))
    segment_table = segment_ids.reshape(SEQS, SEQ_LEN)
    keep_table = keep_mask.reshape(SEQS, SEQ_LEN)

    def whole(values, *weights):

        def one_sequence(element):
            return layer(weights, element[0], element[1], element[2], element[3])
        result = lax.map(jax.checkpoint(one_sequence), (values.reshape(SEQS, SEQ_LEN, D), segment_table, keep_table, timestep))
        return result.reshape(TOKENS, D)
    stream_out, pullback = jax.vjp(whole, inputs.astype(jnp.float32), *params)
    cotangent = d_out.astype(jnp.float32) * keep_mask.astype(jnp.float32)[:, None]
    gradients = pullback(cotangent)
    return (stream_out.astype(jnp.bfloat16), gradients[0], gradients[1], gradients[2], gradients[3], gradients[4], gradients[5], gradients[6], gradients[7], gradients[8], gradients[9], gradients[10])
```

```python
import functools
import math

import jax
import jax.numpy as jnp
from jax import lax
from jax.experimental import pallas as pl
from jax.experimental.pallas import tpu as pltpu
from jax.sharding import Mesh
from jax.sharding import PartitionSpec as P

HEAD = 64
SEQ_LEN = 2048
BLOCK = 256
F32 = jnp.float32
BF = jnp.bfloat16

epsilon = 1e-05
masked = -1e30
highest = lax.Precision.HIGHEST

LIMIT = 60 << 20


def dot(left, right):
    return jnp.dot(left, right, preferred_element_type=F32)


def dot_t(left, right):
    return lax.dot_general(left, right, (((1,), (1,)), ((), ())), preferred_element_type=F32)


def t_dot(left, right):
    return lax.dot_general(left, right, (((0,), (0,)), ((), ())), preferred_element_type=F32)


def params(*semantics, limit=LIMIT):
    return pltpu.CompilerParams(dimension_semantics=semantics, vmem_limit_bytes=limit)


def whole(shape):
    rank = len(shape)
    return pl.BlockSpec(shape, lambda *_: (0,) * rank)


def sinusoid(timesteps, features):
    half_width = features // 2
    frequency = jnp.exp(-math.log(10000.0) * jnp.arange(half_width, dtype=F32) / half_width)
    angles = timesteps.astype(F32)[:, None] * frequency[None, :]
    return jnp.concatenate([jnp.cos(angles), jnp.sin(angles)], axis=1)


def swap(value, axis):
    return lax.ppermute(value, axis, [(0, 1), (1, 0)])


def shift(value, axis, size, by):
    return lax.ppermute(value, axis, [(i, (i + by) % size) for i in range(size)])


def gather_near(value):
    far = swap(value, "t1")
    return [value, swap(value, "t0"), far, swap(far, "t0")]


def spread(block, first, second):
    own, one = block, swap(block, first)
    two, both = swap(own, second), swap(one, second)
    if first == "d0":
        found = {(0, 0): own, (1, 0): one, (0, 1): two, (1, 1): both}
    else:
        found = {(0, 0): own, (0, 1): one, (1, 0): two, (1, 1): both}
    out = {}
    for (a, b), value in found.items():
        out[a, b, 0] = value
        out[a, b, 1] = swap(value, "t0")
    return out


def gather_pack(pack, size, orders):
    rows = pack.shape[0]
    if size > 4:
        full = lax.all_gather(pack, ("d1", "d0"), axis=0, tiled=True)
        return [[(value, None, 0)] for value in gather_near(full)], full.shape[0]
    line = [pack] + [shift(pack, "d1", size, by) for by in range(1, size)]
    groups = [[], [], [], []]
    if len(orders) == 1:
        found = spread(jnp.stack(line), *orders[0])
        for (a, b, c), value in found.items():
            groups[b * 2 + c] += [(value, s, a * size + s) for s in range(size)]
    else:
        for s, block in enumerate(line):
            found = spread(block, *orders[s % 2])
            for (a, b, c), value in found.items():
                groups[b * 2 + c].append((value, None, a * size + s))
    return groups, rows


def loader(pieces, rows, arrays):
    plan = []
    for value, lead, slot in pieces:
        for n, known in enumerate(arrays):
            if known is value:
                break
        else:
            n = len(arrays)
            arrays.append(value)
        plan.append((n, lead, slot))
    return plan


def copies(plan, rows, refs, target, base, table, sems):
    out = []
    for k, (n, lead, slot) in enumerate(plan):
        source = refs[n] if lead is None else refs[n].at[lead]
        if table is None:
            start = slot * rows
        else:
            start = pl.multiple_of(table[base + slot], rows)
        out.append(pltpu.make_async_copy(source, target.at[pl.ds(start, rows), :], sems.at[k]))
    return out


def norm(values):
    average = jnp.mean(values, axis=-1, keepdims=True)
    centered = values - average
    variance = jnp.mean(centered * centered, axis=-1, keepdims=True)
    scale = lax.rsqrt(variance + epsilon)
    return centered * scale, scale


def norm_back(gradient, unit, scale):
    one = jnp.mean(gradient, axis=-1, keepdims=True)
    two = jnp.mean(gradient * unit, axis=-1, keepdims=True)
    return scale * (gradient - one - unit * two)


def pack_columns(query, key, value, out):
    return jnp.concatenate(
        [
            query[..., :128],
            key[..., :128],
            value[..., :128],
            query[..., 128:],
            value[..., 128:],
            key[..., 128:],
            out[..., 128:],
            out[..., :128],
        ],
        axis=-1,
    )


def unpack_columns(pack):
    query = jnp.concatenate([pack[..., 0:128], pack[..., 384:448]], axis=-1)
    key = jnp.concatenate([pack[..., 128:256], pack[..., 512:576]], axis=-1)
    value = jnp.concatenate([pack[..., 256:384], pack[..., 448:512]], axis=-1)
    out = jnp.concatenate([pack[..., 640:768], pack[..., 576:640]], axis=-1)
    return query, key, value, out


def project_kernel(plan, rows, table, *refs):
    x_refs, refs = refs[:4], refs[4:]
    embed, gain, low_shift, bias, scale = refs[:5]
    count = len({n for n, _, _ in plan})
    pieces, refs = refs[5 : 5 + count], refs[5 + count :]
    made_ref, unit_ref, stream_ref, w_ref, sems = refs
    step = pl.program_id(0)
    todo = copies(plan, rows, pieces, w_ref, 1, table, sems)

    @pl.when(step == 0)
    def _():
        for copy in todo:
            copy.start()

    for near in range(4):

        @pl.when(step == near)
        def _(near=near):
            stream = x_refs[near][...].astype(F32) + embed[...]
            unit, _ = norm(stream)
            low = (unit * gain[...] + low_shift[...]).astype(BF)
            unit_ref[...] = low
            if near == 0:
                stream_ref[...] = stream
                for copy in todo:
                    copy.wait()
            made_ref[...] = ((dot(low, w_ref[:, :640]) + bias[...]) * scale[...]).astype(BF)


def project(x_near, embed, gain, low_shift, bias, scale, pieces, rows, table):
    n, d = x_near[0].shape
    arrays = []
    plan = loader(pieces, rows, arrays)
    grid_spec = pltpu.PrefetchScalarGridSpec(
        num_scalar_prefetch=1,
        grid=(4,),
        in_specs=[whole((n, d))] * 4
        + [whole(v.shape) for v in (embed, gain, low_shift, bias, scale)]
        + [pl.BlockSpec(memory_space=pl.ANY)] * len(arrays),
        out_specs=[
            pl.BlockSpec((n, 640), lambda i, t: (t[0] ^ i, 0)),
            pl.BlockSpec((n, d), lambda i, t: (t[0] ^ i, 0)),
            whole((n, d)),
            whole((d, 768)),
        ],
        scratch_shapes=[pltpu.SemaphoreType.DMA((len(plan),))],
    )
    return pl.pallas_call(
        functools.partial(project_kernel, plan, rows),
        grid_spec=grid_spec,
        out_shape=[
            jax.ShapeDtypeStruct((4 * n, 640), BF),
            jax.ShapeDtypeStruct((4 * n, d), BF),
            jax.ShapeDtypeStruct((n, d), F32),
            jax.ShapeDtypeStruct((d, 768), BF),
        ],
        compiler_params=params("arbitrary"),
        cost_estimate=pl.CostEstimate(flops=5 * 10**9, bytes_accessed=14 * 10**6, transcendentals=0),
        name="project",
    )(table, *x_near, embed, gain, low_shift, bias, scale, *arrays)


def low_half(shape):
    return lax.broadcasted_iota(jnp.int32, shape, 1) < HEAD


def pair_bias(key_ref, row, place, start):
    spot = start + lax.broadcasted_iota(jnp.int32, (BLOCK, BLOCK), 0)
    allowed = (key_ref[pl.ds(start, BLOCK), :] == row) | (spot == place)
    return jnp.where(allowed, 0.0, masked)


def block_places(table, near, part, blocks):
    number = (table[0] ^ near) * blocks + part
    return number, pl.multiple_of(number * BLOCK, BLOCK), table[1 + 2 * number], table[2 + 2 * number]


def split_heads(pair, third, third_low):
    half = low_half(pair.shape)
    zero = jnp.zeros_like(pair)
    last = jnp.where(half, third, zero) if third_low else jnp.where(half, zero, third)
    return jnp.where(half, pair, zero), jnp.where(half, zero, pair), last


def attend_kernel(nears, blocks, table, made_ref, key_ref, row_ref, context_ref, total_ref, score_ref):
    for slot, near in enumerate(nears):
        for part in range(blocks):
            here = pl.ds(part * BLOCK, BLOCK)
            number, own, first, last = block_places(table, near, part, blocks)
            rows = pl.ds(own, BLOCK)
            q_all = split_heads(made_ref[rows, 0:128], made_ref[rows, 384:512], True)
            row = row_ref[pl.ds(number, 1), :]
            place = own + lax.broadcasted_iota(jnp.int32, (BLOCK, BLOCK), 1)

            def score(j, tops, q_all=q_all, row=row, place=place):
                start = pl.multiple_of(j * BLOCK, BLOCK)
                spot = pl.ds(start, BLOCK)
                bias = pair_bias(key_ref, row, place, start)
                out = []
                for h in range(3):
                    keys = made_ref[spot, 128:256] if h < 2 else made_ref[spot, 512:640]
                    s = dot_t(keys, q_all[h]) + bias
                    score_ref[h, j] = s
                    out.append(jnp.maximum(tops[h], jnp.max(s.reshape(BLOCK // 8, 8, BLOCK), axis=0)))
                return tuple(out)

            begin = jnp.full((8, BLOCK), masked, F32)
            tops = lax.fori_loop(first, last, score, (begin,) * 3)
            tops = [jnp.max(t, axis=0, keepdims=True) for t in tops]

            def weigh(j, carry, tops=tops):
                spot = pl.ds(pl.multiple_of(j * BLOCK, BLOCK), BLOCK)
                pair_t = made_ref[spot, 256:384].T
                third_t = made_ref[spot, 384:512].T
                values = (pair_t[:HEAD], pair_t[HEAD:], third_t[HEAD:])
                sums, totals = carry
                new_sums, new_totals = [], []
                for h in range(3):
                    p = jnp.exp(score_ref[h, j] - tops[h])
                    new_totals.append(totals[h] + jnp.sum(p.reshape(BLOCK // 8, 8, BLOCK), axis=0))
                    new_sums.append(sums[h] + dot(values[h], p.astype(BF)))
                return tuple(new_sums), tuple(new_totals)

            zeros = (jnp.zeros((HEAD, BLOCK), F32),) * 3
            sums, totals = lax.fori_loop(first, last, weigh, (zeros, (jnp.zeros((8, BLOCK), F32),) * 3))
            done = []
            for h in range(3):
                total = jnp.sum(totals[h], axis=0, keepdims=True)
                done.append(sums[h] / total)
                total_ref[slot, h, here] = (tops[h] + jnp.log(total))[0]
            context_ref[slot, here, 0:128] = jnp.concatenate([jnp.zeros_like(done[2]), done[2]], axis=0).T.astype(BF)
            context_ref[slot, here, 128:256] = jnp.concatenate([done[0], done[1]], axis=0).T.astype(BF)


VMEM = pl.BlockSpec(memory_space=pltpu.VMEM)
SMEM = pl.BlockSpec(memory_space=pltpu.SMEM)


def attend(nears, table, made, key, row):
    keys = made.shape[0]
    n = keys // 4
    blocks = n // BLOCK
    return pl.pallas_call(
        functools.partial(attend_kernel, nears, blocks),
        in_specs=[SMEM] + [VMEM] * 3,
        out_specs=[VMEM] * 2,
        out_shape=[
            jax.ShapeDtypeStruct((len(nears), n, 256), BF),
            jax.ShapeDtypeStruct((len(nears), 8, n), F32),
        ],
        scratch_shapes=[pltpu.VMEM((3, keys // BLOCK, BLOCK, BLOCK), F32)],
        compiler_params=pltpu.CompilerParams(vmem_limit_bytes=LIMIT),
        cost_estimate=pl.CostEstimate(flops=8 * 10**9, bytes_accessed=4 * 10**6, transcendentals=0),
        name="attend",
    )(table, made, key, row)


def outer_kernel(context_a, context_b, context_c, context_d, w_a, w_b, w_c, w_d, stream_ref, gain, low_shift, add,
                 mid_ref, unit_ref):
    mid = stream_ref[...] + add[...]
    for context, w in ((context_a, w_a), (context_b, w_b), (context_c, w_c), (context_d, w_d)):
        mid = mid + dot_t(context[...], w[...])
    mid_ref[...] = mid
    unit, _ = norm(mid)
    unit_ref[...] = (unit * gain[...] + low_shift[...]).astype(BF)


def outer(contexts, weights, stream, gain, low_shift, add):
    n, d = stream.shape
    return pl.pallas_call(
        outer_kernel,
        in_specs=[VMEM] * 12,
        out_specs=[VMEM] * 2,
        out_shape=[jax.ShapeDtypeStruct((n, d), F32), jax.ShapeDtypeStruct((n, d), BF)],
        compiler_params=pltpu.CompilerParams(vmem_limit_bytes=LIMIT),
        cost_estimate=pl.CostEstimate(flops=2 * 10**9, bytes_accessed=6 * 10**6, transcendentals=0),
        name="outer",
    )(*contexts, *weights, stream, gain, low_shift, add)


CHUNK = 256


def feed_kernel(plans_up, plans_down, rows, count_up, table, unit_ref, grad_ref, bias_ref, out_in, back_in, *refs):
    arrays = len(refs) - 9
    pieces, refs = refs[:arrays], refs[arrays:]
    out_ref, back_ref, up_ref, down_ref, column_ref, w_up, w_down, sems_up, sems_down = refs
    todo = []
    for group in range(2):
        todo.append(copies(plans_up[group], rows, pieces, w_up.at[group], 1, table, sems_up.at[group]))
        todo.append(copies(plans_down[group], rows, pieces, w_down.at[group], 1, table, sems_down.at[group]))
    for batch in todo:
        for copy in batch:
            copy.start()
    out_ref[...] = out_in[...]
    back_ref[...] = back_in[...]
    for group in range(2):
        for batch in todo[2 * group : 2 * group + 2]:
            for copy in batch:
                copy.wait()

        @pl.loop(0, w_up.shape[2] // CHUNK)
        def _(step, group=group):
            here = pl.ds(pl.multiple_of(step * CHUNK, CHUNK), CHUNK)
            unit, grad = unit_ref[...], grad_ref[...]
            up, down = w_up[group, :, here], w_down[group, :, here]
            pre = dot(unit, up) + bias_ref[group, :, here]
            d_hidden = dot(grad, down)
            share = 0.5 + 0.5 * lax.erf(pre * math.sqrt(0.5))
            hidden = (pre * share).astype(BF)
            slope = share + pre * (jnp.exp(-0.5 * pre * pre) * (1.0 / math.sqrt(2.0 * math.pi)))
            d_pre = (d_hidden * slope).astype(BF)
            out_ref[...] += dot_t(hidden, down)
            back_ref[...] += dot_t(d_pre, up)
            up_ref[group, :, here] = t_dot(unit, d_pre).astype(BF)
            down_ref[group, :, here] = t_dot(grad, hidden).astype(BF)
            column_ref[group, :, here] = jnp.sum(d_pre.astype(F32), axis=0, keepdims=True)


def feed(table, unit, grad, bias, out, back, up, down, rows):
    n, d = unit.shape
    width = bias.shape[-1]
    arrays = []
    plans_up = [loader(pieces, rows, arrays) for pieces in up]
    plans_down = [loader(pieces, rows, arrays) for pieces in down]
    return pl.pallas_call(
        functools.partial(feed_kernel, plans_up, plans_down, rows, 0),
        in_specs=[SMEM] + [VMEM] * 5
        + [pl.BlockSpec(memory_space=pl.ANY)] * len(arrays),
        out_specs=[VMEM] * 5,
        out_shape=[
            jax.ShapeDtypeStruct((n, d), F32),
            jax.ShapeDtypeStruct((n, d), F32),
            jax.ShapeDtypeStruct((2, d, width), BF),
            jax.ShapeDtypeStruct((2, d, width), BF),
            jax.ShapeDtypeStruct((2, 1, width), F32),
        ],
        scratch_shapes=[
            pltpu.VMEM((2, d, width), BF),
            pltpu.VMEM((2, d, width), BF),
            pltpu.SemaphoreType.DMA((2, len(plans_up[0]))),
            pltpu.SemaphoreType.DMA((2, len(plans_down[0]))),
        ],
        compiler_params=pltpu.CompilerParams(vmem_limit_bytes=LIMIT),
        cost_estimate=pl.CostEstimate(flops=10 * 10**9, bytes_accessed=16 * 10**6, transcendentals=0),
        name="feed",
    )(table, unit, grad, bias, out, back, *arrays)


def middle_kernel(out_ref, back_ref, mid_ref, grad_ref, gain, add, low_ref, full_ref, short_ref, sums_ref):
    mid = mid_ref[...]
    low_ref[...] = (mid + out_ref[...] + add[...]).astype(BF)
    unit, scale = norm(mid)
    back = back_ref[...]
    grad = grad_ref[...].astype(F32)
    full = grad + norm_back(back * gain[...], unit, scale)
    full_ref[...] = full
    short_ref[...] = full.astype(BF)
    sums_ref[...] = jnp.zeros_like(sums_ref)
    sums_ref[0:1] = jnp.sum(back * unit, axis=0, keepdims=True)
    sums_ref[1:2] = jnp.sum(back, axis=0, keepdims=True)
    sums_ref[2:3] = jnp.sum(full, axis=0, keepdims=True)
    sums_ref[3:4] = jnp.sum(grad, axis=0, keepdims=True)


def middle(out, back, mid, grad, gain, add):
    n, d = mid.shape
    return pl.pallas_call(
        middle_kernel,
        in_specs=[VMEM] * 6,
        out_specs=[VMEM] * 4,
        out_shape=[
            jax.ShapeDtypeStruct((n, d), BF),
            jax.ShapeDtypeStruct((n, d), F32),
            jax.ShapeDtypeStruct((n, d), BF),
            jax.ShapeDtypeStruct((8, d), F32),
        ],
        compiler_params=pltpu.CompilerParams(vmem_limit_bytes=LIMIT),
        cost_estimate=pl.CostEstimate(flops=10**7, bytes_accessed=10 * 10**6, transcendentals=0),
        name="middle",
    )(out, back, mid, grad, gain, add)


def back_kernel(nears, blocks, last_call, table, made_ref, key_ref, row_ref, total_ref, w_ref, short_a, short_b, *refs):
    if last_call:
        before_ref, dq_ref, out_ref, d_ref, p_ref, dp_ref, sum_ref = refs
        sum_ref[...] = before_ref[...]
    else:
        dq_ref, sum_ref, d_ref, p_ref, dp_ref = refs
        sum_ref[...] = jnp.zeros_like(sum_ref)
    scale = HEAD ** (-0.5)
    for slot, (near, short) in enumerate(zip(nears, (short_a, short_b), strict=True)):
        d_ref[...] = dot(short[...], w_ref[:, 512:768]).astype(BF)
        for part in range(blocks):
            here = pl.ds(part * BLOCK, BLOCK)
            number, own, first, last = block_places(table, near, part, blocks)
            rows = pl.ds(own, BLOCK)
            q_all = split_heads(made_ref[rows, 0:128], made_ref[rows, 384:512], True)
            d_all = split_heads(d_ref[here, 128:256], d_ref[here, 0:128], False)
            row = row_ref[pl.ds(number, 1), :]
            place = own + lax.broadcasted_iota(jnp.int32, (BLOCK, BLOCK), 1)
            totals = [total_ref[slot, h : h + 1, here] for h in range(3)]

            def weigh(j, inners, q_all=q_all, d_all=d_all, row=row, place=place, totals=totals):
                start = pl.multiple_of(j * BLOCK, BLOCK)
                spot = pl.ds(start, BLOCK)
                bias = pair_bias(key_ref, row, place, start)
                new, add_v = [], []
                for h in range(3):
                    keys = made_ref[spot, 128:256] if h < 2 else made_ref[spot, 512:640]
                    values = made_ref[spot, 256:384] if h < 2 else made_ref[spot, 384:512]
                    p = jnp.exp(dot_t(keys, q_all[h]) + bias - totals[h])
                    d_p = dot_t(values, d_all[h])
                    p_ref[h, j] = p
                    dp_ref[h, j] = d_p
                    new.append(inners[h] + jnp.sum((p * d_p).reshape(BLOCK // 8, 8, BLOCK), axis=0))
                    add_v.append(dot(p.astype(BF), d_all[h]))
                sum_ref[spot, 128:256] += add_v[0] + add_v[1]
                sum_ref[spot, 256:384] += add_v[2]
                return tuple(new)

            inners = lax.fori_loop(first, last, weigh, (jnp.zeros((8, BLOCK), F32),) * 3)
            inners = [jnp.sum(v, axis=0, keepdims=True) for v in inners]

            def turn(j, sums, q_all=q_all, inners=inners):
                spot = pl.ds(pl.multiple_of(j * BLOCK, BLOCK), BLOCK)
                pair_t, third_t = made_ref[spot, 128:256].T, made_ref[spot, 512:640].T
                turned = (pair_t[:HEAD], pair_t[HEAD:], third_t[:HEAD])
                new, add_k = [], []
                for h in range(3):
                    d_s = (p_ref[h, j] * (dp_ref[h, j] - inners[h])).astype(BF)
                    add_k.append(dot(d_s, q_all[h]))
                    new.append(sums[h] + dot(turned[h], d_s))
                sum_ref[spot, 0:128] += add_k[0] + add_k[1]
                sum_ref[spot, 384:512] += add_k[2]
                return tuple(new)

            sums = lax.fori_loop(first, last, turn, (jnp.zeros((HEAD, BLOCK), F32),) * 3)
            two = jnp.concatenate([sums[0], sums[1]], axis=0).T.astype(BF) * jnp.asarray(scale, BF)
            one = jnp.concatenate([sums[2], jnp.zeros_like(sums[2])], axis=0).T.astype(BF) * jnp.asarray(scale, BF)
            dq_ref[slot, here, :] = two
            sum_ref[rows, 256:384] += one.astype(F32)
    if last_call:
        out_ref[...] = sum_ref[...].astype(BF)


def attend_back(nears, table, made, key, row, total, w, shorts, before):
    keys = made.shape[0]
    n = keys // 4
    last_call = before is not None
    operands = [table, made, key, row, total, w, *shorts] + ([before] if last_call else [])
    scores = pltpu.VMEM((3, keys // BLOCK, BLOCK, BLOCK), F32)
    scratch = [pltpu.VMEM((n, 256), BF), scores, scores]
    if last_call:
        scratch.append(pltpu.VMEM((keys, 512), F32))
    return pl.pallas_call(
        functools.partial(back_kernel, nears, n // BLOCK, last_call),
        in_specs=[SMEM] + [VMEM] * (len(operands) - 1),
        out_specs=[VMEM] * 2,
        out_shape=[
            jax.ShapeDtypeStruct((len(nears), n, 128), BF),
            jax.ShapeDtypeStruct((keys, 512), BF if last_call else F32),
        ],
        scratch_shapes=scratch,
        compiler_params=pltpu.CompilerParams(vmem_limit_bytes=LIMIT),
        cost_estimate=pl.CostEstimate(flops=14 * 10**9, bytes_accessed=10 * 10**6, transcendentals=0),
        name="attend_back",
    )(*operands)


def unit_back_kernel(table, dq_ref, dkv_ref, w_ref, out_ref):
    out_ref[0] = (dot_t(dkv_ref[...], w_ref[:, 128:640]) + dot_t(dq_ref[0], w_ref[:, 0:128])).astype(BF)


def unit_back(table, dq, dkv, w):
    n = dq.shape[1]
    d = w.shape[0]
    grid_spec = pltpu.PrefetchScalarGridSpec(
        num_scalar_prefetch=1,
        grid=(4,),
        in_specs=[
            pl.BlockSpec((1, n, 128), lambda i, t: (3 - i, 0, 0)),
            pl.BlockSpec((n, 512), lambda i, t: (t[0] ^ (3 - i), 0)),
            whole((d, 768)),
        ],
        out_specs=pl.BlockSpec((1, n, d), lambda i, t: (3 - i, 0, 0)),
    )
    return pl.pallas_call(
        unit_back_kernel,
        grid_spec=grid_spec,
        out_shape=jax.ShapeDtypeStruct((4, n, d), BF),
        compiler_params=params("arbitrary"),
        cost_estimate=pl.CostEstimate(flops=4 * 10**9, bytes_accessed=6 * 10**6, transcendentals=0),
        name="unit_back",
    )(table, dq, dkv, w)


def grads_kernel(table, unit_ref, dq_ref, dkv_ref, short_ref, context_ref, out_ref, column_ref, sum_ref):
    step = pl.program_id(0)

    @pl.when(step == 0)
    def _():
        sum_ref[...] = jnp.zeros_like(sum_ref)
        column_ref[...] = jnp.zeros_like(column_ref)

    unit, dq, dkv = unit_ref[...], dq_ref[0], dkv_ref[...]
    made = t_dot(unit, dkv)
    out = t_dot(short_ref[0], context_ref[0])
    sum_ref[:, 0:128] += t_dot(unit, dq)
    sum_ref[:, 128:512] += made[:, :384]
    sum_ref[:, 512:640] += made[:, 384:] + out[:, :128]
    sum_ref[:, 640:768] += out[:, 128:]
    column_ref[:, 0:128] += jnp.sum(dq.astype(F32), axis=0, keepdims=True)
    column_ref[:, 128:640] += jnp.sum(dkv.astype(F32), axis=0, keepdims=True)

    @pl.when(step == 3)
    def _():
        out_ref[...] = sum_ref[...].astype(BF)


def grads(table, unit, dq, dkv, short, context):
    n = dq.shape[1]
    d = unit.shape[1]
    grid_spec = pltpu.PrefetchScalarGridSpec(
        num_scalar_prefetch=1,
        grid=(4,),
        in_specs=[
            pl.BlockSpec((n, d), lambda i, t: (t[0] ^ i, 0)),
            pl.BlockSpec((1, n, 128), lambda i, t: (i, 0, 0)),
            pl.BlockSpec((n, 512), lambda i, t: (t[0] ^ i, 0)),
            pl.BlockSpec((1, n, d), lambda i, t: (i, 0, 0)),
            pl.BlockSpec((1, n, 256), lambda i, t: (i, 0, 0)),
        ],
        out_specs=[whole((d, 768)), whole((1, 640))],
        scratch_shapes=[pltpu.VMEM((d, 768), F32)],
    )
    return pl.pallas_call(
        grads_kernel,
        grid_spec=grid_spec,
        out_shape=[jax.ShapeDtypeStruct((d, 768), BF), jax.ShapeDtypeStruct((1, 640), F32)],
        compiler_params=params("arbitrary"),
        cost_estimate=pl.CostEstimate(flops=6 * 10**9, bytes_accessed=12 * 10**6, transcendentals=0),
        name="grads",
    )(table, unit, dq, dkv, short, context)


def final_kernel(one_ref, two_ref, stream_ref, full_ref, gain, grad_ref, sums_ref):
    back = one_ref[...] + two_ref[...].astype(F32)
    unit, scale = norm(stream_ref[...])
    grad = full_ref[...] + norm_back(back * gain[...], unit, scale)
    grad_ref[...] = grad
    sums_ref[...] = jnp.zeros_like(sums_ref)
    sums_ref[0:1] = jnp.sum(back * unit, axis=0, keepdims=True)
    sums_ref[1:2] = jnp.sum(back, axis=0, keepdims=True)
    sums_ref[2:3] = jnp.sum(grad, axis=0, keepdims=True)


def final(one, two, stream, full, gain):
    n, d = stream.shape
    return pl.pallas_call(
        final_kernel,
        grid=(1,),
        in_specs=[whole((n, d))] * 4 + [whole((1, d))],
        out_specs=[whole((n, d)), whole((8, d))],
        out_shape=[jax.ShapeDtypeStruct((n, d), F32), jax.ShapeDtypeStruct((8, d), F32)],
        compiler_params=params("arbitrary"),
        cost_estimate=pl.CostEstimate(flops=10**7, bytes_accessed=7 * 10**6, transcendentals=0),
        name="final",
    )(one, two, stream, full, gain)


def add_low(one, two):
    return (one.astype(F32) + two.astype(F32)).astype(BF)


def tie(values, after):
    return lax.optimization_barrier((values, after))[0]


def side(value, which):
    return lax.dynamic_index_in_dim(value, which, 1, keepdims=False)


def scatter_line(mine, size, z):
    total = lax.dynamic_index_in_dim(mine, z, 0, keepdims=False).astype(F32)
    for by in range(1, size):
        sent = lax.dynamic_index_in_dim(mine, lax.rem(z + by, size), 0, keepdims=False)
        total = total + shift(sent, "d1", size, by).astype(F32)
    return total


def sum_dp(value, size):
    value = value + swap(value, "d0")
    if size > 4:
        return lax.psum(value, "d1")
    total = value
    for by in range(1, size):
        total = total + shift(value, "d1", size, by)
    return total


def sum_tensor(value):
    value = value + swap(value, "t0")
    return value + swap(value, "t1")


def shards(
    inputs,
    segment_ids,
    keep_mask,
    timestep,
    w_qkv,
    b_query,
    b_value,
    w_out,
    w_up,
    b_up,
    w_down,
    time_weight,
    gains,
    row_biases,
    d_out,
):
    size = lax.axis_size("d1")
    long = size > 4
    z, x = lax.axis_index("d1"), lax.axis_index("d0")
    own = lax.axis_index("t1") * 2 + lax.axis_index("t0")
    n, d = inputs.shape
    dp = 2 * size
    place = z * 2 + x
    features = time_weight.shape[0]
    columns = time_weight.shape[1]

    pack_one = pack_columns(w_qkv[0], w_qkv[1], w_qkv[2], w_out.T)
    rows = pack_one.shape[0]
    time_rows = sinusoid(timestep, features).astype(BF)
    if long:
        pieces_one = [(lax.all_gather(pack_one, ("d1", "d0"), axis=0, tiled=True), None, 0)]
        full_time = lax.all_gather(time_weight, ("d1", "d0"), axis=1, tiled=True)
        embed = dot(time_rows, full_time)
        all_rows = lax.all_gather(time_rows, ("d1", "d0"), axis=0, tiled=True)
        line = None
    else:
        line = [pack_one] + [shift(pack_one, "d1", size, by) for by in range(1, size)]
        time_pack = jnp.concatenate(
            [jnp.pad(time_weight, ((0, 0), (0, 128 - columns))), jnp.pad(time_rows, ((0, 15), (0, 0)))]
        )
        time_both = jnp.stack([time_pack, swap(time_pack, "d0")])
        time_line = [time_both] + [shift(time_both, "d1", size, by) for by in range(1, size)]
        spots = [lax.rem(z - by + size, size) * 2 + (x ^ a) for by in range(size) for a in range(2)]
        order = (jnp.arange(dp)[:, None] == jnp.stack(spots)[None, :]).astype(F32)
        time_all = jnp.concatenate(time_line)
        parts = jnp.einsum("of,pfc->pc", time_rows, time_all[:, :features, :columns], preferred_element_type=F32)
        embed = jnp.dot(order, parts, precision=highest).reshape(1, d)
        all_rows = jnp.dot(order, time_all[:, features, :].astype(F32), precision=highest)
        half = jnp.stack(line)
        other_half = swap(half, "d0")
        pieces_one = [(half, s, s) for s in range(size)] + [(other_half, s, size + s) for s in range(size)]
    embed = embed + row_biases[4][None, :]
    x_near = gather_near(inputs)
    up_near = [b[None, :] for b in gather_near(b_up)]
    zero_bias = jnp.zeros_like(b_query)
    bias_one = pack_columns(b_query, zero_bias, b_value, zero_bias)[None, :640]

    blocks = 4 * n // BLOCK
    ids = segment_ids.reshape(blocks, BLOCK)
    first = jnp.sum(segment_ids[None, :] < ids[:, :1], axis=1, dtype=jnp.int32)
    last = jnp.sum(segment_ids[None, :] <= ids[:, -1:], axis=1, dtype=jnp.int32)
    span = jnp.stack([first // BLOCK, (last + BLOCK - 1) // BLOCK], axis=1).reshape(-1)
    slots = [(lax.rem(z - s + size, size) * 2 + (x ^ a)) * rows for a in range(2) for s in range(size)]
    if long:
        slots = [jnp.zeros_like(own)]
    table_one = jnp.stack([own, *slots]).astype(jnp.int32)
    table_two = jnp.concatenate([jnp.stack([own]), span]).astype(jnp.int32)
    key = jnp.where(keep_mask > 0, segment_ids, -1)[:, None]
    own_keep = lax.dynamic_slice_in_dim(keep_mask, own * n, n, 0)
    grad_two = jnp.where(own_keep[:, None] > 0, d_out, jnp.zeros_like(d_out))
    scale = jnp.where(
        (jnp.arange(640) < 128) | ((jnp.arange(640) >= 384) & (jnp.arange(640) < 448)), HEAD ** (-0.5), 1.0
    ).astype(F32)[None, :]

    after = line[1:] if line else []
    groups_up, rows_two = gather_pack(tie(w_up, after), size, [("d0", "t1")])
    groups_down, _ = gather_pack(tie(w_down.T, after), size, [("t1", "d0")])

    made, unit_one, stream_in, w_one = project(
        x_near, embed, gains[0:1], row_biases[0:1], bias_one, scale, pieces_one, rows if not long else d, table_one
    )
    outer_near = gather_near(w_one[:, 512:768])
    context_far, total_far = attend((2, 3), table_two, made, key, ids)
    context_over = swap(context_far, "t1")
    context_near, total_near = attend((0, 1), table_two, made, key, ids)
    contexts = [
        context_near[0],
        swap(context_near[1], "t0"),
        context_over[0],
        swap(context_over[1], "t0"),
    ]
    stream_mid, unit_two = outer(contexts, outer_near, stream_in, gains[1:2], row_biases[1:2], row_biases[2:3])

    zeros = jnp.zeros((n, d), F32)
    far, near = (1, 3), (0, 2)
    out, back = zeros, zeros
    made_up = {}
    for batch in (far, near):
        out, back, g_up, g_down, g_column = feed(
            table_one, unit_two, grad_two, jnp.stack([up_near[g] for g in batch]), out, back,
            [groups_up[g] for g in batch], [groups_down[g] for g in batch], rows_two,
        )
        made_up[batch] = (g_up, g_down, g_column)
    swapped = [swap(v, "t0") for v in made_up[far]]
    output, full, short, sums_two = middle(out, back, stream_mid, grad_two, gains[1:2], row_biases[3:4])
    short_near = gather_near(short)
    both_up, both_down = [add_low(a, b) for a, b in zip(made_up[near][:2], swapped[:2], strict=True)]
    both_column = made_up[near][2] + swapped[2]
    up_bias = both_column[0] + swap(both_column[1], "t1")

    def split(value):
        return value.reshape(2, size, 2, rows, value.shape[-1])

    if long:
        up_mine = add_low(both_up[0], swap(both_up[1], "t1"))
        down_mine = add_low(both_down[0], swap(both_down[1], "t1"))
        up_share = lax.psum_scatter(up_mine, ("d1", "d0"), scatter_dimension=0, tiled=True).astype(F32)
        down_share = lax.psum_scatter(down_mine, ("d1", "d0"), scatter_dimension=0, tiled=True).astype(F32)
    else:
        up_split, down_split = split(both_up), split(both_down)
        up_sent = swap(lax.dynamic_index_in_dim(up_split, 1 - x, 2, keepdims=False), "d0")
        down_sent = swap(down_split[1], "t1")

    dq_near, sum_near = attend_back((0, 1), table_two, made, key, ids, total_near, w_one, short_near[:2], None)
    if not long:
        up_kept = add_low(lax.dynamic_index_in_dim(up_split, x, 2, keepdims=False), up_sent)
        down_kept = add_low(down_split[0], down_sent)
        up_next = swap(up_kept[1], "t1")
        down_next = swap(side(down_kept, 1 - x), "d0")
    dq_far, dkv = attend_back((2, 3), table_two, made, key, ids, total_far, w_one, short_near[2:], sum_near)
    if not long:
        up_mine = add_low(up_kept[0], up_next)
        down_mine = add_low(side(down_kept, x), down_next)
        up_share = scatter_line(up_mine, size, z)
        down_share = scatter_line(down_mine, size, z)
    dq = jnp.concatenate([dq_near, dq_far])
    back_near = unit_back(table_two, dq, dkv, w_one)
    mine = add_low(back_near[0], swap(back_near[1], "t0"))
    other = swap(add_low(back_near[2], swap(back_near[3], "t0")), "t1")
    grad_one, column_one = grads(
        table_two, unit_one, dq, dkv, jnp.stack(short_near), jnp.concatenate([context_near, context_far])
    )
    if long:
        one_share = lax.psum_scatter(grad_one, ("d1", "d0"), scatter_dimension=0, tiled=True).astype(F32)
    else:
        one_split = grad_one.reshape(size, 2, rows, 768)
        one_mine = add_low(side(one_split, x), swap(side(one_split, 1 - x), "d0"))
        one_share = scatter_line(one_mine, size, z)
    grad_input, sums_one = final(mine.astype(F32), other, stream_in, full, gains[0:1])

    early = sum_dp(jnp.concatenate([sum_tensor(sums_two[:4]), up_bias]), size)
    heads = sum_dp(column_one, size)
    seat = (jnp.arange(dp) == place).astype(F32)
    sums_one = sum_tensor(sums_one[:3])
    late = sum_dp(jnp.concatenate([sums_one[:2], seat[:, None] * sums_one[2:3]]), size)
    by_sequence = late[2:]
    own_columns = lax.dynamic_slice_in_dim(by_sequence, place * columns, columns, 1)
    grad_time = lax.dot_general(
        all_rows.astype(F32), own_columns, (((0,), (0,)), ((), ())), precision=highest, preferred_element_type=F32
    )
    d_query, d_key, d_value, d_outer = unpack_columns(one_share)
    column_query, _, column_value, _ = unpack_columns(jnp.pad(heads[0], (0, 128)))
    gain_total = jnp.stack([late[0], early[0]])
    bias_total = jnp.stack([late[1], early[1], early[2], early[3], jnp.sum(by_sequence, axis=0)])
    return (
        output,
        grad_input,
        jnp.stack([d_query, d_key, d_value]),
        column_query,
        column_value,
        d_outer.T,
        up_share,
        early[4],
        down_share.T,
        grad_time,
        gain_total,
        bias_total,
    )


def solution(mesh):
    dp, tensor = mesh.shape["dp"], mesh.shape["tensor"]
    fine = Mesh(mesh.devices.reshape(dp // 2, 2, tensor // 2, 2), ("d1", "d0", "t1", "t0"))
    rows, cols = ("d1", "d0"), ("t1", "t0")
    every = rows + cols
    in_specs = (
        P(every, None),
        P(rows),
        P(rows),
        P(rows),
        P(None, rows, cols),
        P(cols),
        P(cols),
        P(cols, rows),
        P(rows, cols),
        P(cols),
        P(cols, rows),
        P(None, rows),
        P(),
        P(),
        P(every, None),
    )
    out_specs = (
        P(every, None),
        P(every, None),
        P(None, rows, cols),
        P(cols),
        P(cols),
        P(cols, rows),
        P(rows, cols),
        P(cols),
        P(cols, rows),
        P(None, rows),
        P(),
        P(),
    )
    return jax.shard_map(shards, mesh=fine, in_specs=in_specs, out_specs=out_specs, check_vma=False)
```

```python
import functools
import math

import jax
import jax.numpy as jnp
from jax import lax
from jax.experimental import pallas as pl
from jax.experimental.pallas import tpu as pltpu
from jax.sharding import Mesh
from jax.sharding import PartitionSpec as P

HEAD = 64
SEQ_LEN = 2048
BLOCK = 256
F32 = jnp.float32
BF = jnp.bfloat16

epsilon = 1e-05
masked = -1e30
highest = lax.Precision.HIGHEST

LIMIT = 32 << 20


def dot(left, right):
    return jnp.dot(left, right, preferred_element_type=F32)


def dot_t(left, right):
    return lax.dot_general(left, right, (((1,), (1,)), ((), ())), preferred_element_type=F32)


def t_dot(left, right):
    return lax.dot_general(left, right, (((0,), (0,)), ((), ())), preferred_element_type=F32)


def params(*semantics, limit=LIMIT):
    return pltpu.CompilerParams(dimension_semantics=semantics, vmem_limit_bytes=limit)


def whole(shape):
    rank = len(shape)
    return pl.BlockSpec(shape, lambda *_: (0,) * rank)


def sinusoid(timesteps, features):
    half_width = features // 2
    frequency = jnp.exp(-math.log(10000.0) * jnp.arange(half_width, dtype=F32) / half_width)
    angles = timesteps.astype(F32)[:, None] * frequency[None, :]
    return jnp.concatenate([jnp.cos(angles), jnp.sin(angles)], axis=1)


def swap(value, axis):
    return lax.ppermute(value, axis, [(0, 1), (1, 0)])


def shift(value, axis, size, by):
    return lax.ppermute(value, axis, [(i, (i + by) % size) for i in range(size)])


def gather_near(value):
    far = swap(value, "t1")
    return [value, swap(value, "t0"), far, swap(far, "t0")]


def spread(block, first, second):
    own, one = block, swap(block, first)
    two, both = swap(own, second), swap(one, second)
    if first == "d0":
        found = {(0, 0): own, (1, 0): one, (0, 1): two, (1, 1): both}
    else:
        found = {(0, 0): own, (0, 1): one, (1, 0): two, (1, 1): both}
    out = {}
    for (a, b), value in found.items():
        out[a, b, 0] = value
        out[a, b, 1] = swap(value, "t0")
    return out


def gather_pack(pack, size, orders):
    rows = pack.shape[0]
    if size > 4:
        full = lax.all_gather(pack, ("d1", "d0"), axis=0, tiled=True)
        return [[(value, None, 0)] for value in gather_near(full)], full.shape[0]
    line = [pack] + [shift(pack, "d1", size, by) for by in range(1, size)]
    groups = [[], [], [], []]
    if len(orders) == 1:
        found = spread(jnp.stack(line), *orders[0])
        for (a, b, c), value in found.items():
            groups[b * 2 + c] += [(value, s, a * size + s) for s in range(size)]
    else:
        for s, block in enumerate(line):
            found = spread(block, *orders[s % 2])
            for (a, b, c), value in found.items():
                groups[b * 2 + c].append((value, None, a * size + s))
    return groups, rows


def loader(pieces, rows, arrays):
    plan = []
    for value, lead, slot in pieces:
        for n, known in enumerate(arrays):
            if known is value:
                break
        else:
            n = len(arrays)
            arrays.append(value)
        plan.append((n, lead, slot))
    return plan


def copies(plan, rows, refs, target, base, table, sems):
    out = []
    for k, (n, lead, slot) in enumerate(plan):
        source = refs[n] if lead is None else refs[n].at[lead]
        if table is None:
            start = slot * rows
        else:
            start = pl.multiple_of(table[base + slot], rows)
        out.append(pltpu.make_async_copy(source, target.at[pl.ds(start, rows), :], sems.at[k]))
    return out


def norm(values):
    average = jnp.mean(values, axis=-1, keepdims=True)
    centered = values - average
    variance = jnp.mean(centered * centered, axis=-1, keepdims=True)
    scale = lax.rsqrt(variance + epsilon)
    return centered * scale, scale


def norm_back(gradient, unit, scale):
    one = jnp.mean(gradient, axis=-1, keepdims=True)
    two = jnp.mean(gradient * unit, axis=-1, keepdims=True)
    return scale * (gradient - one - unit * two)


def pack_columns(query, key, value):
    zeros = jnp.zeros_like(key[..., 128:])
    return jnp.concatenate(
        [query[..., :128], key[..., :128], value[..., :128], query[..., 128:], value[..., 128:], key[..., 128:], zeros],
        axis=-1,
    )


def pack_outer(out):
    return jnp.concatenate([jnp.zeros_like(out[..., 128:]), out[..., 128:], out[..., :128]], axis=-1)


def unpack_columns(pack):
    query = jnp.concatenate([pack[..., 0:128], pack[..., 384:448]], axis=-1)
    key = jnp.concatenate([pack[..., 128:256], pack[..., 512:576]], axis=-1)
    value = jnp.concatenate([pack[..., 256:384], pack[..., 448:512]], axis=-1)
    out = jnp.concatenate([pack[..., 640:768], pack[..., 576:640]], axis=-1)
    return query, key, value, out


VMEM = pl.BlockSpec(memory_space=pltpu.VMEM)
SMEM = pl.BlockSpec(memory_space=pltpu.SMEM)


def put_turned(table, base, rows, value, target):
    for k in range(value.shape[0] // rows):
        here = pl.ds(pl.multiple_of(table[base + k], rows), rows)
        target[here, :] = value[k * rows : (k + 1) * rows]


def stem_kernel(rows, base, table, x_a, x_b, x_c, x_d, embed, gain, low_shift, d_ref, keep_ref,
                turned_ref, unit_ref, stream_ref, grad_ref, grad_turned_ref):
    step = pl.program_id(0)
    for near, x_ref in enumerate((x_a, x_b, x_c, x_d)):

        @pl.when(step == near)
        def _(near=near, x_ref=x_ref):
            stream = x_ref[...].astype(F32) + embed[...]
            unit, _ = norm(stream)
            low = (unit * gain[...] + low_shift[...]).astype(BF)
            unit_ref[...] = low
            put_turned(table, base, rows, low.T, turned_ref)
            if near == 0:
                stream_ref[...] = stream
                grad = jnp.where(keep_ref[...] > 0, d_ref[...], jnp.zeros_like(d_ref))
                grad_ref[...] = grad
                put_turned(table, base, rows, grad.T, grad_turned_ref)


def stem(x_near, embed, gain, low_shift, d_out, keep, table, rows, base):
    n, d = x_near[0].shape
    grid_spec = pltpu.PrefetchScalarGridSpec(
        num_scalar_prefetch=1,
        grid=(4,),
        in_specs=[whole((n, d))] * 4 + [whole((1, d))] * 3 + [whole((n, d)), whole((n, 1))],
        out_specs=[
            pl.BlockSpec((d, n), lambda i, t: (0, t[0] ^ i)),
            pl.BlockSpec((n, d), lambda i, t: (t[0] ^ i, 0)),
            whole((n, d)),
            whole((n, d)),
            whole((d, n)),
        ],
    )
    return pl.pallas_call(
        functools.partial(stem_kernel, rows, base),
        grid_spec=grid_spec,
        out_shape=[
            jax.ShapeDtypeStruct((d, 4 * n), BF),
            jax.ShapeDtypeStruct((4 * n, d), BF),
            jax.ShapeDtypeStruct((n, d), F32),
            jax.ShapeDtypeStruct((n, d), BF),
            jax.ShapeDtypeStruct((d, n), BF),
        ],
        compiler_params=params("arbitrary"),
        cost_estimate=pl.CostEstimate(flops=10**7, bytes_accessed=16 * 10**6, transcendentals=0),
        name="stem",
    )(table, *x_near, embed, gain, low_shift, d_out, keep)


def project_kernel(plan, rows, table, unit_ref, bias, scale, *refs):
    count = len({n for n, _, _ in plan})
    pieces, (made_ref, w_ref, sems) = refs[:count], refs[count:]
    todo = copies(plan, rows, pieces, w_ref, 1, table, sems)

    @pl.when(pl.program_id(0) == 0)
    def _():
        for copy in todo:
            copy.start()
        for copy in todo:
            copy.wait()

    made_ref[...] = ((dot(unit_ref[...], w_ref[...]) + bias[...]) * scale[...]).astype(BF)


def project(unit, bias, scale, pieces, rows, table):
    keys, d = unit.shape
    n = keys // 4
    arrays = []
    plan = loader(pieces, rows, arrays)
    grid_spec = pltpu.PrefetchScalarGridSpec(
        num_scalar_prefetch=1,
        grid=(4,),
        in_specs=[pl.BlockSpec((n, d), lambda i, t: (i, 0)), whole(bias.shape), whole(scale.shape)]
        + [pl.BlockSpec(memory_space=pl.ANY)] * len(arrays),
        out_specs=[pl.BlockSpec((n, 640), lambda i, t: (i, 0)), whole((d, 640))],
        scratch_shapes=[pltpu.SemaphoreType.DMA((len(plan),))],
    )
    return pl.pallas_call(
        functools.partial(project_kernel, plan, rows),
        grid_spec=grid_spec,
        out_shape=[jax.ShapeDtypeStruct((keys, 640), BF), jax.ShapeDtypeStruct((d, 640), BF)],
        compiler_params=params("arbitrary"),
        cost_estimate=pl.CostEstimate(flops=4 * 10**9, bytes_accessed=8 * 10**6, transcendentals=0),
        name="project",
    )(table, unit, bias, scale, *arrays)


def low_half(shape):
    return lax.broadcasted_iota(jnp.int32, shape, 1) < HEAD


def pair_bias(key_ref, row, place, start):
    spot = start + lax.broadcasted_iota(jnp.int32, (BLOCK, BLOCK), 0)
    allowed = (key_ref[pl.ds(start, BLOCK), :] == row) | (spot == place)
    return jnp.where(allowed, 0.0, masked)


def block_places(table, near, part, blocks):
    number = (table[0] ^ near) * blocks + part
    return number, pl.multiple_of(number * BLOCK, BLOCK), table[1 + 2 * number], table[2 + 2 * number]


def split_heads(pair, third, third_low):
    half = low_half(pair.shape)
    zero = jnp.zeros_like(pair)
    last = jnp.where(half, third, zero) if third_low else jnp.where(half, zero, third)
    return jnp.where(half, pair, zero), jnp.where(half, zero, pair), last


def attend_kernel(nears, blocks, table, made_ref, key_ref, row_ref, context_a, context_b, total_ref, score_ref):
    for slot, (near, context_ref) in enumerate(zip(nears, (context_a, context_b), strict=True)):
        for part in range(blocks):
            here = pl.ds(part * BLOCK, BLOCK)
            number, own, first, last = block_places(table, near, part, blocks)
            rows = pl.ds(own, BLOCK)
            q_all = split_heads(made_ref[rows, 0:128], made_ref[rows, 384:512], True)
            row = row_ref[pl.ds(number, 1), :]
            place = own + lax.broadcasted_iota(jnp.int32, (BLOCK, BLOCK), 1)

            def score(j, tops, q_all=q_all, row=row, place=place):
                start = pl.multiple_of(j * BLOCK, BLOCK)
                spot = pl.ds(start, BLOCK)
                bias = pair_bias(key_ref, row, place, start)
                out = []
                for h in range(3):
                    keys = made_ref[spot, 128:256] if h < 2 else made_ref[spot, 512:640]
                    s = dot_t(keys, q_all[h]) + bias
                    score_ref[h, j] = s
                    out.append(jnp.maximum(tops[h], jnp.max(s.reshape(BLOCK // 8, 8, BLOCK), axis=0)))
                return tuple(out)

            begin = jnp.full((8, BLOCK), masked, F32)
            tops = lax.fori_loop(first, last, score, (begin,) * 3)
            tops = [jnp.max(t, axis=0, keepdims=True) for t in tops]

            def weigh(j, carry, tops=tops):
                spot = pl.ds(pl.multiple_of(j * BLOCK, BLOCK), BLOCK)
                pair_t = made_ref[spot, 256:384].T
                third_t = made_ref[spot, 384:512].T
                values = (pair_t[:HEAD], pair_t[HEAD:], third_t[HEAD:])
                sums, totals = carry
                new_sums, new_totals = [], []
                for h in range(3):
                    p = jnp.exp(score_ref[h, j] - tops[h])
                    new_totals.append(totals[h] + jnp.sum(p.reshape(BLOCK // 8, 8, BLOCK), axis=0))
                    new_sums.append(sums[h] + dot(values[h], p.astype(BF)))
                return tuple(new_sums), tuple(new_totals)

            zeros = (jnp.zeros((HEAD, BLOCK), F32),) * 3
            sums, totals = lax.fori_loop(first, last, weigh, (zeros, (jnp.zeros((8, BLOCK), F32),) * 3))
            done = []
            for h in range(3):
                total = jnp.sum(totals[h], axis=0, keepdims=True)
                done.append(sums[h] / total)
                total_ref[slot, h, here] = (tops[h] + jnp.log(total))[0]
            context_ref[here, 0:128] = jnp.concatenate([jnp.zeros_like(done[2]), done[2]], axis=0).T.astype(BF)
            context_ref[here, 128:256] = jnp.concatenate([done[0], done[1]], axis=0).T.astype(BF)


def attend(nears, table, made, key, row):
    keys = made.shape[0]
    n = keys // 4
    blocks = n // BLOCK
    return pl.pallas_call(
        functools.partial(attend_kernel, nears, blocks),
        in_specs=[SMEM] + [VMEM] * 3,
        out_specs=[VMEM] * 3,
        out_shape=[
            jax.ShapeDtypeStruct((n, 256), BF),
            jax.ShapeDtypeStruct((n, 256), BF),
            jax.ShapeDtypeStruct((len(nears), 8, n), F32),
        ],
        scratch_shapes=[pltpu.VMEM((3, keys // BLOCK, BLOCK, BLOCK), F32)],
        compiler_params=pltpu.CompilerParams(vmem_limit_bytes=LIMIT),
        cost_estimate=pl.CostEstimate(flops=8 * 10**9, bytes_accessed=4 * 10**6, transcendentals=0),
        name="attend",
    )(table, made, key, row)


def outer_kernel(rows, base, table, context_a, context_b, context_c, context_d, w_ref, stream_ref, gain, low_shift, add,
                 mid_ref, unit_ref, turned_ref):
    mid = stream_ref[...] + add[...]
    for near, context in enumerate((context_a, context_b, context_c, context_d)):
        mid = mid + dot_t(context[...], w_ref[table[0] ^ near])
    mid_ref[...] = mid
    unit, _ = norm(mid)
    low = (unit * gain[...] + low_shift[...]).astype(BF)
    unit_ref[...] = low
    put_turned(table, base, rows, low.T, turned_ref)


def outer(table, contexts, weights, stream, gain, low_shift, add, rows, base):
    n, d = stream.shape
    part = n // 2
    grid_spec = pltpu.PrefetchScalarGridSpec(
        num_scalar_prefetch=1,
        grid=(2,),
        in_specs=[pl.BlockSpec((part, 256), lambda i, t: (i, 0))] * 4
        + [whole(weights.shape), pl.BlockSpec((part, d), lambda i, t: (i, 0))]
        + [whole((1, d))] * 3,
        out_specs=[
            pl.BlockSpec((part, d), lambda i, t: (i, 0)),
            pl.BlockSpec((part, d), lambda i, t: (i, 0)),
            pl.BlockSpec((d, part), lambda i, t: (0, i)),
        ],
    )
    return pl.pallas_call(
        functools.partial(outer_kernel, rows, base),
        grid_spec=grid_spec,
        out_shape=[
            jax.ShapeDtypeStruct((n, d), F32),
            jax.ShapeDtypeStruct((n, d), BF),
            jax.ShapeDtypeStruct((d, n), BF),
        ],
        compiler_params=params("arbitrary"),
        cost_estimate=pl.CostEstimate(flops=2 * 10**9, bytes_accessed=6 * 10**6, transcendentals=0),
        name="outer",
    )(table, *contexts, weights, stream, gain, low_shift, add)


CHUNK = 256


def feed_kernel(near, plan_up, plan_down, rows, table, unit_ref, turned_ref, grad_ref, grad_turned_ref, bias_ref,
                *refs):
    first = near == 1
    arrays = len(refs) - 11 - (0 if first else 2)
    pieces, refs = refs[:arrays], refs[arrays:]
    if not first:
        (out_in, back_in), refs = refs[:2], refs[2:]
    out_ref, back_ref, up_keep, down_keep, up_send, down_send, column_ref, w_up, w_down, sems_up, sems_down = refs
    half = up_keep.shape[0]
    todo_up = copies(plan_up, rows, pieces, w_up, 1, table, sems_up)
    todo_down = copies(plan_down, rows, pieces, w_down, 1, table, sems_down)
    for copy in todo_up + todo_down:
        copy.start()
    for copy in todo_up + todo_down:
        copy.wait()
    bias = bias_ref[...]
    hidden_all, pre_all = [], []
    for step in range(w_up.shape[1] // CHUNK):
        here = slice(step * CHUNK, (step + 1) * CHUNK)
        unit, grad = unit_ref[...], grad_ref[...]
        pre = dot(unit, w_up[:, here]) + bias[:, here]
        d_hidden = dot(grad, w_down[:, here])
        share = 0.5 + 0.5 * lax.erf(pre * math.sqrt(0.5))
        hidden = (pre * share).astype(BF)
        slope = share + pre * (jnp.exp(-0.5 * pre * pre) * (1.0 / math.sqrt(2.0 * math.pi)))
        d_pre = (d_hidden * slope).astype(BF)
        up = dot(turned_ref[...], d_pre).astype(BF)
        down = dot(grad_turned_ref[...], hidden).astype(BF)
        up_keep[:, here], up_send[:, here] = up[:half], up[half:]
        down_keep[:, here], down_send[:, here] = down[:half], down[half:]
        column_ref[:, here] = jnp.sum(d_pre.astype(F32), axis=0, keepdims=True)
        hidden_all.append(hidden)
        pre_all.append(d_pre)
    hidden, d_pre = jnp.concatenate(hidden_all, axis=1), jnp.concatenate(pre_all, axis=1)
    out = dot_t(hidden, w_down[...])
    back = dot_t(d_pre, w_up[...])
    out_ref[...] = out if first else out_in[...] + out
    back_ref[...] = back if first else back_in[...] + back


def feed(near, table, unit, turned, grad, grad_turned, bias, before, up, down, rows):
    n, d = unit.shape
    width = bias.shape[-1]
    arrays = []
    plan_up, plan_down = loader(up, rows, arrays), loader(down, rows, arrays)
    operands = [table, unit, turned, grad, grad_turned, bias, *arrays, *before]
    return pl.pallas_call(
        functools.partial(feed_kernel, near, plan_up, plan_down, rows),
        in_specs=[SMEM] + [VMEM] * 5 + [pl.BlockSpec(memory_space=pl.ANY)] * len(arrays) + [VMEM] * len(before),
        out_specs=[VMEM] * 7,
        out_shape=[jax.ShapeDtypeStruct((n, d), F32)] * 2
        + [jax.ShapeDtypeStruct((d // 2, width), BF)] * 4
        + [jax.ShapeDtypeStruct((1, width), F32)],
        scratch_shapes=[
            pltpu.VMEM((d, width), BF),
            pltpu.VMEM((d, width), BF),
            pltpu.SemaphoreType.DMA((len(plan_up),)),
            pltpu.SemaphoreType.DMA((len(plan_down),)),
        ],
        compiler_params=pltpu.CompilerParams(vmem_limit_bytes=LIMIT),
        cost_estimate=pl.CostEstimate(flops=5 * 10**9, bytes_accessed=8 * 10**6, transcendentals=0),
        name="feed",
    )(*operands)


def middle_kernel(out_ref, back_ref, mid_ref, grad_ref, gain, add, low_ref, full_ref, short_ref, sums_ref):
    mid = mid_ref[...]
    low_ref[...] = (mid + out_ref[...] + add[...]).astype(BF)
    unit, scale = norm(mid)
    back = back_ref[...]
    grad = grad_ref[...].astype(F32)
    full = grad + norm_back(back * gain[...], unit, scale)
    full_ref[...] = full
    short_ref[...] = full.astype(BF)
    sums_ref[...] = jnp.zeros_like(sums_ref)
    sums_ref[0:1] = jnp.sum(back * unit, axis=0, keepdims=True)
    sums_ref[1:2] = jnp.sum(back, axis=0, keepdims=True)
    sums_ref[2:3] = jnp.sum(full, axis=0, keepdims=True)
    sums_ref[3:4] = jnp.sum(grad, axis=0, keepdims=True)


def middle(out, back, mid, grad, gain, add):
    n, d = mid.shape
    return pl.pallas_call(
        middle_kernel,
        in_specs=[VMEM] * 6,
        out_specs=[VMEM] * 4,
        out_shape=[
            jax.ShapeDtypeStruct((n, d), BF),
            jax.ShapeDtypeStruct((n, d), F32),
            jax.ShapeDtypeStruct((n, d), BF),
            jax.ShapeDtypeStruct((8, d), F32),
        ],
        compiler_params=pltpu.CompilerParams(vmem_limit_bytes=LIMIT),
        cost_estimate=pl.CostEstimate(flops=10**7, bytes_accessed=10 * 10**6, transcendentals=0),
        name="middle",
    )(out, back, mid, grad, gain, add)


def back_kernel(nears, blocks, last_call, table, made_ref, key_ref, row_ref, total_ref, w_ref, short_a, short_b, *refs):
    if last_call:
        before_ref, dq_a, dq_b, out_ref, d_ref, p_ref, dp_ref, sum_ref = refs
        sum_ref[...] = before_ref[...]
    else:
        dq_a, dq_b, sum_ref, d_ref, p_ref, dp_ref = refs
        sum_ref[...] = jnp.zeros_like(sum_ref)
    scale = HEAD ** (-0.5)
    for slot, (near, short, dq_ref) in enumerate(zip(nears, (short_a, short_b), (dq_a, dq_b), strict=True)):
        d_ref[...] = dot(short[...], w_ref[table[0]]).astype(BF)
        for part in range(blocks):
            here = pl.ds(part * BLOCK, BLOCK)
            number, own, first, last = block_places(table, near, part, blocks)
            rows = pl.ds(own, BLOCK)
            q_all = split_heads(made_ref[rows, 0:128], made_ref[rows, 384:512], True)
            d_all = split_heads(d_ref[here, 128:256], d_ref[here, 0:128], False)
            row = row_ref[pl.ds(number, 1), :]
            place = own + lax.broadcasted_iota(jnp.int32, (BLOCK, BLOCK), 1)
            totals = [total_ref[slot, h : h + 1, here] for h in range(3)]

            def weigh(j, inners, q_all=q_all, d_all=d_all, row=row, place=place, totals=totals):
                start = pl.multiple_of(j * BLOCK, BLOCK)
                spot = pl.ds(start, BLOCK)
                bias = pair_bias(key_ref, row, place, start)
                new, add_v = [], []
                for h in range(3):
                    keys = made_ref[spot, 128:256] if h < 2 else made_ref[spot, 512:640]
                    values = made_ref[spot, 256:384] if h < 2 else made_ref[spot, 384:512]
                    p = jnp.exp(dot_t(keys, q_all[h]) + bias - totals[h])
                    d_p = dot_t(values, d_all[h])
                    p_ref[h, j] = p
                    dp_ref[h, j] = d_p
                    new.append(inners[h] + jnp.sum((p * d_p).reshape(BLOCK // 8, 8, BLOCK), axis=0))
                    add_v.append(dot(p.astype(BF), d_all[h]))
                sum_ref[spot, 128:256] += add_v[0] + add_v[1]
                sum_ref[spot, 256:384] += add_v[2]
                return tuple(new)

            inners = lax.fori_loop(first, last, weigh, (jnp.zeros((8, BLOCK), F32),) * 3)
            inners = [jnp.sum(v, axis=0, keepdims=True) for v in inners]

            def turn(j, sums, q_all=q_all, inners=inners):
                spot = pl.ds(pl.multiple_of(j * BLOCK, BLOCK), BLOCK)
                pair_t, third_t = made_ref[spot, 128:256].T, made_ref[spot, 512:640].T
                turned = (pair_t[:HEAD], pair_t[HEAD:], third_t[:HEAD])
                new, add_k = [], []
                for h in range(3):
                    d_s = (p_ref[h, j] * (dp_ref[h, j] - inners[h])).astype(BF)
                    add_k.append(dot(d_s, q_all[h]))
                    new.append(sums[h] + dot(turned[h], d_s))
                sum_ref[spot, 0:128] += add_k[0] + add_k[1]
                sum_ref[spot, 384:512] += add_k[2]
                return tuple(new)

            sums = lax.fori_loop(first, last, turn, (jnp.zeros((HEAD, BLOCK), F32),) * 3)
            two = jnp.concatenate([sums[0], sums[1]], axis=0).T.astype(BF) * jnp.asarray(scale, BF)
            one = jnp.concatenate([sums[2], jnp.zeros_like(sums[2])], axis=0).T.astype(BF) * jnp.asarray(scale, BF)
            dq_ref[here, :] = two
            sum_ref[rows, 256:384] += one.astype(F32)
    if last_call:
        out_ref[...] = sum_ref[...].astype(BF)


def attend_back(nears, table, made, key, row, total, w, shorts, before):
    keys = made.shape[0]
    n = keys // 4
    last_call = before is not None
    operands = [table, made, key, row, total, w, *shorts] + ([before] if last_call else [])
    scores = pltpu.VMEM((3, keys // BLOCK, BLOCK, BLOCK), F32)
    scratch = [pltpu.VMEM((n, 256), BF), scores, scores]
    if last_call:
        scratch.append(pltpu.VMEM((keys, 512), F32))
    return pl.pallas_call(
        functools.partial(back_kernel, nears, n // BLOCK, last_call),
        in_specs=[SMEM] + [VMEM] * (len(operands) - 1),
        out_specs=[VMEM] * 3,
        out_shape=[
            jax.ShapeDtypeStruct((n, 128), BF),
            jax.ShapeDtypeStruct((n, 128), BF),
            jax.ShapeDtypeStruct((keys, 512), BF if last_call else F32),
        ],
        scratch_shapes=scratch,
        compiler_params=pltpu.CompilerParams(vmem_limit_bytes=LIMIT),
        cost_estimate=pl.CostEstimate(flops=14 * 10**9, bytes_accessed=10 * 10**6, transcendentals=0),
        name="attend_back",
    )(*operands)


def unit_back_kernel(table, dq_a, dq_b, dq_c, dq_d, dkv_ref, w_ref, out_a, out_b, out_c, out_d):
    n = dq_a.shape[0]
    for near, (dq, out) in enumerate(zip((dq_a, dq_b, dq_c, dq_d), (out_a, out_b, out_c, out_d), strict=True)):
        rows = pl.ds(pl.multiple_of((table[0] ^ near) * n, n), n)
        out[...] = (dot_t(dkv_ref[rows, :], w_ref[:, 128:640]) + dot_t(dq[...], w_ref[:, 0:128])).astype(BF)


def unit_back(table, dqs, dkv, w):
    n, d = dqs[0].shape[0], w.shape[0]
    return pl.pallas_call(
        unit_back_kernel,
        in_specs=[SMEM] + [VMEM] * 6,
        out_specs=[VMEM] * 4,
        out_shape=[jax.ShapeDtypeStruct((n, d), BF)] * 4,
        compiler_params=pltpu.CompilerParams(vmem_limit_bytes=LIMIT),
        cost_estimate=pl.CostEstimate(flops=4 * 10**9, bytes_accessed=6 * 10**6, transcendentals=0),
        name="unit_back",
    )(table, *dqs, dkv, w)


def grads_kernel(rows, base, table, turned_ref, dkv_ref, *refs):
    dqs, shorts, contexts, (keep_ref, send_ref, column_ref, sum_ref) = refs[:4], refs[4:8], refs[8:12], refs[12:]
    n = dqs[0].shape[0]
    half = keep_ref.shape[0]
    dkv = dkv_ref[...]
    sum_ref[:, 128:640] = dot(turned_ref[...], dkv)
    column_ref[:, 128:640] = jnp.sum(dkv.astype(F32), axis=0, keepdims=True)
    made, column, out = 0.0, 0.0, 0.0
    for near in range(4):
        here = pl.ds(pl.multiple_of((table[0] ^ near) * n, n), n)
        dq = dqs[near][...]
        made = made + dot(turned_ref[:, here], dq)
        column = column + jnp.sum(dq.astype(F32), axis=0, keepdims=True)
        out = out + t_dot(shorts[near][...], contexts[near][...])
    sum_ref[:, 0:128] = made
    column_ref[:, 0:128] = column
    for k in range(out.shape[0] // rows):
        here = pl.ds(pl.multiple_of(table[base + k], rows), rows)
        part = out[k * rows : (k + 1) * rows]
        sum_ref[here, 512:640] += part[:, :128]
        sum_ref[here, 640:768] = part[:, 128:]
    keep_ref[...] = sum_ref[:half, :].astype(BF)
    send_ref[...] = sum_ref[half:, :].astype(BF)


def grads(table, turned, dqs, dkv, shorts, contexts, rows, base):
    d = turned.shape[0]
    return pl.pallas_call(
        functools.partial(grads_kernel, rows, base),
        in_specs=[SMEM] + [VMEM] * 14,
        out_specs=[VMEM] * 3,
        out_shape=[
            jax.ShapeDtypeStruct((d // 2, 768), BF),
            jax.ShapeDtypeStruct((d // 2, 768), BF),
            jax.ShapeDtypeStruct((1, 640), F32),
        ],
        scratch_shapes=[pltpu.VMEM((d, 768), F32)],
        compiler_params=pltpu.CompilerParams(vmem_limit_bytes=LIMIT),
        cost_estimate=pl.CostEstimate(flops=6 * 10**9, bytes_accessed=12 * 10**6, transcendentals=0),
        name="grads",
    )(table, turned, dkv, *dqs, *shorts, *contexts)


def final_kernel(one_ref, two_ref, stream_ref, full_ref, gain, grad_ref, sums_ref):
    back = one_ref[...] + two_ref[...].astype(F32)
    unit, scale = norm(stream_ref[...])
    grad = full_ref[...] + norm_back(back * gain[...], unit, scale)
    grad_ref[...] = grad
    sums_ref[...] = jnp.zeros_like(sums_ref)
    sums_ref[0:1] = jnp.sum(back * unit, axis=0, keepdims=True)
    sums_ref[1:2] = jnp.sum(back, axis=0, keepdims=True)
    sums_ref[2:3] = jnp.sum(grad, axis=0, keepdims=True)


def final(one, two, stream, full, gain):
    n, d = stream.shape
    return pl.pallas_call(
        final_kernel,
        grid=(1,),
        in_specs=[whole((n, d))] * 4 + [whole((1, d))],
        out_specs=[whole((n, d)), whole((8, d))],
        out_shape=[jax.ShapeDtypeStruct((n, d), F32), jax.ShapeDtypeStruct((8, d), F32)],
        compiler_params=params("arbitrary"),
        cost_estimate=pl.CostEstimate(flops=10**7, bytes_accessed=7 * 10**6, transcendentals=0),
        name="final",
    )(one, two, stream, full, gain)


def add_low(one, two):
    return (one.astype(F32) + two.astype(F32)).astype(BF)


def tie(values, after):
    return lax.optimization_barrier((values, after))[0]


def scatter_line(mine, size):
    rows = mine.shape[0] // size
    total = mine[:rows].astype(F32)
    for by in range(1, size):
        total = total + shift(mine[by * rows : (by + 1) * rows], "d1", size, by).astype(F32)
    return total


def sum_dp(value, size):
    value = value + swap(value, "d0")
    if size > 4:
        return lax.psum(value, "d1")
    total = value
    for by in range(1, size):
        total = total + shift(value, "d1", size, by)
    return total


def scatter_dp(value):
    return lax.psum_scatter(value, ("d1", "d0"), scatter_dimension=0, tiled=True).astype(F32)


def shards(
    inputs,
    segment_ids,
    keep_mask,
    timestep,
    w_qkv,
    b_query,
    b_value,
    w_out,
    w_up,
    b_up,
    w_down,
    time_weight,
    gains,
    row_biases,
    d_out,
):
    size = lax.axis_size("d1")
    long = size > 4
    z, x = lax.axis_index("d1"), lax.axis_index("d0")
    own = lax.axis_index("t1") * 2 + lax.axis_index("t0")
    n, d = inputs.shape
    dp = 2 * size
    place = z * 2 + x
    features = time_weight.shape[0]
    columns = time_weight.shape[1]

    pack_one = pack_columns(w_qkv[0], w_qkv[1], w_qkv[2])
    rows = pack_one.shape[0]
    if long:
        pieces_one = [(lax.all_gather(pack_one, ("d1", "d0"), axis=0, tiled=True), None, 0)]
        line, half = [pack_one], pack_one
    else:
        line = [pack_one] + [shift(pack_one, "d1", size, by) for by in range(1, size)]
        half = jnp.stack(line)
        other_half = swap(half, "d0")
        pieces_one = [(half, s, s) for s in range(size)] + [(other_half, s, size + s) for s in range(size)]
    x_near = gather_near(inputs)
    time_rows = sinusoid(timestep, features).astype(BF)
    if long:
        full_time = lax.all_gather(time_weight, ("d1", "d0"), axis=1, tiled=True)
        embed = dot(time_rows, full_time)
        all_rows = lax.all_gather(time_rows, ("d1", "d0"), axis=0, tiled=True)
    else:
        time_pack = jnp.concatenate(
            [jnp.pad(time_weight, ((0, 0), (0, 128 - columns))), jnp.pad(time_rows, ((0, 15), (0, 0)))]
        )
        time_both = jnp.stack([time_pack, swap(time_pack, "d0")])
        time_line = [time_both] + [shift(time_both, "d1", size, by) for by in range(1, size)]
        spots = [lax.rem(z - by + size, size) * 2 + (x ^ a) for by in range(size) for a in range(2)]
        order = (jnp.arange(dp)[:, None] == jnp.stack(spots)[None, :]).astype(F32)
        time_all = jnp.concatenate(time_line)
        parts = jnp.einsum("of,pfc->pc", time_rows, time_all[:, :features, :columns], preferred_element_type=F32)
        embed = jnp.dot(order, parts, precision=highest).reshape(1, d)
        all_rows = jnp.dot(order, time_all[:, features, :].astype(F32), precision=highest)
    embed = embed + row_biases[4][None, :]
    outer_all = lax.all_gather(pack_outer(w_out.T), ("t1", "t0", "d1", "d0"), axis=0, tiled=True).reshape(4, d, 256)
    up_near = gather_near(b_up[None])
    bias_one = pack_columns(b_query, jnp.zeros_like(b_query), b_value)[None, :]

    blocks = 4 * n // BLOCK
    ids = segment_ids.reshape(blocks, BLOCK)
    first = jnp.sum(segment_ids[None, :] < ids[:, :1], axis=1, dtype=jnp.int32)
    last = jnp.sum(segment_ids[None, :] <= ids[:, -1:], axis=1, dtype=jnp.int32)
    span = jnp.stack([first // BLOCK, (last + BLOCK - 1) // BLOCK], axis=1).reshape(-1)
    slots = [(lax.rem(z - s + size, size) * 2 + (x ^ a)) * rows for a in range(2) for s in range(size)]
    places = [((k % 2 ^ x) * size + lax.rem(k // 2 - z + size, size)) * rows for k in range(dp)]
    if long:
        slots, places, turn_rows = [jnp.zeros_like(own)], [jnp.zeros_like(own)], d
    else:
        turn_rows = rows
    base = 1 + len(slots)
    table_one = jnp.stack([own, *slots, *places]).astype(jnp.int32)
    table_two = jnp.concatenate([jnp.stack([own]), span]).astype(jnp.int32)
    key = jnp.where(keep_mask > 0, segment_ids, -1)[:, None]
    own_keep = lax.dynamic_slice_in_dim(keep_mask, own * n, n, 0)[:, None]
    scale = jnp.where(
        (jnp.arange(640) < 128) | ((jnp.arange(640) >= 384) & (jnp.arange(640) < 448)), HEAD ** (-0.5), 1.0
    ).astype(F32)[None, :]

    groups_up, rows_two = gather_pack(tie(w_up, half), size, [("d0", "t1")])
    groups_down, _ = gather_pack(tie(w_down.T, half), size, [("t1", "d0")])

    turned_one, unit_one, stream_in, grad_two, grad_turned = stem(
        x_near, embed, gains[0:1], row_biases[0:1], d_out, own_keep, table_one, turn_rows, base
    )
    made, w_one = project(unit_one, bias_one, scale, pieces_one, d if long else rows, table_one)
    context_c, context_d, total_far = attend((2, 3), table_two, made, key, ids)
    over_c, over_d = swap(context_c, "t1"), swap(context_d, "t1")
    context_a, context_b, total_near = attend((0, 1), table_two, made, key, ids)
    contexts = [context_a, swap(context_b, "t0"), over_c, swap(over_d, "t0")]
    stream_mid, unit_two, turned_two = outer(
        table_one, contexts, outer_all, stream_in, gains[1:2], row_biases[1:2], row_biases[2:3], turn_rows, base
    )

    def feed_group(near, before, after):
        unit = tie(unit_two, after) if after else unit_two
        out, back, up_keep, down_keep, up_send, down_send, column = feed(
            near, table_one, unit, turned_two, grad_two, grad_turned, up_near[near], before,
            groups_up[near], groups_down[near], rows_two,
        )
        return (out, back), (up_keep, down_keep), (up_send, down_send), column

    def to_core(values):
        return [swap(v, "t0") for v in values]

    def low_sums(*terms):
        return [functools.reduce(jnp.add, [v.astype(F32) for v in vs]).astype(BF) for vs in zip(*terms, strict=True)]

    sums, keep, send, column_b = feed_group(1, (), ())
    keep_b, send_b = to_core(keep), to_core(send)
    sums, keep_a, send_a, column_a = feed_group(0, sums, ())
    sent_a = low_sums(send_a, send_b)
    over_a = sent_a if long else [swap(v, "d0") for v in sent_a]
    sums, keep, send, column_d = feed_group(3, sums, sent_a)
    keep_d, send_d = to_core(keep), to_core(send)
    sums, keep_c, send_c, column_c = feed_group(2, sums, ())
    output, full, short, sums_two = middle(*sums, stream_mid, grad_two, gains[1:2], row_biases[3:4])
    short_near = gather_near(short)
    sent_c = low_sums(tie(send_c, short), send_d)
    over_c = sent_c if long else [swap(v, "d0") for v in sent_c]
    shorts = tie(short_near[:2], sent_c)
    dq_a, dq_b, sum_near = attend_back((0, 1), table_two, made, key, ids, total_near, outer_all, shorts, None)
    if long:
        kept_c = low_sums(keep_c, keep_d)
        kept_over = [swap(v, "t1") for v in kept_c + sent_c]
        kept_a = low_sums(keep_a, keep_b)
        mines = low_sums(kept_a + sent_a, kept_over)
        up_share, down_share = [scatter_dp(jnp.concatenate([mines[k], mines[2 + k]])) for k in range(2)]
        shorts = short_near[2:]
    else:
        kept_c = low_sums(keep_c, keep_d, tie(over_c, sum_near))
        kept_over = [swap(v, "t1") for v in kept_c]
        shorts = tie(short_near[2:], kept_c)
    dq_c, dq_d, dkv = attend_back((2, 3), table_two, made, key, ids, total_far, outer_all, shorts, sum_near)
    dqs = [dq_a, dq_b, dq_c, dq_d]
    back_a, back_b, back_c, back_d = unit_back(table_two, dqs, dkv, w_one)
    back_b, back_d = swap(back_b, "t0"), swap(back_d, "t0")
    dqs_late = dqs
    if not long:
        mines = low_sums(keep_a, keep_b, over_a, tie(kept_over, back_a))
        dqs_late = tie(dqs, mines)
        up_share, down_share = [scatter_line(v, size) for v in mines]
    mine = add_low(back_a, back_b)
    other = swap(add_low(back_c, back_d), "t1")
    grad_keep, grad_send, column_one = grads(
        table_one, turned_one, dqs_late, dkv, short_near, [context_a, context_b, context_c, context_d], turn_rows, base
    )
    if long:
        one_share = scatter_dp(jnp.concatenate([grad_keep, grad_send]))
    else:
        (one_mine,) = low_sums([grad_keep], [swap(grad_send, "d0")])
        one_share = scatter_line(one_mine, size)
        other, up_share, down_share = lax.optimization_barrier((other, up_share, down_share))
    grad_input, sums_one = final(mine.astype(F32), other, stream_in, full, gains[0:1])

    both = jnp.concatenate([sums_one[:3], sums_two[:4], column_b, column_d])
    there = swap(both, "t0")
    both = jnp.concatenate([both[:7] + there[:7], column_a + there[7:8], column_c + there[8:9]])
    there = swap(jnp.concatenate([both[:7], both[8:9]]), "t1")
    both = jnp.concatenate([both[:7] + there[:7], both[7:8] + there[7:8], jnp.pad(column_one, ((0, 0), (0, d - 640)))])
    seat = (jnp.arange(dp) == place).astype(F32)
    total = sum_dp(jnp.concatenate([both[:2], both[3:], seat[:, None] * both[2:3]]), size)
    by_sequence = total[8:]
    own_columns = lax.dynamic_slice_in_dim(by_sequence, place * columns, columns, 1)
    grad_time = lax.dot_general(
        all_rows.astype(F32), own_columns, (((0,), (0,)), ((), ())), precision=highest, preferred_element_type=F32
    )
    d_query, d_key, d_value, d_outer = unpack_columns(one_share)
    column_query, _, column_value, _ = unpack_columns(total[7])
    gain_total = jnp.stack([total[0], total[2]])
    bias_total = jnp.stack([total[1], total[3], total[4], total[5], jnp.sum(by_sequence, axis=0)])
    return (
        output,
        grad_input,
        jnp.stack([d_query, d_key, d_value]),
        column_query,
        column_value,
        d_outer.T,
        up_share,
        total[6],
        down_share.T,
        grad_time,
        gain_total,
        bias_total,
    )


def solution(mesh):
    dp, tensor = mesh.shape["dp"], mesh.shape["tensor"]
    fine = Mesh(mesh.devices.reshape(dp // 2, 2, tensor // 2, 2), ("d1", "d0", "t1", "t0"))
    rows, cols = ("d1", "d0"), ("t1", "t0")
    every = rows + cols
    in_specs = (
        P(every, None),
        P(rows),
        P(rows),
        P(rows),
        P(None, rows, cols),
        P(cols),
        P(cols),
        P(cols, rows),
        P(rows, cols),
        P(cols),
        P(cols, rows),
        P(None, rows),
        P(),
        P(),
        P(every, None),
    )
    out_specs = (
        P(every, None),
        P(every, None),
        P(None, rows, cols),
        P(cols),
        P(cols),
        P(cols, rows),
        P(rows, cols),
        P(cols),
        P(cols, rows),
        P(None, rows),
        P(),
        P(),
    )
    return jax.shard_map(shards, mesh=fine, in_specs=in_specs, out_specs=out_specs, check_vma=False)
```

```python
import functools
import math

import jax
import jax.numpy as jnp
from jax import lax
from jax.experimental import pallas as pl
from jax.experimental.pallas import tpu as pltpu
from jax.sharding import Mesh
from jax.sharding import PartitionSpec as P

HEAD = 64
SEQ_LEN = 2048
BLOCK = 256
F32 = jnp.float32
BF = jnp.bfloat16

epsilon = 1e-05
masked = -1e30
highest = lax.Precision.HIGHEST

LIMIT = 32 << 20
COST = pl.CostEstimate(flops=10**5, bytes_accessed=10**5, transcendentals=0)


def dot(left, right):
    return jnp.dot(left, right, preferred_element_type=F32)


def dot_t(left, right):
    return lax.dot_general(left, right, (((1,), (1,)), ((), ())), preferred_element_type=F32)


def t_dot(left, right):
    return lax.dot_general(left, right, (((0,), (0,)), ((), ())), preferred_element_type=F32)


def params(*semantics, limit=LIMIT):
    return pltpu.CompilerParams(dimension_semantics=semantics, vmem_limit_bytes=limit)


def whole(shape):
    rank = len(shape)
    return pl.BlockSpec(shape, lambda *_: (0,) * rank)


def stage(sources, buffers, sems):
    going = [pltpu.make_async_copy(s, b, sems.at[k]) for k, (s, b) in enumerate(zip(sources, buffers, strict=True))]
    for copy in going:
        copy.start()
    return going


def buffers_of(values):
    return [pltpu.VMEM(v.shape, v.dtype) for v in values] + [pltpu.SemaphoreType.DMA((len(values),))]


def sinusoid(timesteps, features):
    half_width = features // 2
    frequency = jnp.exp(-math.log(10000.0) * jnp.arange(half_width, dtype=F32) / half_width)
    angles = timesteps.astype(F32)[:, None] * frequency[None, :]
    return jnp.concatenate([jnp.cos(angles), jnp.sin(angles)], axis=1)


def swap(value, axis):
    return lax.ppermute(value, axis, [(0, 1), (1, 0)])


def shift(value, axis, size, by):
    return lax.ppermute(value, axis, [(i, (i + by) % size) for i in range(size)])


def gather_near(value):
    far = swap(value, "t1")
    return [value, swap(value, "t0"), far, swap(far, "t0")]


def to_core(values):
    return [swap(v, "t0") for v in values]


def loader(pieces, rows, arrays):
    plan = []
    for value, lead, slot in pieces:
        for n, known in enumerate(arrays):
            if known is value:
                break
        else:
            n = len(arrays)
            arrays.append(value)
        plan.append((n, lead, slot))
    return plan


def copies(plan, rows, refs, target, base, table, sems):
    out = []
    for k, (n, lead, slot) in enumerate(plan):
        source = refs[n] if lead is None else refs[n].at[lead]
        if table is None:
            start = slot * rows
        else:
            start = pl.multiple_of(table[base + slot], rows)
        out.append(pltpu.make_async_copy(source, target.at[pl.ds(start, rows), :], sems.at[k]))
    return out


def norm(values):
    average = jnp.mean(values, axis=-1, keepdims=True)
    centered = values - average
    variance = jnp.mean(centered * centered, axis=-1, keepdims=True)
    scale = lax.rsqrt(variance + epsilon)
    return centered * scale, scale


def norm_back(gradient, unit, scale):
    one = jnp.mean(gradient, axis=-1, keepdims=True)
    two = jnp.mean(gradient * unit, axis=-1, keepdims=True)
    return scale * (gradient - one - unit * two)


def pack_columns(query, key, value):
    zeros = jnp.zeros_like(key[..., 128:])
    return jnp.concatenate(
        [query[..., :128], key[..., :128], value[..., :128], query[..., 128:], value[..., 128:], key[..., 128:], zeros],
        axis=-1,
    )


def pack_outer(out):
    return jnp.concatenate([jnp.zeros_like(out[..., 128:]), out[..., 128:], out[..., :128]], axis=-1)


def unpack_columns(pack):
    query = jnp.concatenate([pack[..., 0:128], pack[..., 384:448]], axis=-1)
    key = jnp.concatenate([pack[..., 128:256], pack[..., 512:576]], axis=-1)
    value = jnp.concatenate([pack[..., 256:384], pack[..., 448:512]], axis=-1)
    out = jnp.concatenate([pack[..., 640:768], pack[..., 576:640]], axis=-1)
    return query, key, value, out


VMEM = pl.BlockSpec(memory_space=pltpu.VMEM)
SMEM = pl.BlockSpec(memory_space=pltpu.SMEM)
HBM = pl.BlockSpec(memory_space=pltpu.HBM)


def put_turned(table, base, rows, value, target):
    for k in range(value.shape[0] // rows):
        here = pl.ds(pl.multiple_of(table[base + k], rows), rows)
        target[here, :] = value[k * rows : (k + 1) * rows]


def cotangent_kernel(rows, base, table, d_ref, keep_ref, grad_ref, turned_ref):
    grad = jnp.where(keep_ref[...] > 0, d_ref[...], jnp.zeros_like(d_ref))
    grad_ref[...] = grad
    put_turned(table, base, rows, grad.T, turned_ref)


def cotangent(table, d_out, keep, rows, base):
    n, d = d_out.shape
    return pl.pallas_call(
        functools.partial(cotangent_kernel, rows, base),
        in_specs=[SMEM, VMEM, VMEM],
        out_specs=[VMEM, VMEM],
        out_shape=[jax.ShapeDtypeStruct((n, d), BF), jax.ShapeDtypeStruct((d, n), BF)],
        compiler_params=pltpu.CompilerParams(vmem_limit_bytes=LIMIT),
        cost_estimate=COST,
        name="cotangent",
    )(table, d_out, keep)


def project_kernel(plan, rows, turn_rows, base, table, x_a, x_b, x_c, x_d, times, add, gain, low_shift, bias, scale, *refs):
    count = len({n for n, _, _ in plan})
    pieces, (made_ref, turned_ref, stream_ref, w_ref, sems, *buffers, stage_sems) = refs[:count], refs[count:]
    n = x_a.shape[0]
    todo = copies(plan, rows, pieces, w_ref, 1, table, sems)
    for copy in todo:
        copy.start()
    inputs = stage((x_a, x_b, x_c, x_d), buffers, stage_sems)
    for copy in todo:
        copy.wait()
    embed = dot_t(times[...], w_ref[:, 640:768])[0:1] + add[...]

    def rows_of(near):
        inputs[near].wait()
        stream = buffers[near][...].astype(F32) + embed
        if near == 0:
            stream_ref[...] = stream
        unit, _ = norm(stream)
        return (unit * gain[...] + low_shift[...]).astype(BF)

    low = rows_of(0)
    for near in range(4):
        here = pl.ds(pl.multiple_of((table[0] ^ near) * n, n), n)
        made_ref[here, :] = ((dot(low, w_ref[:, :640]) + bias[...]) * scale[...]).astype(BF)
        put_turned(table, base, turn_rows, low.T, turned_ref.at[:, here])
        if near < 3:
            low = rows_of(near + 1)


def project(x_near, times, add, gain, low_shift, bias, scale, pieces, rows, table, turn_rows, base):
    n, d = x_near[0].shape
    arrays = []
    plan = loader(pieces, rows, arrays)
    return pl.pallas_call(
        functools.partial(project_kernel, plan, rows, turn_rows, base),
        in_specs=[SMEM] + [HBM] * 4 + [VMEM] * 6 + [pl.BlockSpec(memory_space=pl.ANY)] * len(arrays),
        out_specs=[VMEM] * 4,
        out_shape=[
            jax.ShapeDtypeStruct((4 * n, 640), BF),
            jax.ShapeDtypeStruct((d, 4 * n), BF),
            jax.ShapeDtypeStruct((n, d), F32),
            jax.ShapeDtypeStruct((d, 768), BF),
        ],
        scratch_shapes=[pltpu.SemaphoreType.DMA((len(plan),))] + buffers_of(x_near),
        compiler_params=pltpu.CompilerParams(vmem_limit_bytes=LIMIT),
        cost_estimate=COST,
        name="project",
    )(table, *x_near, times, add, gain, low_shift, bias, scale, *arrays)


def low_half(shape):
    return lax.broadcasted_iota(jnp.int32, shape, 1) < HEAD


def pair_bias(key_ref, row, place, start):
    spot = start + lax.broadcasted_iota(jnp.int32, (BLOCK, BLOCK), 0)
    allowed = (key_ref[pl.ds(start, BLOCK), :] == row) | (spot == place)
    return jnp.where(allowed, 0.0, masked)


def block_places(table, near, part, blocks):
    number = (table[0] ^ near) * blocks + part
    return number, pl.multiple_of(number * BLOCK, BLOCK), table[1 + 2 * number], table[2 + 2 * number]


def split_heads(pair, third, third_low):
    half = low_half(pair.shape)
    zero = jnp.zeros_like(pair)
    last = jnp.where(half, third, zero) if third_low else jnp.where(half, zero, third)
    return jnp.where(half, pair, zero), jnp.where(half, zero, pair), last


def attend_kernel(nears, blocks, table, made_ref, key_ref, row_ref, *refs):
    context_refs, (total_ref, score_ref) = refs[:-2], refs[-2:]
    n = blocks * BLOCK
    for slot, near in enumerate(nears):
        context_ref = context_refs[slot] if len(context_refs) > 1 else context_refs[0].at[pl.ds(slot * n, n)]
        for part in range(blocks):
            here = pl.ds(part * BLOCK, BLOCK)
            number, own, first, last = block_places(table, near, part, blocks)
            rows = pl.ds(own, BLOCK)
            q_all = split_heads(made_ref[rows, 0:128], made_ref[rows, 384:512], True)
            row = row_ref[pl.ds(number, 1), :]
            place = own + lax.broadcasted_iota(jnp.int32, (BLOCK, BLOCK), 1)

            def score(j, tops, q_all=q_all, row=row, place=place):
                start = pl.multiple_of(j * BLOCK, BLOCK)
                spot = pl.ds(start, BLOCK)
                bias = pair_bias(key_ref, row, place, start)
                out = []
                for h in range(3):
                    keys = made_ref[spot, 128:256] if h < 2 else made_ref[spot, 512:640]
                    s = dot_t(keys, q_all[h]) + bias
                    score_ref[h, j] = s
                    out.append(jnp.maximum(tops[h], jnp.max(s.reshape(BLOCK // 8, 8, BLOCK), axis=0)))
                return tuple(out)

            begin = jnp.full((8, BLOCK), masked, F32)
            tops = lax.fori_loop(first, last, score, (begin,) * 3)
            tops = [jnp.max(t, axis=0, keepdims=True) for t in tops]

            def weigh(j, carry, tops=tops):
                spot = pl.ds(pl.multiple_of(j * BLOCK, BLOCK), BLOCK)
                pair_t = made_ref[spot, 256:384].T
                third_t = made_ref[spot, 384:512].T
                values = (pair_t[:HEAD], pair_t[HEAD:], third_t[HEAD:])
                sums, totals = carry
                new_sums, new_totals = [], []
                for h in range(3):
                    p = jnp.exp(score_ref[h, j] - tops[h])
                    new_totals.append(totals[h] + jnp.sum(p.reshape(BLOCK // 8, 8, BLOCK), axis=0))
                    new_sums.append(sums[h] + dot(values[h], p.astype(BF)))
                return tuple(new_sums), tuple(new_totals)

            zeros = (jnp.zeros((HEAD, BLOCK), F32),) * 3
            sums, totals = lax.fori_loop(first, last, weigh, (zeros, (jnp.zeros((8, BLOCK), F32),) * 3))
            done = []
            for h in range(3):
                total = jnp.sum(totals[h], axis=0, keepdims=True)
                done.append(sums[h] / total)
                total_ref[slot, h, here] = (tops[h] + jnp.log(total))[0]
            context_ref[here, 0:128] = jnp.concatenate([jnp.zeros_like(done[2]), done[2]], axis=0).T.astype(BF)
            context_ref[here, 128:256] = jnp.concatenate([done[0], done[1]], axis=0).T.astype(BF)


def attend(nears, table, made, key, row, joined):
    keys = made.shape[0]
    n = keys // 4
    blocks = n // BLOCK
    return pl.pallas_call(
        functools.partial(attend_kernel, nears, blocks),
        in_specs=[SMEM] + [VMEM] * 3,
        out_specs=[VMEM] * (2 if joined else 3),
        out_shape=([jax.ShapeDtypeStruct((2 * n, 256), BF)] if joined else [jax.ShapeDtypeStruct((n, 256), BF)] * 2)
        + [jax.ShapeDtypeStruct((len(nears), 8, n), F32)],
        scratch_shapes=[pltpu.VMEM((3, keys // BLOCK, BLOCK, BLOCK), F32)],
        compiler_params=pltpu.CompilerParams(vmem_limit_bytes=LIMIT),
        cost_estimate=COST,
        name="attend",
    )(table, made, key, row)


def outer_kernel(table, *refs):
    sources, (gain, low_shift, add, mid_ref, unit_ref, *buffers, sems) = refs[:6], refs[6:]
    going = stage(sources, buffers, sems)
    contexts, w_ref, stream_ref = buffers[:4], buffers[4], buffers[5]
    for copy in going:
        copy.wait()
    mid = stream_ref[...] + add[...]
    for near, context in enumerate(contexts):
        mid = mid + dot_t(context[...], w_ref[table[0] ^ near])
    mid_ref[...] = mid
    unit, _ = norm(mid)
    unit_ref[...] = (unit * gain[...] + low_shift[...]).astype(BF)


def outer(table, contexts, weights, stream, gain, low_shift, add):
    n, d = stream.shape
    staged = [*contexts, weights, stream]
    return pl.pallas_call(
        outer_kernel,
        in_specs=[SMEM] + [HBM] * 6 + [VMEM] * 3,
        out_specs=[VMEM, VMEM],
        out_shape=[jax.ShapeDtypeStruct((n, d), F32), jax.ShapeDtypeStruct((n, d), BF)],
        scratch_shapes=buffers_of(staged),
        compiler_params=pltpu.CompilerParams(vmem_limit_bytes=LIMIT),
        cost_estimate=COST,
        name="outer",
    )(table, *staged, gain, low_shift, add)


CHUNK = 256


def feed_kernel(plans, rows, turn_rows, base, table, unit_ref, grad_ref, bias_a, bias_b, *refs):
    if plans is None:
        (w_up, w_down), refs = refs[:2], refs[2:]
        hidden_ref, pre_ref, out_ref, back_ref, turned_ref = refs
    else:
        hidden_ref, pre_ref, out_ref, back_ref, turned_ref, w_up, w_down, sems = refs[-8:]
        pieces = refs[:-8]
        todo = []
        for group in range(2):
            batch = []
            for k, target in enumerate((w_up, w_down)):
                batch += copies(plans[group][k], rows, pieces, target.at[group], 1, table, sems.at[group, k])
            for copy in batch:
                copy.start()
            todo.append(batch)
    width = w_up.shape[2]
    unit, grad = unit_ref[...], grad_ref[...]
    put_turned(table, base, turn_rows, unit.T, turned_ref)
    out, back = 0.0, 0.0
    for group, bias in enumerate((bias_a, bias_b)):
        if plans is not None:
            for copy in todo[group]:
                copy.wait()
        for step in range(width // CHUNK):
            here = slice(step * CHUNK, (step + 1) * CHUNK)
            there = slice(group * width + step * CHUNK, group * width + (step + 1) * CHUNK)
            pre = dot(unit, w_up[group, :, here]) + bias[:, here]
            d_hidden = dot(grad, w_down[group, :, here])
            share = 0.5 + 0.5 * lax.erf(pre * math.sqrt(0.5))
            hidden_ref[:, there] = (pre * share).astype(BF)
            slope = share + pre * (jnp.exp(-0.5 * pre * pre) * (1.0 / math.sqrt(2.0 * math.pi)))
            pre_ref[:, there] = (d_hidden * slope).astype(BF)
        mine = slice(group * width, (group + 1) * width)
        out = out + dot_t(hidden_ref[:, mine], w_down[group])
        back = back + dot_t(pre_ref[:, mine], w_up[group])
    out_ref[...] = out.astype(out_ref.dtype)
    back_ref[...] = back.astype(back_ref.dtype)


def feed(table, unit, grad, biases, weights, rows, turn_rows, base, dtype):
    n, d = unit.shape
    width = biases[0].shape[-1]
    made = [
        jax.ShapeDtypeStruct((n, 2 * width), BF),
        jax.ShapeDtypeStruct((n, 2 * width), BF),
        jax.ShapeDtypeStruct((n, d), dtype),
        jax.ShapeDtypeStruct((n, d), dtype),
        jax.ShapeDtypeStruct((d, n), BF),
    ]
    if isinstance(weights[0], tuple):
        arrays = []
        plans = [[loader(pieces, rows, arrays) for pieces in group] for group in weights]
        specs = [pl.BlockSpec(memory_space=pl.ANY)] * len(arrays)
        made += [jax.ShapeDtypeStruct((2, d, width), BF)] * 2
        scratch = [pltpu.SemaphoreType.DMA((2, 2, len(plans[0][0])))]
    else:
        arrays, plans, specs, scratch = list(weights), None, [VMEM, VMEM], []
    return pl.pallas_call(
        functools.partial(feed_kernel, plans, rows, turn_rows, base),
        in_specs=[SMEM] + [VMEM] * 4 + specs,
        out_specs=[VMEM] * len(made),
        out_shape=made,
        scratch_shapes=scratch,
        compiler_params=pltpu.CompilerParams(vmem_limit_bytes=LIMIT),
        cost_estimate=COST,
        name="feed",
    )(table, unit, grad, *biases, *arrays)


def weights_kernel(block, turned_a, turned_b, grad_a, grad_b, hidden_a, hidden_b, pre_a, pre_b,
                   keep_ref, send_ref, column_ref, keep, send, sems):
    half = keep.shape[0] // 2
    going = []
    for step in range(keep.shape[1] // CHUNK):
        here = slice(step * CHUNK, (step + 1) * CHUNK)
        up = (dot(turned_a[...], pre_a[:, here]) + dot(turned_b[...], pre_b[:, here])).astype(BF)
        down = (dot(grad_a[...], hidden_a[:, here]) + dot(grad_b[...], hidden_b[:, here])).astype(BF)
        for k in range(half // block):
            for target, start in ((keep, 0), (send, half)):
                part = slice(start + k * block, start + (k + 1) * block)
                target[2 * k * block : (2 * k + 1) * block, here] = up[part]
                target[(2 * k + 1) * block : (2 * k + 2) * block, here] = down[part]
        for n, (source, target) in enumerate(((keep, keep_ref), (send, send_ref))):
            copy = pltpu.make_async_copy(source.at[:, here], target.at[:, here], sems.at[step, n])
            copy.start()
            going.append(copy)
        column_ref[:, here] = jnp.sum(pre_a[:, here].astype(F32), axis=0, keepdims=True) + jnp.sum(
            pre_b[:, here].astype(F32), axis=0, keepdims=True
        )
    for copy in going:
        copy.wait()


def weights_grad(group, turned, grads_turned, hiddens, pres, block):
    d, n = turned[0].shape
    width = hiddens[0].shape[1] // 2
    half = pl.BlockSpec((n, width), lambda i: (0, group))
    hbm = pl.BlockSpec(memory_space=pltpu.HBM)
    return pl.pallas_call(
        functools.partial(weights_kernel, block),
        grid=(1,),
        in_specs=[whole((d, n))] * 4 + [half] * 4,
        out_specs=[hbm, hbm, whole((1, width))],
        out_shape=[jax.ShapeDtypeStruct((d, width), BF)] * 2 + [jax.ShapeDtypeStruct((1, width), F32)],
        scratch_shapes=[
            pltpu.VMEM((d, width), BF),
            pltpu.VMEM((d, width), BF),
            pltpu.SemaphoreType.DMA((width // CHUNK, 2)),
        ],
        compiler_params=params("arbitrary"),
        cost_estimate=COST,
        name="weights_grad",
    )(*turned, *grads_turned, *hiddens, *pres)


def middle_kernel(back_a, back_b, mid_ref, grad_ref, gain, full_ref, short_ref, sums_ref):
    unit, scale = norm(mid_ref[...])
    back = back_a[...] + back_b[...].astype(F32)
    grad = grad_ref[...].astype(F32)
    full = grad + norm_back(back * gain[...], unit, scale)
    full_ref[...] = full
    short_ref[...] = full.astype(BF)
    sums_ref[...] = jnp.zeros_like(sums_ref)
    sums_ref[0:1] = jnp.sum(back * unit, axis=0, keepdims=True)
    sums_ref[1:2] = jnp.sum(back, axis=0, keepdims=True)
    sums_ref[2:3] = jnp.sum(full, axis=0, keepdims=True)
    sums_ref[3:4] = jnp.sum(grad, axis=0, keepdims=True)


def middle(back_a, back_b, mid, grad, gain):
    n, d = mid.shape
    return pl.pallas_call(
        middle_kernel,
        in_specs=[VMEM] * 5,
        out_specs=[VMEM] * 3,
        out_shape=[
            jax.ShapeDtypeStruct((n, d), F32),
            jax.ShapeDtypeStruct((n, d), BF),
            jax.ShapeDtypeStruct((8, d), F32),
        ],
        compiler_params=pltpu.CompilerParams(vmem_limit_bytes=LIMIT),
        cost_estimate=COST,
        name="middle",
    )(back_a, back_b, mid, grad, gain)


def last_kernel(mid_ref, out_a, out_b, add, out_ref):
    out_ref[...] = (mid_ref[...] + out_a[...] + out_b[...].astype(F32) + add[...]).astype(BF)


def last_sum(mid, out_a, out_b, add):
    n, d = mid.shape
    rows = pl.BlockSpec((n // 4, d), lambda i: (i, 0))
    return pl.pallas_call(
        last_kernel,
        grid=(4,),
        in_specs=[rows, rows, rows, whole((1, d))],
        out_specs=rows,
        out_shape=jax.ShapeDtypeStruct((n, d), BF),
        compiler_params=params("arbitrary"),
        cost_estimate=COST,
        name="last_sum",
    )(mid, out_a, out_b, add)


def back_kernel(nears, blocks, last_call, table, made_ref, key_ref, row_ref, total_ref, w_ref, short_a, short_b, *refs):
    if last_call:
        before_ref, dq_a, dq_b, out_ref, d_ref, p_ref, dp_ref, sum_ref = refs
        sum_ref[...] = before_ref[...]
    else:
        dq_a, dq_b, sum_ref, d_ref, p_ref, dp_ref = refs
        sum_ref[...] = jnp.zeros_like(sum_ref)
    scale = HEAD ** (-0.5)
    for slot, (near, short, dq_ref) in enumerate(zip(nears, (short_a, short_b), (dq_a, dq_b), strict=True)):
        d_ref[...] = dot(short[...], w_ref[table[0]]).astype(BF)
        for part in range(blocks):
            here = pl.ds(part * BLOCK, BLOCK)
            number, own, first, last = block_places(table, near, part, blocks)
            rows = pl.ds(own, BLOCK)
            q_all = split_heads(made_ref[rows, 0:128], made_ref[rows, 384:512], True)
            d_all = split_heads(d_ref[here, 128:256], d_ref[here, 0:128], False)
            row = row_ref[pl.ds(number, 1), :]
            place = own + lax.broadcasted_iota(jnp.int32, (BLOCK, BLOCK), 1)
            totals = [total_ref[slot, h : h + 1, here] for h in range(3)]

            def weigh(j, inners, q_all=q_all, d_all=d_all, row=row, place=place, totals=totals):
                start = pl.multiple_of(j * BLOCK, BLOCK)
                spot = pl.ds(start, BLOCK)
                bias = pair_bias(key_ref, row, place, start)
                new, add_v = [], []
                for h in range(3):
                    keys = made_ref[spot, 128:256] if h < 2 else made_ref[spot, 512:640]
                    values = made_ref[spot, 256:384] if h < 2 else made_ref[spot, 384:512]
                    p = jnp.exp(dot_t(keys, q_all[h]) + bias - totals[h])
                    d_p = dot_t(values, d_all[h])
                    p_ref[h, j] = p
                    dp_ref[h, j] = d_p
                    new.append(inners[h] + jnp.sum((p * d_p).reshape(BLOCK // 8, 8, BLOCK), axis=0))
                    add_v.append(dot(p.astype(BF), d_all[h]))
                sum_ref[spot, 128:256] += add_v[0] + add_v[1]
                sum_ref[spot, 256:384] += add_v[2]
                return tuple(new)

            inners = lax.fori_loop(first, last, weigh, (jnp.zeros((8, BLOCK), F32),) * 3)
            inners = [jnp.sum(v, axis=0, keepdims=True) for v in inners]

            def turn(j, sums, q_all=q_all, inners=inners):
                spot = pl.ds(pl.multiple_of(j * BLOCK, BLOCK), BLOCK)
                pair_t, third_t = made_ref[spot, 128:256].T, made_ref[spot, 512:640].T
                turned = (pair_t[:HEAD], pair_t[HEAD:], third_t[:HEAD])
                new, add_k = [], []
                for h in range(3):
                    d_s = (p_ref[h, j] * (dp_ref[h, j] - inners[h])).astype(BF)
                    add_k.append(dot(d_s, q_all[h]))
                    new.append(sums[h] + dot(turned[h], d_s))
                sum_ref[spot, 0:128] += add_k[0] + add_k[1]
                sum_ref[spot, 384:512] += add_k[2]
                return tuple(new)

            sums = lax.fori_loop(first, last, turn, (jnp.zeros((HEAD, BLOCK), F32),) * 3)
            two = jnp.concatenate([sums[0], sums[1]], axis=0).T.astype(BF) * jnp.asarray(scale, BF)
            one = jnp.concatenate([sums[2], jnp.zeros_like(sums[2])], axis=0).T.astype(BF) * jnp.asarray(scale, BF)
            dq_ref[here, :] = two
            sum_ref[rows, 256:384] += one.astype(F32)
    if last_call:
        out_ref[...] = sum_ref[...].astype(BF)


def attend_back(nears, table, made, key, row, total, w, shorts, before):
    keys = made.shape[0]
    n = keys // 4
    last_call = before is not None
    operands = [table, made, key, row, total, w, *shorts] + ([before] if last_call else [])
    scores = pltpu.VMEM((3, keys // BLOCK, BLOCK, BLOCK), F32)
    scratch = [pltpu.VMEM((n, 256), BF), scores, scores]
    if last_call:
        scratch.append(pltpu.VMEM((keys, 512), F32))
    return pl.pallas_call(
        functools.partial(back_kernel, nears, n // BLOCK, last_call),
        in_specs=[SMEM] + [VMEM] * (len(operands) - 1),
        out_specs=[VMEM] * 3,
        out_shape=[
            jax.ShapeDtypeStruct((n, 128), BF),
            jax.ShapeDtypeStruct((n, 128), BF),
            jax.ShapeDtypeStruct((keys, 512), BF if last_call else F32),
        ],
        scratch_shapes=scratch,
        compiler_params=pltpu.CompilerParams(vmem_limit_bytes=LIMIT),
        cost_estimate=COST,
        name="attend_back",
    )(*operands)


def grads_kernel(rows, base, table, dkv_ref, dq_a, dq_b, dq_c, dq_d, *refs):
    sources, refs = refs[:9], refs[9:]
    outs, (keep_ref, send_ref, column_ref, sum_ref), (*buffers, sems) = refs[:4], refs[4:8], refs[8:]
    going = stage(sources, buffers, sems)
    w_ref, turned_ref, shorts, contexts = buffers[0], buffers[1], buffers[2:6], buffers[6:9]
    dqs = (dq_a, dq_b, dq_c, dq_d)
    n = dq_a.shape[0]
    half = keep_ref.shape[0]
    contexts = [contexts[0], contexts[1], contexts[2].at[:n], contexts[2].at[n:]]
    going[0].wait()
    for near in (3, 2, 1, 0):
        here = pl.ds(pl.multiple_of((table[0] ^ near) * n, n), n)
        outs[near][...] = (dot_t(dkv_ref[here, :], w_ref[:, 128:640]) + dot_t(dqs[near][...], w_ref[:, 0:128])).astype(BF)
    for copy in going[1:]:
        copy.wait()
    dkv = dkv_ref[...]
    sum_ref[:, 128:640] = dot(turned_ref[...], dkv)
    column_ref[:, 128:640] = jnp.sum(dkv.astype(F32), axis=0, keepdims=True)
    made, column, out = 0.0, 0.0, 0.0
    for near in range(4):
        here = pl.ds(pl.multiple_of((table[0] ^ near) * n, n), n)
        dq = dqs[near][...]
        made = made + dot(turned_ref[:, here], dq)
        column = column + jnp.sum(dq.astype(F32), axis=0, keepdims=True)
        out = out + t_dot(shorts[near][...], contexts[near][...])
    sum_ref[:, 0:128] = made
    column_ref[:, 0:128] = column
    for k in range(out.shape[0] // rows):
        here = pl.ds(pl.multiple_of(table[base + k], rows), rows)
        part = out[k * rows : (k + 1) * rows]
        sum_ref[here, 512:640] += part[:, :128]
        sum_ref[here, 640:768] = part[:, 128:]
    keep_ref[...] = sum_ref[:half, :].astype(BF)
    send_ref[...] = sum_ref[half:, :].astype(BF)


def grads(table, w, turned, dqs, dkv, shorts, contexts, rows, base):
    n, d = dqs[0].shape[0], turned.shape[0]
    staged = [w, turned, *shorts, *contexts]
    return pl.pallas_call(
        functools.partial(grads_kernel, rows, base),
        in_specs=[SMEM] + [VMEM] * 5 + [HBM] * 9,
        out_specs=[VMEM] * 7,
        out_shape=[jax.ShapeDtypeStruct((n, d), BF)] * 4
        + [jax.ShapeDtypeStruct((d // 2, 768), BF)] * 2
        + [jax.ShapeDtypeStruct((1, 640), F32)],
        scratch_shapes=[pltpu.VMEM((d, 768), F32)] + buffers_of(staged),
        compiler_params=pltpu.CompilerParams(vmem_limit_bytes=40 << 20),
        cost_estimate=COST,
        name="grads",
    )(table, dkv, *dqs, *staged)


def final_kernel(one_ref, core_ref, two_ref, stream_hbm, full_hbm, gain, early_ref, col_a, col_b, col_one,
                 grad_ref, sums_ref, stream_ref, full_ref, sems):
    going = stage((stream_hbm, full_hbm), (stream_ref, full_ref), sems)
    back = one_ref[...].astype(F32) + core_ref[...].astype(F32) + two_ref[...].astype(F32)
    for copy in going:
        copy.wait()
    unit, scale = norm(stream_ref[...])
    grad = full_ref[...] + norm_back(back * gain[...], unit, scale)
    grad_ref[...] = grad
    sums_ref[0:1] = jnp.sum(back * unit, axis=0, keepdims=True)
    sums_ref[1:2] = jnp.sum(back, axis=0, keepdims=True)
    sums_ref[2:3] = jnp.sum(grad, axis=0, keepdims=True)
    sums_ref[3:7] = early_ref[0:4]
    sums_ref[7:8] = col_b[...]
    sums_ref[8:9] = col_a[...]
    sums_ref[9:16] = jnp.zeros_like(sums_ref[9:16])
    sums_ref[9:10, : col_one.shape[1]] = col_one[...]


def small_call(kernel, shapes, limit=LIMIT):
    def call(*operands):
        return pl.pallas_call(
            kernel,
            in_specs=[VMEM] * len(operands),
            out_specs=[VMEM] * len(shapes),
            out_shape=[jax.ShapeDtypeStruct(shape, F32) for shape in shapes],
            compiler_params=pltpu.CompilerParams(vmem_limit_bytes=limit),
            cost_estimate=COST,
            name=getattr(kernel, "__name__", "finish"),
        )(*operands)

    return call


def core_sums(own, there, out):
    out[0:7] = own[0:7] + there[0:7]
    out[7:8] = own[8:9] + there[7:8]
    out[8:9] = own[9:10]
    out[9:16] = jnp.zeros_like(own[9:16])


def row_sums(own, there, seat, spread, out):
    dp = seat.shape[0]
    both = own[0:7] + there[0:7]
    out[0:2] = both[0:2]
    out[2:6] = both[3:7]
    out[6:8] = own[7:9]
    out[8 : 8 + dp] = seat[...] * both[2:3]
    out[8 + dp : 8 + dp + spread.shape[0]] = spread[...]


def finish_kernel(dp, features, columns, count, *refs):
    parts, (pick, gain_ref, bias_ref, query_ref, value_ref, up_ref, time_ref) = refs[:count], refs[count:]
    total = parts[0][...]
    for part in parts[1:]:
        total = total + part[...]
    by_sequence = total[8 : 8 + dp]
    gain_ref[0:1] = total[0:1]
    gain_ref[1:2] = total[2:3]
    bias_ref[0:1] = total[1:2]
    bias_ref[1:4] = total[3:6]
    bias_ref[4:5] = jnp.sum(by_sequence, axis=0, keepdims=True)
    up_ref[...] = total[6:7]
    query_ref[...] = jnp.concatenate([total[7:8, 0:128], total[7:8, 384:448]], axis=1)
    value_ref[...] = jnp.concatenate([total[7:8, 256:384], total[7:8, 448:512]], axis=1)
    wide = total.shape[1] // features
    rows = [total[8 + dp + k // wide : 9 + dp + k // wide, k % wide * features : (k % wide + 1) * features] for k in range(dp)]
    share = jnp.dot(by_sequence, pick[...], precision=highest, preferred_element_type=F32)
    time_ref[...] = lax.dot_general(
        jnp.concatenate(rows, axis=0), share, (((0,), (0,)), ((), ())), precision=highest, preferred_element_type=F32
    )


def final(one, core, two, stream, full, gain, early, cols, col_one):
    n, d = stream.shape
    return pl.pallas_call(
        final_kernel,
        in_specs=[VMEM] * 3 + [HBM] * 2 + [VMEM] * 5,
        out_specs=[VMEM] * 2,
        out_shape=[jax.ShapeDtypeStruct((n, d), F32), jax.ShapeDtypeStruct((16, d), F32)],
        scratch_shapes=buffers_of((stream, full)),
        compiler_params=pltpu.CompilerParams(vmem_limit_bytes=LIMIT),
        cost_estimate=COST,
        name="final",
    )(one, core, two, stream, full, gain, early, *cols, col_one)


def add_kernel(*refs):
    total = refs[0][...].astype(F32)
    for ref in refs[1:-1]:
        total = total + ref[...].astype(F32)
    refs[-1][...] = total.astype(refs[-1].dtype)


def low_sum(*terms, rows=None, dtype=BF):
    terms = [v if isinstance(v, tuple) else (v, 0) for v in terms]
    rows = rows or min(v.shape[0] for v, _ in terms)
    block = rows // (4 if rows % 64 == 0 else 1)
    width = terms[0][0].shape[1]
    return pl.pallas_call(
        add_kernel,
        grid=(rows // block,),
        in_specs=[
            pl.BlockSpec((block, width), functools.partial(lambda first, i: (i + first, 0), start // block))
            for _, start in terms
        ],
        out_specs=pl.BlockSpec((block, width), lambda i: (i, 0)),
        out_shape=jax.ShapeDtypeStruct((rows, width), dtype),
        compiler_params=params("arbitrary"),
        cost_estimate=COST,
        name="low_sum",
    )(*[v for v, _ in terms])


def stack_kernel(*refs):
    for k, ref in enumerate(refs[:-1]):
        refs[-1][k] = ref[...]


def stack(values):
    return pl.pallas_call(
        stack_kernel,
        in_specs=[VMEM] * len(values),
        out_specs=VMEM,
        out_shape=jax.ShapeDtypeStruct((len(values),) + values[0].shape, values[0].dtype),
        compiler_params=pltpu.CompilerParams(vmem_limit_bytes=LIMIT),
        cost_estimate=COST,
        name="stack",
    )(*values)


def tie(values, after):
    return lax.optimization_barrier((values, after))[0]


def line_sums(terms, size, rows):
    own = low_sum(*terms, rows=rows, dtype=F32)
    return own, [low_sum(*[(v, by * rows) for v in terms], rows=rows) for by in range(1, size)]


def along_line(sent, size):
    return [shift(v, "d1", size, by + 1) for by, v in enumerate(sent)]


def scatter_dp(value):
    return lax.psum_scatter(value, ("d1", "d0"), scatter_dimension=0, tiled=True).astype(F32)


def shards(
    inputs,
    segment_ids,
    keep_mask,
    timestep,
    w_qkv,
    b_query,
    b_value,
    w_out,
    w_up,
    b_up,
    w_down,
    time_weight,
    gains,
    row_biases,
    d_out,
):
    size = lax.axis_size("d1")
    long = size > 4
    z, x = lax.axis_index("d1"), lax.axis_index("d0")
    own = lax.axis_index("t1") * 2 + lax.axis_index("t0")
    n, d = inputs.shape
    dp = 2 * size
    place = z * 2 + x
    features = time_weight.shape[0]
    columns = time_weight.shape[1]

    pack_one = jnp.concatenate([pack_columns(w_qkv[0], w_qkv[1], w_qkv[2]), time_weight.T], axis=1)
    rows = pack_one.shape[0]
    if long:
        half = lax.all_gather(pack_one, ("d1", "d0"), axis=0, tiled=True)
        pieces_one = [(half, None, 0)]
    else:
        line = [pack_one] + [shift(pack_one, "d1", size, by) for by in range(1, size)]
        x_core = swap(inputs, "t0")
        half = stack(tie(line, x_core))
        other_half = swap(half, "d0")
        pieces_one = [(half, s, s) for s in range(size)] + [(other_half, s, size + s) for s in range(size)]
    x_far = swap(inputs, "t1")
    x_far = x_far if long else tie(x_far, half)
    x_near = [inputs, swap(inputs, "t0") if long else x_core, x_far, swap(x_far, "t0")]
    time_rows = sinusoid(timestep, features).astype(BF)
    times = jnp.pad(time_rows, ((0, 7), (0, 0)))
    seat = (jnp.arange(dp) == place).astype(F32)[:, None]
    spread = (seat * time_rows.astype(F32)).reshape(1, -1)
    spread = jnp.pad(spread, ((0, 0), (0, -spread.shape[1] % d))).reshape(-1, d)
    outer_all = lax.all_gather(pack_outer(w_out.T), ("t1", "t0", "d1", "d0"), axis=0, tiled=True).reshape(4, d, 256)
    bias_one = pack_columns(b_query, jnp.zeros_like(b_query), b_value)[None, :]

    blocks = 4 * n // BLOCK
    ids = segment_ids.reshape(blocks, BLOCK)
    first = jnp.sum(segment_ids[None, :] < ids[:, :1], axis=1, dtype=jnp.int32)
    last = jnp.sum(segment_ids[None, :] <= ids[:, -1:], axis=1, dtype=jnp.int32)
    span = jnp.stack([first // BLOCK, (last + BLOCK - 1) // BLOCK], axis=1).reshape(-1)
    slots = [(lax.rem(z - s + size, size) * 2 + (x ^ a)) * rows for a in range(2) for s in range(size)]
    places = [((k % 2 ^ x) * size + lax.rem(k // 2 - z + size, size)) * rows for k in range(dp)]
    if long:
        slots, places, turn_rows = [jnp.zeros_like(own)], [jnp.zeros_like(own)], d
    else:
        turn_rows = rows
    base = 1 + len(slots)
    table_one = jnp.stack([own, *slots, *places]).astype(jnp.int32)
    table_two = jnp.concatenate([jnp.stack([own]), span]).astype(jnp.int32)
    key = jnp.where(keep_mask > 0, segment_ids, -1)[:, None]
    own_keep = lax.dynamic_slice_in_dim(keep_mask, own * n, n, 0)[:, None]
    scale = jnp.where(
        (jnp.arange(640) < 128) | ((jnp.arange(640) >= 384) & (jnp.arange(640) < 448)), HEAD ** (-0.5), 1.0
    ).astype(F32)[None, :]

    far_keep = lax.dynamic_slice_in_dim(keep_mask, (own ^ 2) * n, n, 0)[:, None]
    d_far = swap(tie(d_out, x_far), "t1")
    grad_two, grad_turned = cotangent(table_one, d_out, own_keep, turn_rows, base)

    if long:
        gathered = lax.all_gather(jnp.stack([w_up, w_down.T]), ("d1", "d0"), axis=1, tiled=True)
        other = swap(gathered, "t0")
        feed_weights = [tuple([(v, k, 0)] for k in range(2)) for v in (gathered, other)]
        rows_two = d
    else:
        def along(pack):
            return [pack] + [shift(pack, "d1", size, by) for by in range(1, size)]

        line_up = along(tie(w_up, half))
        line_down = along(tie(w_down.T, line_up))
        up_own = tie(stack(line_up), other_half)
        up_two = swap(up_own, "d0")
        x_near = tie(x_near, (up_own, grad_two))
    made, turned_one, stream_in, w_one = project(
        x_near, times, row_biases[4:5], gains[0:1], row_biases[0:1], bias_one, scale, pieces_one, d if long else rows,
        table_one, turn_rows, base,
    )
    made_near = made_far = made
    if not long:
        down_own = stack(tie(line_down, made))
        down_two = swap(down_own, "d0")
        made_far = tie(made, down_own)
    context_far, total_far = attend((2, 3), table_two, made_far, key, ids, True)
    context_over = swap(context_far, "t1")
    if not long:
        made_near = tie(made, (context_far, up_two, d_far))
    context_a, context_b, total_near = attend((0, 1), table_two, made_near, key, ids, False)
    grad_far, grad_turned_far = cotangent(table_one, tie(d_far, context_a), far_keep, turn_rows, base)
    context_over = tie(context_over, grad_far)
    contexts = [context_a, swap(context_b, "t0"), context_over[:n], swap(context_over[n:], "t0")]
    if not long:
        def pieces_of(near, other):
            return [(v, s, a * size + s) for a, v in enumerate((near, other)) for s in range(size)]

        feed_weights = [
            (pieces_of(up_own, up_two), pieces_of(down_own, down_two)),
            (pieces_of(*to_core((up_own, up_two))), pieces_of(*to_core((down_own, down_two)))),
        ]
        rows_two = rows
    stream_mid, unit_two = outer(
        table_one, contexts, outer_all, stream_in, gains[1:2], row_biases[1:2], row_biases[2:3]
    )

    biases = [b_up[None], swap(b_up[None], "t0")]
    unit_far = swap(unit_two, "t1")
    hidden, pre, out, back, turned_two, *feed_arrays = feed(
        table_one, unit_two, grad_two, biases, feed_weights, rows_two, turn_rows, base, F32
    )
    hidden_far, pre_far, out_far, back_far, turned_far = feed(
        table_one, tie(unit_far, back), grad_far, biases, feed_arrays, rows_two, turn_rows, base, BF
    )
    back_over = swap(back_far, "t1")
    block = d // 2 if long else rows
    parts = ((turned_two, turned_far), (grad_turned, grad_turned_far), (hidden, hidden_far), (pre, pre_far))
    keep_b, send_b, column_b = weights_grad(1, *parts, block)
    keep_b, send_b = to_core((keep_b, send_b))
    keep_a, send_a, column_a = weights_grad(0, *parts, block)
    full, short, sums_two = middle(back, tie(back_over, keep_a), stream_mid, grad_two, gains[1:2])
    short_core, short_over = swap(short, "t0"), swap(short, "t1")
    sent = low_sum(send_a, tie(send_b, short))
    over = sent if long else swap(sent, "d0")
    shorts = tie([short, short_core], sent)
    dq_a, dq_b, sum_near = attend_back((0, 1), table_two, made, key, ids, total_near, outer_all, shorts, None)
    short_over = tie(short_over, sum_near)
    shorts = [short_over, swap(short_over, "t0")]
    short_near = [short, short_core] + shorts
    out_over = swap(tie(out_far, short_over), "t1")
    if long:
        kept = low_sum(keep_a, keep_b)
        up_share = scatter_dp(jnp.concatenate([kept[: d // 2], sent[: d // 2]]))
        down_share = scatter_dp(jnp.concatenate([kept[d // 2 :], sent[d // 2 :]]))
    dq_c, dq_d, dkv = attend_back((2, 3), table_two, made, key, ids, total_far, outer_all, shorts, sum_near)
    output = last_sum(stream_mid, out, tie(out_over, dkv), row_biases[3:4])
    if not long:
        sent_terms = (keep_a, keep_b, tie(over, dkv))
        own_part, going = line_sums(sent_terms, size, 2 * rows)
        dkv = tie(dkv, (own_part, going))
    dqs = [dq_a, dq_b, dq_c, dq_d]
    back_a, back_b, back_c, back_d, grad_keep, grad_send, column_one = grads(
        table_one, w_one, turned_one, dqs, dkv, short_near, [context_a, context_b, context_far], turn_rows, base
    )
    back_d, back_b = swap(back_d, "t0"), swap(back_b, "t0")
    back_far = low_sum(back_c, tie(back_d, back_b))
    other = swap(back_far, "t1")
    if long:
        one_share = scatter_dp(jnp.concatenate([grad_keep, grad_send]))
    else:
        grad_over = swap(grad_send, "d0")
        shares = along_line(tie(going, back_far), size)
        other, shares, grad_over = lax.optimization_barrier((other, shares, grad_over))
    grad_input, small = final(
        back_a, back_b, other, stream_in, full, gains[0:1], sums_two, (column_a, column_b), column_one
    )

    if not long:
        one_own, one_sent = line_sums((grad_keep, tie(grad_over, small)), size, rows)
        one_shares = along_line(one_sent, size)

    (small,) = small_call(core_sums, [(16, d)])(small, swap(small, "t0"))
    height = 8 + dp + spread.shape[0]
    (small,) = small_call(row_sums, [(height, d)])(small, swap(small, "t1"), seat, spread)
    small = small + swap(small, "d0")
    parts = [lax.psum(small, "d1")] if long else [small] + [shift(small, "d1", size, by) for by in range(1, size)]
    pick = (jnp.arange(d)[:, None] == place * columns + jnp.arange(columns)[None, :]).astype(F32)
    width = b_query.shape[0]
    gain_total, bias_total, column_query, column_value, up_bias, grad_time = small_call(
        functools.partial(finish_kernel, dp, features, columns, len(parts)),
        [(2, d), (5, d), (1, width), (1, width), (1, d), (features, columns)],
    )(*parts, pick)
    if not long:
        own_share = low_sum(own_part, *tie(shares, small), dtype=F32)
        up_share, down_share = own_share[:rows], own_share[rows:]
        one_share = low_sum(one_own, *one_shares, dtype=F32)
    d_query, d_key, d_value, d_outer = unpack_columns(one_share)
    return (
        output,
        grad_input,
        jnp.stack([d_query, d_key, d_value]),
        column_query[0],
        column_value[0],
        d_outer.T,
        up_share,
        up_bias[0],
        down_share.T,
        grad_time,
        gain_total,
        bias_total,
    )


def solution(mesh):
    dp, tensor = mesh.shape["dp"], mesh.shape["tensor"]
    fine = Mesh(mesh.devices.reshape(dp // 2, 2, tensor // 2, 2), ("d1", "d0", "t1", "t0"))
    rows, cols = ("d1", "d0"), ("t1", "t0")
    every = rows + cols
    in_specs = (
        P(every, None),
        P(rows),
        P(rows),
        P(rows),
        P(None, rows, cols),
        P(cols),
        P(cols),
        P(cols, rows),
        P(rows, cols),
        P(cols),
        P(cols, rows),
        P(None, rows),
        P(),
        P(),
        P(every, None),
    )
    out_specs = (
        P(every, None),
        P(every, None),
        P(None, rows, cols),
        P(cols),
        P(cols),
        P(cols, rows),
        P(rows, cols),
        P(cols),
        P(cols, rows),
        P(None, rows),
        P(),
        P(),
    )
    return jax.shard_map(shards, mesh=fine, in_specs=in_specs, out_specs=out_specs, check_vma=False)
```

```python
import functools
import math

import jax
import jax.numpy as jnp
from jax import lax
from jax.experimental import pallas as pl
from jax.experimental.pallas import tpu as pltpu
from jax.sharding import Mesh
from jax.sharding import PartitionSpec as P

HEAD = 64
SEQ_LEN = 2048
BLOCK = 256
F32 = jnp.float32
BF = jnp.bfloat16

epsilon = 1e-05
masked = -1e30
highest = lax.Precision.HIGHEST

LIMIT = 32 << 20
COST = pl.CostEstimate(flops=10**5, bytes_accessed=10**5, transcendentals=0)


def dot(left, right):
    return jnp.dot(left, right, preferred_element_type=F32)


def dot_t(left, right):
    return lax.dot_general(left, right, (((1,), (1,)), ((), ())), preferred_element_type=F32)


def t_dot(left, right):
    return lax.dot_general(left, right, (((0,), (0,)), ((), ())), preferred_element_type=F32)


def params(*semantics, limit=LIMIT):
    return pltpu.CompilerParams(dimension_semantics=semantics, vmem_limit_bytes=limit)


def whole(shape):
    rank = len(shape)
    return pl.BlockSpec(shape, lambda *_: (0,) * rank)


def stage(sources, buffers, sems):
    going = [pltpu.make_async_copy(s, b, sems.at[k]) for k, (s, b) in enumerate(zip(sources, buffers, strict=True))]
    for copy in going:
        copy.start()
    return going


def buffers_of(values):
    return [pltpu.VMEM(v.shape, v.dtype) for v in values] + [pltpu.SemaphoreType.DMA((len(values),))]


def sinusoid(timesteps, features):
    half_width = features // 2
    frequency = jnp.exp(-math.log(10000.0) * jnp.arange(half_width, dtype=F32) / half_width)
    angles = timesteps.astype(F32)[:, None] * frequency[None, :]
    return jnp.concatenate([jnp.cos(angles), jnp.sin(angles)], axis=1)


def swap(value, axis):
    return lax.ppermute(value, axis, [(0, 1), (1, 0)])


def shift(value, axis, size, by):
    return lax.ppermute(value, axis, [(i, (i + by) % size) for i in range(size)])


def gather_near(value):
    far = swap(value, "t1")
    return [value, swap(value, "t0"), far, swap(far, "t0")]


def to_core(values):
    return [swap(v, "t0") for v in values]


def loader(pieces, rows, arrays):
    plan = []
    for value, lead, slot in pieces:
        for n, known in enumerate(arrays):
            if known is value:
                break
        else:
            n = len(arrays)
            arrays.append(value)
        plan.append((n, lead, slot))
    return plan


def copies(plan, rows, refs, target, base, table, sems):
    out = []
    for k, (n, lead, slot) in enumerate(plan):
        source = refs[n] if lead is None else refs[n].at[lead[0], pl.ds(lead[1] * rows, rows), :]
        if table is None:
            start = slot * rows
        else:
            start = pl.multiple_of(table[base + slot], rows)
        out.append(pltpu.make_async_copy(source, target.at[pl.ds(start, rows), :], sems.at[k]))
    return out


def norm(values):
    average = jnp.mean(values, axis=-1, keepdims=True)
    centered = values - average
    variance = jnp.mean(centered * centered, axis=-1, keepdims=True)
    scale = lax.rsqrt(variance + epsilon)
    return centered * scale, scale


def norm_back(gradient, unit, scale):
    one = jnp.mean(gradient, axis=-1, keepdims=True)
    two = jnp.mean(gradient * unit, axis=-1, keepdims=True)
    return scale * (gradient - one - unit * two)


def pack_columns(query, key, value):
    zeros = jnp.zeros_like(key[..., 128:])
    return jnp.concatenate(
        [query[..., :128], key[..., :128], value[..., :128], query[..., 128:], value[..., 128:], key[..., 128:], zeros],
        axis=-1,
    )


def pack_outer(out):
    return jnp.concatenate([jnp.zeros_like(out[..., 128:]), out[..., 128:], out[..., :128]], axis=-1)


def unpack_columns(pack):
    query = jnp.concatenate([pack[..., 0:128], pack[..., 384:448]], axis=-1)
    key = jnp.concatenate([pack[..., 128:256], pack[..., 512:576]], axis=-1)
    value = jnp.concatenate([pack[..., 256:384], pack[..., 448:512]], axis=-1)
    out = jnp.concatenate([pack[..., 640:768], pack[..., 576:640]], axis=-1)
    return query, key, value, out


VMEM = pl.BlockSpec(memory_space=pltpu.VMEM)
SMEM = pl.BlockSpec(memory_space=pltpu.SMEM)
HBM = pl.BlockSpec(memory_space=pltpu.HBM)


def put_turned(table, base, rows, value, target):
    for k in range(value.shape[0] // rows):
        here = pl.ds(pl.multiple_of(table[base + k], rows), rows)
        target[here, :] = value[k * rows : (k + 1) * rows]


def cotangent_kernel(rows, base, table, d_ref, keep_ref, grad_ref, turned_ref):
    value = d_ref[0]
    grad = jnp.where(keep_ref[...] > 0, value, jnp.zeros_like(value))
    grad_ref[...] = grad
    put_turned(table, base, rows, grad.T, turned_ref)


def cotangent(table, d_out, keep, rows, base):
    _, n, d = d_out.shape
    return pl.pallas_call(
        functools.partial(cotangent_kernel, rows, base),
        in_specs=[SMEM, VMEM, VMEM],
        out_specs=[VMEM, VMEM],
        out_shape=[jax.ShapeDtypeStruct((n, d), BF), jax.ShapeDtypeStruct((d, n), BF)],
        compiler_params=pltpu.CompilerParams(vmem_limit_bytes=LIMIT),
        cost_estimate=COST,
        name="cotangent",
    )(table, d_out, keep)


def project_kernel(plan, rows, turn_rows, base, table, x_a, x_b, x_c, x_d, x_e, x_f, times, add, gain, low_shift, bias, scale, *refs):
    count = len({n for n, _, _ in plan})
    pieces, (made_ref, turned_ref, stream_ref, w_out_ref, outer_ref, w_ref, sems, x_all, stage_sems) = refs[:count], refs[count:]
    n = x_a.shape[0]
    todo = copies(plan, rows, pieces, w_ref, 1, table, sems)
    for copy in todo:
        copy.start()
    part = n // 2
    targets = [x_all.at[0], x_all.at[1], x_all.at[2, :part], x_all.at[2, part:], x_all.at[3, :part], x_all.at[3, part:]]
    inputs = stage((x_a, x_b, x_c, x_d, x_e, x_f), targets, stage_sems)
    for copy in todo + inputs:
        copy.wait()
    w_out_ref[...] = w_ref[:, 0:640]
    outer_ref[...] = w_ref[:, 768:1024]
    embed = dot_t(times[...], w_ref[:, 640:768])[0:1] + add[...]

    @pl.loop(0, 4)
    def _(near):
        stream = x_all[near].astype(F32) + embed

        @pl.when(near == 0)
        def _():
            stream_ref[...] = stream

        unit, _ = norm(stream)
        low = (unit * gain[...] + low_shift[...]).astype(BF)
        here = pl.ds(pl.multiple_of((table[0] ^ near) * n, n), n)
        made_ref[here, :] = ((dot(low, w_ref[:, :640]) + bias[...]) * scale[...]).astype(BF)
        put_turned(table, base, turn_rows, low.T, turned_ref.at[:, here])


def project(x_near, times, add, gain, low_shift, bias, scale, pieces, rows, table, turn_rows, base):
    n, d = x_near[0].shape
    arrays = []
    plan = loader(pieces, rows, arrays)
    return pl.pallas_call(
        functools.partial(project_kernel, plan, rows, turn_rows, base),
        in_specs=[SMEM] + [HBM] * 6 + [VMEM] * 6 + [pl.BlockSpec(memory_space=pl.ANY)] * len(arrays),
        out_specs=[VMEM] * 5,
        out_shape=[
            jax.ShapeDtypeStruct((4 * n, 640), BF),
            jax.ShapeDtypeStruct((d, 4 * n), BF),
            jax.ShapeDtypeStruct((n, d), F32),
            jax.ShapeDtypeStruct((d, 640), BF),
            jax.ShapeDtypeStruct((d, 256), BF),
        ],
        scratch_shapes=[
            pltpu.VMEM((d, 1024), BF),
            pltpu.SemaphoreType.DMA((len(plan),)), pltpu.VMEM((4, n, d), x_near[0].dtype), pltpu.SemaphoreType.DMA((6,))
        ],
        compiler_params=pltpu.CompilerParams(vmem_limit_bytes=60 << 20),
        cost_estimate=COST,
        name="project",
    )(table, *x_near, times, add, gain, low_shift, bias, scale, *arrays)


def low_half(shape):
    return lax.broadcasted_iota(jnp.int32, shape, 1) < HEAD


def pair_bias(key_ref, row, place, start):
    spot = start + lax.broadcasted_iota(jnp.int32, (BLOCK, BLOCK), 0)
    allowed = (key_ref[pl.ds(start, BLOCK), :] == row) | (spot == place)
    return jnp.where(allowed, 0.0, masked)


def block_places(table, first_near, step, blocks):
    number = (table[0] ^ (first_near + step // blocks)) * blocks + step % blocks
    return number, pl.multiple_of(number * BLOCK, BLOCK), table[1 + 2 * number], table[2 + 2 * number]


def split_heads(pair, third, third_low):
    half = low_half(pair.shape)
    zero = jnp.zeros_like(pair)
    last = jnp.where(half, third, zero) if third_low else jnp.where(half, zero, third)
    return jnp.where(half, pair, zero), jnp.where(half, zero, pair), last


def attend_kernel(first_near, blocks, table, made_ref, key_ref, row_ref, context_ref, total_ref, score_ref):
    @pl.loop(0, 2 * blocks)
    def _(step):
        here = pl.ds(pl.multiple_of(step * BLOCK, BLOCK), BLOCK)
        number, own, first, last = block_places(table, first_near, step, blocks)
        rows = pl.ds(own, BLOCK)
        q_all = split_heads(made_ref[rows, 0:128], made_ref[rows, 384:512], True)
        row = row_ref[pl.ds(number, 1), :]
        place = own + lax.broadcasted_iota(jnp.int32, (BLOCK, BLOCK), 1)

        def score(j, tops):
            start = pl.multiple_of(j * BLOCK, BLOCK)
            spot = pl.ds(start, BLOCK)
            bias = pair_bias(key_ref, row, place, start)
            out = []
            for h in range(3):
                keys = made_ref[spot, 128:256] if h < 2 else made_ref[spot, 512:640]
                s = dot_t(keys, q_all[h]) + bias
                score_ref[h, j] = s
                out.append(jnp.maximum(tops[h], jnp.max(s.reshape(BLOCK // 8, 8, BLOCK), axis=0)))
            return tuple(out)

        begin = jnp.full((8, BLOCK), masked, F32)
        tops = lax.fori_loop(first, last, score, (begin,) * 3)
        tops = [jnp.max(t, axis=0, keepdims=True) for t in tops]

        def weigh(j, carry):
            spot = pl.ds(pl.multiple_of(j * BLOCK, BLOCK), BLOCK)
            pair_t = made_ref[spot, 256:384].T
            third_t = made_ref[spot, 384:512].T
            values = (pair_t[:HEAD], pair_t[HEAD:], third_t[HEAD:])
            sums, totals = carry
            new_sums, new_totals = [], []
            for h in range(3):
                p = jnp.exp(score_ref[h, j] - tops[h])
                new_totals.append(totals[h] + jnp.sum(p.reshape(BLOCK // 8, 8, BLOCK), axis=0))
                new_sums.append(sums[h] + dot(values[h], p.astype(BF)))
            return tuple(new_sums), tuple(new_totals)

        zeros = (jnp.zeros((HEAD, BLOCK), F32),) * 3
        sums, totals = lax.fori_loop(first, last, weigh, (zeros, (jnp.zeros((8, BLOCK), F32),) * 3))
        done = []
        for h in range(3):
            total = jnp.sum(totals[h], axis=0, keepdims=True)
            done.append(sums[h] / total)
            total_ref[h : h + 1, here] = tops[h] + jnp.log(total)
        context_ref[here, 0:128] = jnp.concatenate([jnp.zeros_like(done[2]), done[2]], axis=0).T.astype(BF)
        context_ref[here, 128:256] = jnp.concatenate([done[0], done[1]], axis=0).T.astype(BF)


def attend(first_near, table, made, key, row):
    keys = made.shape[0]
    n = keys // 4
    blocks = n // BLOCK
    return pl.pallas_call(
        functools.partial(attend_kernel, first_near, blocks),
        in_specs=[SMEM] + [VMEM] * 3,
        out_specs=[VMEM] * 2,
        out_shape=[jax.ShapeDtypeStruct((2 * n, 256), BF), jax.ShapeDtypeStruct((8, 2 * n), F32)],
        scratch_shapes=[pltpu.VMEM((3, keys // BLOCK, BLOCK, BLOCK), F32)],
        compiler_params=pltpu.CompilerParams(vmem_limit_bytes=LIMIT),
        cost_estimate=COST,
        name="attend",
    )(table, made, key, row)


def outer_kernel(table, *refs):
    sources, (gain, low_shift, add, mid_ref, unit_ref, *buffers, sems) = refs[:9], refs[9:]
    going = stage(sources, buffers, sems)
    contexts, stream_ref = buffers[:4], buffers[8]
    for copy in going:
        copy.wait()
    mid = stream_ref[...] + add[...]
    n = stream_ref.shape[0]
    contexts = [context.at[k % 2 * n : (k % 2 + 1) * n] for k, context in enumerate(contexts)]
    for near, context in enumerate(contexts):
        mid = mid + dot_t(context[...], buffers[4 + near][...])
    mid_ref[...] = mid
    unit, _ = norm(mid)
    unit_ref[...] = (unit * gain[...] + low_shift[...]).astype(BF)


def outer(table, contexts, weights, stream, gain, low_shift, add):
    n, d = stream.shape
    staged = [*contexts, *weights, stream]
    return pl.pallas_call(
        outer_kernel,
        in_specs=[SMEM] + [HBM] * 9 + [VMEM] * 3,
        out_specs=[VMEM, VMEM],
        out_shape=[jax.ShapeDtypeStruct((n, d), F32), jax.ShapeDtypeStruct((n, d), BF)],
        scratch_shapes=buffers_of(staged),
        compiler_params=pltpu.CompilerParams(vmem_limit_bytes=60 << 20),
        cost_estimate=COST,
        name="outer",
    )(table, *staged, gain, low_shift, add)


CHUNK = 256


def feed_kernel(plans, rows, turn_rows, base, first_slot, table, unit_ref, grad_ref, bias, *refs):
    if plans is None:
        (w_up, w_down), refs = refs[:2], refs[2:]
        hidden_ref, pre_ref, out_ref, back_ref, turned_ref = refs
    else:
        hidden_ref, pre_ref, out_ref, back_ref, turned_ref, w_up, w_down, sems = refs[-8:]
        pieces = refs[:-8]
        todo = []
        for group in range(2):
            batch = []
            for k, target in enumerate((w_up, w_down)):
                batch += copies(plans[group][k], rows, pieces, target.at[group], first_slot, table, sems.at[group, k])
            for copy in batch:
                copy.start()
            todo.append(batch)
    width = w_up.shape[2]
    each = width // CHUNK
    put_turned(table, base, turn_rows, unit_ref[...].T, turned_ref)

    @pl.loop(0, 2 * each)
    def _(step):
        if plans is not None:
            for group in range(2):

                @pl.when(step == group * each)
                def _(group=group):
                    for copy in todo[group]:
                        copy.wait()

        group = step // each
        here = pl.ds(pl.multiple_of(step % each * CHUNK, CHUNK), CHUNK)
        there = pl.ds(pl.multiple_of(step * CHUNK, CHUNK), CHUNK)
        pre = dot(unit_ref[...], w_up[group, :, here]) + bias[:, there]
        d_hidden = dot(grad_ref[...], w_down[group, :, here])
        share = 0.5 + 0.5 * lax.erf(pre * math.sqrt(0.5))
        hidden_ref[:, there] = (pre * share).astype(BF)
        slope = share + pre * (jnp.exp(-0.5 * pre * pre) * (1.0 / math.sqrt(2.0 * math.pi)))
        pre_ref[:, there] = (d_hidden * slope).astype(BF)

    for target, values, weights in ((out_ref, hidden_ref, w_down), (back_ref, pre_ref, w_up)):
        made = dot_t(values[:, :width], weights[0]) + dot_t(values[:, width:], weights[1])
        target[...] = made.astype(target.dtype)


def feed(table, unit, grad, bias, weights, rows, turn_rows, base, first_slot, dtype):
    n, d = unit.shape
    width = bias.shape[-1] // 2
    made = [
        jax.ShapeDtypeStruct((n, 2 * width), BF),
        jax.ShapeDtypeStruct((n, 2 * width), BF),
        jax.ShapeDtypeStruct((n, d), dtype),
        jax.ShapeDtypeStruct((n, d), dtype),
        jax.ShapeDtypeStruct((d, n), BF),
    ]
    if isinstance(weights[0], tuple):
        arrays = []
        plans = [[loader(pieces, rows, arrays) for pieces in group] for group in weights]
        specs = [pl.BlockSpec(memory_space=pl.ANY)] * len(arrays)
        made += [jax.ShapeDtypeStruct((2, d, width), BF)] * 2
        scratch = [pltpu.SemaphoreType.DMA((2, 2, len(plans[0][0])))]
    else:
        arrays, plans, specs, scratch = list(weights), None, [VMEM, VMEM], []
    return pl.pallas_call(
        functools.partial(feed_kernel, plans, rows, turn_rows, base, first_slot),
        in_specs=[SMEM] + [VMEM] * 3 + specs,
        out_specs=[VMEM] * len(made),
        out_shape=made,
        scratch_shapes=scratch,
        compiler_params=pltpu.CompilerParams(vmem_limit_bytes=LIMIT),
        cost_estimate=COST,
        name="feed",
    )(table, unit, grad, bias, *arrays)


def weights_kernel(last, block, turned, grad, hidden, pre, *refs):
    before, refs = (refs[:6], refs[6:]) if last else (None, refs)
    half = refs[0].shape[0] // 2
    width = refs[0].shape[1]
    for group in (1, 0):
        outs = refs[3 * group : 3 * group + 3]
        olds = before[3 * group : 3 * group + 3] if last else None

        @pl.loop(0, width // CHUNK)
        def _(step, group=group, outs=outs, olds=olds):
            here = pl.ds(pl.multiple_of(step * CHUNK, CHUNK), CHUNK)
            there = pl.ds(pl.multiple_of(group * width + step * CHUNK, CHUNK), CHUNK)
            made = (dot(turned[...], pre[:, there]), dot(grad[...], hidden[:, there]))
            for side in range(2):
                for k in range(2 * half // block):
                    rows = slice(k * block, (k + 1) * block)
                    start = side * half + k // 2 * block
                    part = made[k % 2][start : start + block]
                    if last:
                        part = part + olds[side][rows, here].astype(F32)
                    outs[side][rows, here] = part.astype(BF)
            column = jnp.sum(pre[:, there].astype(F32), axis=0, keepdims=True)
            outs[2][:, here] = column + olds[2][:, here] if last else column


def weights_grad(turned, grad_turned, hidden, pre, before, block):
    d = turned.shape[0]
    width = hidden.shape[1] // 2
    made = [jax.ShapeDtypeStruct((d, width), BF)] * 2 + [jax.ShapeDtypeStruct((1, width), F32)]
    return pl.pallas_call(
        functools.partial(weights_kernel, bool(before), block),
        in_specs=[VMEM] * (4 + len(before)),
        out_specs=[VMEM] * 6,
        out_shape=made * 2,
        input_output_aliases={4 + k: k for k in range(len(before))},
        compiler_params=pltpu.CompilerParams(vmem_limit_bytes=LIMIT),
        cost_estimate=COST,
        name="weights_grad",
    )(turned, grad_turned, hidden, pre, *before)


def middle_kernel(back_a, back_b, mid_ref, grad_ref, gain, full_ref, short_ref, sums_ref):
    unit, scale = norm(mid_ref[...])
    back = back_a[...] + back_b[...].astype(F32)
    grad = grad_ref[...].astype(F32)
    full = grad + norm_back(back * gain[...], unit, scale)
    full_ref[...] = full
    short_ref[...] = full.astype(BF)
    sums_ref[...] = jnp.zeros_like(sums_ref)
    sums_ref[0:1] = jnp.sum(back * unit, axis=0, keepdims=True)
    sums_ref[1:2] = jnp.sum(back, axis=0, keepdims=True)
    sums_ref[2:3] = jnp.sum(full, axis=0, keepdims=True)
    sums_ref[3:4] = jnp.sum(grad, axis=0, keepdims=True)


def middle(back_a, back_b, mid, grad, gain):
    n, d = mid.shape
    return pl.pallas_call(
        middle_kernel,
        in_specs=[VMEM] * 5,
        out_specs=[VMEM] * 3,
        out_shape=[
            jax.ShapeDtypeStruct((n, d), F32),
            jax.ShapeDtypeStruct((n, d), BF),
            jax.ShapeDtypeStruct((8, d), F32),
        ],
        compiler_params=pltpu.CompilerParams(vmem_limit_bytes=LIMIT),
        cost_estimate=COST,
        name="middle",
    )(back_a, back_b, mid, grad, gain)


def back_kernel(first_near, blocks, last_call, table, made_ref, key_ref, row_ref, total_ref, w_ref, short_a, short_b, *refs):
    if last_call:
        before_ref, dq_ref, out_ref, d_ref, p_ref, dp_ref, sum_ref = refs
        sum_ref[...] = before_ref[...]
    else:
        dq_ref, sum_ref, d_ref, p_ref, dp_ref = refs
        sum_ref[...] = jnp.zeros_like(sum_ref)
    scale = HEAD ** (-0.5)
    n = blocks * BLOCK
    for slot, short in enumerate((short_a, short_b)):
        d_ref[slot * n : (slot + 1) * n] = dot(short[...], w_ref[...]).astype(BF)

    @pl.loop(0, 2 * blocks)
    def _(step):
        here = pl.ds(pl.multiple_of(step * BLOCK, BLOCK), BLOCK)
        number, own, first, last = block_places(table, first_near, step, blocks)
        rows = pl.ds(own, BLOCK)
        q_all = split_heads(made_ref[rows, 0:128], made_ref[rows, 384:512], True)
        d_all = split_heads(d_ref[here, 128:256], d_ref[here, 0:128], False)
        row = row_ref[pl.ds(number, 1), :]
        place = own + lax.broadcasted_iota(jnp.int32, (BLOCK, BLOCK), 1)
        totals = [total_ref[h : h + 1, here] for h in range(3)]

        def weigh(j, inners):
            start = pl.multiple_of(j * BLOCK, BLOCK)
            spot = pl.ds(start, BLOCK)
            bias = pair_bias(key_ref, row, place, start)
            new, add_v = [], []
            for h in range(3):
                keys = made_ref[spot, 128:256] if h < 2 else made_ref[spot, 512:640]
                values = made_ref[spot, 256:384] if h < 2 else made_ref[spot, 384:512]
                p = jnp.exp(dot_t(keys, q_all[h]) + bias - totals[h])
                d_p = dot_t(values, d_all[h])
                p_ref[h, j] = p
                dp_ref[h, j] = d_p
                new.append(inners[h] + jnp.sum((p * d_p).reshape(BLOCK // 8, 8, BLOCK), axis=0))
                add_v.append(dot(p.astype(BF), d_all[h]))
            sum_ref[spot, 128:256] += add_v[0] + add_v[1]
            sum_ref[spot, 256:384] += add_v[2]
            return tuple(new)

        inners = lax.fori_loop(first, last, weigh, (jnp.zeros((8, BLOCK), F32),) * 3)
        inners = [jnp.sum(v, axis=0, keepdims=True) for v in inners]

        def turn(j, sums):
            spot = pl.ds(pl.multiple_of(j * BLOCK, BLOCK), BLOCK)
            pair_t, third_t = made_ref[spot, 128:256].T, made_ref[spot, 512:640].T
            turned = (pair_t[:HEAD], pair_t[HEAD:], third_t[:HEAD])
            new, add_k = [], []
            for h in range(3):
                d_s = (p_ref[h, j] * (dp_ref[h, j] - inners[h])).astype(BF)
                add_k.append(dot(d_s, q_all[h]))
                new.append(sums[h] + dot(turned[h], d_s))
            sum_ref[spot, 0:128] += add_k[0] + add_k[1]
            sum_ref[spot, 384:512] += add_k[2]
            return tuple(new)

        sums = lax.fori_loop(first, last, turn, (jnp.zeros((HEAD, BLOCK), F32),) * 3)
        two = jnp.concatenate([sums[0], sums[1]], axis=0).T.astype(BF) * jnp.asarray(scale, BF)
        one = jnp.concatenate([sums[2], jnp.zeros_like(sums[2])], axis=0).T.astype(BF) * jnp.asarray(scale, BF)
        dq_ref[here, :] = two
        sum_ref[rows, 256:384] += one.astype(F32)

    if last_call:
        out_ref[...] = sum_ref[...].astype(BF)


def attend_back(first_near, table, made, key, row, total, w, shorts, before):
    keys = made.shape[0]
    n = keys // 4
    last_call = before is not None
    operands = [table, made, key, row, total, w, *shorts] + ([before] if last_call else [])
    scores = pltpu.VMEM((3, keys // BLOCK, BLOCK, BLOCK), F32)
    scratch = [pltpu.VMEM((2 * n, 256), BF), scores, scores]
    if last_call:
        scratch.append(pltpu.VMEM((keys, 512), F32))
    return pl.pallas_call(
        functools.partial(back_kernel, first_near, n // BLOCK, last_call),
        in_specs=[SMEM] + [VMEM] * (len(operands) - 1),
        out_specs=[VMEM] * 2,
        out_shape=[
            jax.ShapeDtypeStruct((2 * n, 128), BF),
            jax.ShapeDtypeStruct((keys, 512), BF if last_call else F32),
        ],
        scratch_shapes=scratch,
        compiler_params=pltpu.CompilerParams(vmem_limit_bytes=LIMIT),
        cost_estimate=COST,
        name="attend_back",
    )(*operands)


def grads_kernel(rows, base, table, dkv_ref, dq_a, dq_b, *refs):
    sources, refs = refs[:8], refs[8:]
    outs, (keep_ref, send_ref, column_ref, sum_ref, w_ref, turned_ref, shorts, contexts, dqs, sems) = refs[:4], refs[4:]
    n = shorts.shape[1]
    half = keep_ref.shape[0]
    targets = [w_ref, dqs.at[: 2 * n], dqs.at[2 * n :], turned_ref, *[shorts.at[k] for k in range(4)]]
    targets += [contexts.at[: 2 * n], contexts.at[2 * n :]]
    going = stage((sources[0], dq_a, dq_b, *sources[1:]), targets, sems)
    for copy in going[:3]:
        copy.wait()
    for near in (3, 2, 1, 0):
        here = pl.ds(pl.multiple_of((table[0] ^ near) * n, n), n)
        own = slice(near * n, (near + 1) * n)
        outs[near][...] = (dot_t(dkv_ref[here, :], w_ref[:, 128:640]) + dot_t(dqs[own, :], w_ref[:, 0:128])).astype(BF)
    for copy in going[3:]:
        copy.wait()
    sum_ref[:, 128:640] = dot(turned_ref[...], dkv_ref[...])
    column_ref[:, 128:640] = jnp.sum(dkv_ref[...].astype(F32), axis=0, keepdims=True)
    column_ref[:, 0:128] = jnp.sum(dqs[...].astype(F32), axis=0, keepdims=True)
    sum_ref[:, 0:128] = jnp.zeros_like(sum_ref[:, 0:128])
    sum_ref[:, 640:768] = jnp.zeros_like(sum_ref[:, 640:768])

    @pl.loop(0, 4)
    def _(near):
        here = pl.ds(pl.multiple_of((table[0] ^ near) * n, n), n)
        own = pl.ds(pl.multiple_of(near * n, n), n)
        sum_ref[:, 0:128] += dot(turned_ref[:, here], dqs[own, :])
        out = t_dot(shorts[near], contexts[own, :])
        for k in range(out.shape[0] // rows):
            spot = pl.ds(pl.multiple_of(table[base + k], rows), rows)
            sum_ref[spot, 512:768] += out[k * rows : (k + 1) * rows]

    keep_ref[...] = sum_ref[:half, :].astype(BF)
    send_ref[...] = sum_ref[half:, :].astype(BF)


def grads(table, w, turned, dqs, dkv, shorts, contexts, rows, base):
    d = turned.shape[0]
    n = shorts[0].shape[0]
    return pl.pallas_call(
        functools.partial(grads_kernel, rows, base),
        in_specs=[SMEM] + [VMEM] * 3 + [HBM] * 8,
        out_specs=[VMEM] * 7,
        out_shape=[jax.ShapeDtypeStruct((n, d), BF)] * 4
        + [jax.ShapeDtypeStruct((d // 2, 768), BF)] * 2
        + [jax.ShapeDtypeStruct((1, 640), F32)],
        scratch_shapes=[
            pltpu.VMEM((d, 768), F32),
            pltpu.VMEM(w.shape, BF),
            pltpu.VMEM(turned.shape, BF),
            pltpu.VMEM((4, n, d), BF),
            pltpu.VMEM((4 * n, 256), BF),
            pltpu.VMEM((4 * n, 128), BF),
            pltpu.SemaphoreType.DMA((10,)),
        ],
        compiler_params=pltpu.CompilerParams(vmem_limit_bytes=60 << 20),
        cost_estimate=COST,
        name="grads",
    )(table, dkv, *dqs, w, turned, *shorts, *contexts)


def final_kernel(one_ref, core_ref, two_ref, stream_hbm, full_hbm, gain, early_ref, col_a, col_b, col_one,
                 grad_ref, sums_ref, stream_ref, full_ref, sems):
    going = stage((stream_hbm, full_hbm), (stream_ref, full_ref), sems)
    back = one_ref[...].astype(F32) + core_ref[...].astype(F32) + two_ref[...].astype(F32)
    for copy in going:
        copy.wait()
    unit, scale = norm(stream_ref[...])
    grad = full_ref[...] + norm_back(back * gain[...], unit, scale)
    grad_ref[...] = grad
    sums_ref[0:1] = jnp.sum(back * unit, axis=0, keepdims=True)
    sums_ref[1:2] = jnp.sum(back, axis=0, keepdims=True)
    sums_ref[2:3] = jnp.sum(grad, axis=0, keepdims=True)
    sums_ref[3:7] = early_ref[0:4]
    sums_ref[7:8] = col_b[...]
    sums_ref[8:9] = col_a[...]
    sums_ref[9:16] = jnp.zeros_like(sums_ref[9:16])
    sums_ref[9:10, : col_one.shape[1]] = col_one[...]


def small_call(kernel, shapes, limit=LIMIT):
    def call(*operands):
        return pl.pallas_call(
            kernel,
            in_specs=[VMEM] * len(operands),
            out_specs=[VMEM] * len(shapes),
            out_shape=[jax.ShapeDtypeStruct(shape, F32) for shape in shapes],
            compiler_params=pltpu.CompilerParams(vmem_limit_bytes=limit),
            cost_estimate=COST,
            name=getattr(kernel, "__name__", "finish"),
        )(*operands)

    return call


def core_sums(own, there, out):
    out[0:7] = own[0:7] + there[0:7]
    out[7:8] = own[8:9] + there[7:8]
    out[8:9] = own[9:10]
    out[9:16] = jnp.zeros_like(own[9:16])


def row_sums(own, there, seat, spread, out):
    dp = seat.shape[0]
    both = own[0:7] + there[0:7]
    out[0:2] = both[0:2]
    out[2:6] = both[3:7]
    out[6:8] = own[7:9]
    out[8 : 8 + dp] = seat[...] * both[2:3]
    out[8 + dp : 8 + dp + spread.shape[0]] = spread[...]


def finish_kernel(dp, features, columns, count, *refs):
    parts, (pick, gain_ref, bias_ref, query_ref, value_ref, up_ref, time_ref) = refs[:count], refs[count:]
    total = parts[0][...]
    for part in parts[1:]:
        total = total + part[...]
    by_sequence = total[8 : 8 + dp]
    gain_ref[0:1] = total[0:1]
    gain_ref[1:2] = total[2:3]
    bias_ref[0:1] = total[1:2]
    bias_ref[1:4] = total[3:6]
    bias_ref[4:5] = jnp.sum(by_sequence, axis=0, keepdims=True)
    up_ref[...] = total[6:7]
    query_ref[...] = jnp.concatenate([total[7:8, 0:128], total[7:8, 384:448]], axis=1)
    value_ref[...] = jnp.concatenate([total[7:8, 256:384], total[7:8, 448:512]], axis=1)
    wide = total.shape[1] // features
    rows = [total[8 + dp + k // wide : 9 + dp + k // wide, k % wide * features : (k % wide + 1) * features] for k in range(dp)]
    share = jnp.dot(by_sequence, pick[...], precision=highest, preferred_element_type=F32)
    time_ref[...] = lax.dot_general(
        jnp.concatenate(rows, axis=0), share, (((0,), (0,)), ((), ())), precision=highest, preferred_element_type=F32
    )


def final(one, core, two, stream, full, gain, early, cols, col_one):
    n, d = stream.shape
    return pl.pallas_call(
        final_kernel,
        in_specs=[VMEM] * 3 + [HBM] * 2 + [VMEM] * 5,
        out_specs=[VMEM] * 2,
        out_shape=[jax.ShapeDtypeStruct((n, d), F32), jax.ShapeDtypeStruct((16, d), F32)],
        scratch_shapes=buffers_of((stream, full)),
        compiler_params=pltpu.CompilerParams(vmem_limit_bytes=60 << 20),
        cost_estimate=COST,
        name="final",
    )(one, core, two, stream, full, gain, early, *cols, col_one)


def add_kernel(*refs):
    total = refs[0][...].astype(F32)
    for ref in refs[1:-1]:
        total = total + ref[...].astype(F32)
    refs[-1][...] = total.astype(refs[-1].dtype)


def low_sum(*terms, rows=None, dtype=BF):
    terms = [v if isinstance(v, tuple) else (v, 0) for v in terms]
    rows = rows or min(v.shape[0] for v, _ in terms)
    block = rows // (4 if rows % 64 == 0 else 1)
    width = terms[0][0].shape[1]
    return pl.pallas_call(
        add_kernel,
        grid=(rows // block,),
        in_specs=[
            pl.BlockSpec((block, width), functools.partial(lambda first, i: (i + first, 0), start // block))
            for _, start in terms
        ],
        out_specs=pl.BlockSpec((block, width), lambda i: (i, 0)),
        out_shape=jax.ShapeDtypeStruct((rows, width), dtype),
        compiler_params=params("arbitrary"),
        cost_estimate=COST,
        name="low_sum",
    )(*[v for v, _ in terms])


def stack_kernel(*refs):
    for k, ref in enumerate(refs[:-1]):
        refs[-1][k] = ref[...]


def stack(values):
    return pl.pallas_call(
        stack_kernel,
        in_specs=[VMEM] * len(values),
        out_specs=VMEM,
        out_shape=jax.ShapeDtypeStruct((len(values),) + values[0].shape, values[0].dtype),
        compiler_params=pltpu.CompilerParams(vmem_limit_bytes=LIMIT),
        cost_estimate=COST,
        name="stack",
    )(*values)


def tie(values, after):
    return lax.optimization_barrier((values, after))[0]


def line_sums(terms, starts, size, rows):
    found = [[(v, start + by * rows) for v, start in zip(terms, starts, strict=True)] for by in range(size)]
    return low_sum(*found[0], rows=rows, dtype=F32), [low_sum(*pairs, rows=rows) for pairs in found[1:]]


def along_line(sent, size):
    return [shift(v, "d1", size, by + 1) for by, v in enumerate(sent)]


def scatter_dp(value):
    return lax.psum_scatter(value, ("d1", "d0"), scatter_dimension=0, tiled=True).astype(F32)


def shards(
    inputs,
    segment_ids,
    keep_mask,
    timestep,
    w_qkv,
    b_query,
    b_value,
    w_out,
    w_up,
    b_up,
    w_down,
    time_weight,
    gains,
    row_biases,
    d_out,
):
    size = lax.axis_size("d1")
    long = size > 4
    z, x = lax.axis_index("d1"), lax.axis_index("d0")
    own = lax.axis_index("t1") * 2 + lax.axis_index("t0")
    n, d = inputs.shape
    dp = 2 * size
    place = z * 2 + x
    features = time_weight.shape[0]
    columns = time_weight.shape[1]

    rows = w_up.shape[0]
    blocks = 4 * n // BLOCK
    ids = segment_ids.reshape(blocks, BLOCK)
    first = jnp.sum(segment_ids[None, :] < ids[:, :1], axis=1, dtype=jnp.int32)
    last = jnp.sum(segment_ids[None, :] <= ids[:, -1:], axis=1, dtype=jnp.int32)
    span = jnp.stack([first // BLOCK, (last + BLOCK - 1) // BLOCK], axis=1).reshape(-1)
    slots = [(lax.rem(z - s + size, size) * 2 + (x ^ a)) * rows for a in range(2) for s in range(size)]
    places = [((k % 2 ^ x) * size + k // 2) * rows for k in range(dp)]
    slots_two = [(s * 2 + (x ^ a)) * rows for a in range(2) for s in range(size)]
    if long:
        nothing = [jnp.zeros_like(own)]
        slots, places, slots_two, turn_rows = nothing, nothing, nothing, d
    else:
        turn_rows = rows
    base = 1 + len(slots)
    slot_two = base + len(places)
    table_one = jnp.stack([own, *slots, *places, *slots_two]).astype(jnp.int32)
    table_two = jnp.concatenate([jnp.stack([own]), span]).astype(jnp.int32)
    key = jnp.where(keep_mask > 0, segment_ids, -1)[:, None]
    own_keep = lax.dynamic_slice_in_dim(keep_mask, own * n, n, 0)[:, None]
    up_core = swap(b_up[None], "t0")
    grad_two, grad_turned = cotangent(table_one, d_out[None], own_keep, turn_rows, base)

    pack_one = jnp.concatenate(
        [pack_columns(w_qkv[0], w_qkv[1], w_qkv[2]), time_weight.T, pack_outer(w_out.T)], axis=1
    )
    rows = pack_one.shape[0]
    if long:
        half = lax.all_gather(pack_one, ("d1", "d0"), axis=0, tiled=True)
        pieces_one = [(half, None, 0)]
    else:
        line = [pack_one] + [shift(pack_one, "d1", size, by) for by in range(1, size)]
    x_core = swap(inputs, "t0")
    x_far_a = swap(inputs[: n // 2], "t1")
    if not long:
        half = stack(tie(line, (x_core, grad_two, grad_turned, key, x_far_a)))
        other_half = swap(half, "d0")
        pieces_one = [(half, (s, 0), s) for s in range(size)] + [(other_half, (s, 0), size + s) for s in range(size)]
    x_far_b = tie(swap(inputs[n // 2 :], "t1"), half)
    x_near = [inputs, x_core, x_far_a, x_far_b, swap(x_far_a, "t0"), swap(x_far_b, "t0")]
    time_rows = sinusoid(timestep, features).astype(BF)
    times = jnp.pad(time_rows, ((0, 7), (0, 0)))
    seat = (jnp.arange(dp) == place).astype(F32)[:, None]
    spread = (seat * time_rows.astype(F32)).reshape(1, -1)
    spread = jnp.pad(spread, ((0, 0), (0, -spread.shape[1] % d))).reshape(-1, d)
    bias_one = pack_columns(b_query, jnp.zeros_like(b_query), b_value)[None, :]

    scale = jnp.where(
        (jnp.arange(640) < 128) | ((jnp.arange(640) >= 384) & (jnp.arange(640) < 448)), HEAD ** (-0.5), 1.0
    ).astype(F32)[None, :]

    far_keep = lax.dynamic_slice_in_dim(keep_mask, (own ^ 2) * n, n, 0)[:, None]
    d_far = swap(tie(d_out, x_far_b), "t1")
    d_far = swap(tie(d_out, x_far_b), "t1")

    if long:
        gathered = lax.all_gather(jnp.stack([w_up, w_down.T]), ("d1", "d0"), axis=1, tiled=True)
        other = swap(gathered, "t0")
        feed_weights = [tuple([(v[k], None, 0)] for k in range(2)) for v in (gathered, other)]
        rows_two = d
    else:
        gathered = lax.all_gather(tie(jnp.concatenate([w_up, w_down.T]), half), "d1")
        x_near = tie(x_near, up_core)
    made, turned_one, stream_in, w_one, outer_own = project(
        x_near, times, row_biases[4:5], gains[0:1], row_biases[0:1], bias_one, scale, pieces_one, d if long else rows,
        table_one, turn_rows, base,
    )
    outer_near = gather_near(outer_own)
    made_near = made_far = made
    if not long:
        gathered = tie(gathered, made)
        gathered_side, gathered_core = swap(gathered, "d0"), swap(gathered, "t0")
    context_far, total_far = attend(2, table_two, made_far, key, ids)
    context_over = swap(context_far, "t1")
    if not long:
        made_near = tie(made, (d_far, gathered_core))
    context_near, total_near = attend(0, table_two, made_near, key, ids)
    grad_far, grad_turned_far = cotangent(table_one, tie(d_far, context_near)[None], far_keep, turn_rows, base)
    context_over = tie(context_over, grad_far if long else (grad_far, gathered_side))
    contexts = [context_near, swap(context_near, "t0"), context_over, swap(context_over, "t0")]
    if not long:
        def pieces_of(near, other, part):
            return [(v, (s, part), a * size + s) for a, v in enumerate((near, other)) for s in range(size)]

        pairs = ((gathered, gathered_side), (gathered_core, swap(gathered_side, "t0")))
        feed_weights = [tuple(pieces_of(*pair, part) for part in range(2)) for pair in pairs]
        rows_two = rows
    stream_mid, unit_two = outer(
        table_one, contexts, outer_near, stream_in, gains[1:2], row_biases[1:2], row_biases[2:3]
    )

    biases = jnp.concatenate([b_up[None], up_core], axis=1)
    block = d // 2 if long else rows
    unit_far = swap(unit_two, "t1")
    hidden, pre, out, back, turned_two, *feed_arrays = feed(
        table_one, unit_two, grad_two, biases, feed_weights, rows_two, turn_rows, base, slot_two, F32
    )
    own_grads = weights_grad(turned_two, grad_turned, hidden, pre, [], block)
    hidden_far, pre_far, out_far, back_far, turned_far = feed(
        table_one, tie(unit_far, own_grads), grad_far, biases, feed_arrays, rows_two, turn_rows, base, slot_two, BF
    )
    back_over = swap(back_far, "t1")
    part = d // 2
    keep_a, send_a, column_a, keep_b, send_b, column_b = weights_grad(turned_far, grad_turned_far, hidden_far, pre_far, own_grads, block)
    keep_b, send_b = to_core((keep_b, send_b))
    full, short, sums_two = middle(back, back_over, stream_mid, grad_two, gains[1:2])
    short_core, short_over = swap(short, "t0"), swap(short, "t1")
    send_b = tie(send_b, short)
    sent = low_sum(send_a, send_b)
    over = sent if long else swap(sent, "d0")
    shorts = tie([short, short_core], sent)
    dq_near, sum_near = attend_back(0, table_two, made, key, ids, total_near, outer_own, shorts, None)
    short_over = tie(short_over, sum_near)
    shorts = [short_over, swap(short_over, "t0")]
    short_near = [short, short_core] + shorts
    if long:
        kept = low_sum(keep_a, keep_b)
        up_share = scatter_dp(jnp.concatenate([kept[:part], sent[:part]]))
        down_share = scatter_dp(jnp.concatenate([kept[part:], sent[part:]]))
    dq_far, dkv = attend_back(2, table_two, made, key, ids, total_far, outer_own, shorts, sum_near)
    if not long:
        kept = low_sum(keep_a, keep_b, tie(over, dkv))
        both_share = lax.psum_scatter(kept, "d1", scatter_dimension=0, tiled=True)
        dkv = tie(dkv, kept)
    out_over, dkv = tie((swap(tie(out_far, short_over), "t1"), dkv), dkv)
    back_a, back_b, back_c, back_d, grad_keep, grad_send, column_one = grads(
        table_one, w_one, turned_one, [dq_near, dq_far], dkv, short_near, [context_near, context_far], turn_rows, base
    )
    back_d, back_b = swap(back_d, "t0"), swap(back_b, "t0")
    back_far = low_sum(back_c, tie(back_d, back_b))
    other = swap(back_far, "t1")
    if long:
        one_share = scatter_dp(jnp.concatenate([grad_keep, grad_send]))
    else:
        grad_over = swap(grad_send, "d0")
        one_sum = (grad_keep.astype(F32) + tie(grad_over, other).astype(F32)).astype(BF)
        one_share = lax.psum_scatter(one_sum, "d1", scatter_dimension=0, tiled=True).astype(F32)
    grad_input, small = final(
        back_a, back_b, other, stream_in, full, gains[0:1], sums_two, (column_a, column_b), column_one
    )

    out_over = tie(out_over, small)
    output = (stream_mid + out + out_over.astype(F32) + row_biases[3]).astype(BF)

    (small,) = small_call(core_sums, [(16, d)])(small, swap(small, "t0"))
    height = 8 + dp + spread.shape[0]
    (small,) = small_call(row_sums, [(height, d)])(small, swap(small, "t1"), seat, spread)
    small = small + swap(small, "d0")
    parts = [lax.psum(small, "d1")] if long else [small] + [shift(small, "d1", size, by) for by in range(1, size)]
    pick = (jnp.arange(d)[:, None] == place * columns + jnp.arange(columns)[None, :]).astype(F32)
    width = b_query.shape[0]
    gain_total, bias_total, column_query, column_value, up_bias, grad_time = small_call(
        functools.partial(finish_kernel, dp, features, columns, len(parts)),
        [(2, d), (5, d), (1, width), (1, width), (1, d), (features, columns)],
    )(*parts, pick)
    if not long:
        up_share, down_share = both_share[:rows].astype(F32), both_share[rows:].astype(F32)
    d_query, d_key, d_value, d_outer = unpack_columns(one_share)
    return (
        output,
        grad_input,
        jnp.stack([d_query, d_key, d_value]),
        column_query[0],
        column_value[0],
        d_outer.T,
        up_share,
        up_bias[0],
        down_share.T,
        grad_time,
        gain_total,
        bias_total,
    )


def solution(mesh):
    dp, tensor = mesh.shape["dp"], mesh.shape["tensor"]
    fine = Mesh(mesh.devices.reshape(dp // 2, 2, tensor // 2, 2), ("d1", "d0", "t1", "t0"))
    rows, cols = ("d1", "d0"), ("t1", "t0")
    every = rows + cols
    in_specs = (
        P(every, None),
        P(rows),
        P(rows),
        P(rows),
        P(None, rows, cols),
        P(cols),
        P(cols),
        P(cols, rows),
        P(rows, cols),
        P(cols),
        P(cols, rows),
        P(None, rows),
        P(),
        P(),
        P(every, None),
    )
    out_specs = (
        P(every, None),
        P(every, None),
        P(None, rows, cols),
        P(cols),
        P(cols),
        P(cols, rows),
        P(rows, cols),
        P(cols),
        P(cols, rows),
        P(None, rows),
        P(),
        P(),
    )
    return jax.shard_map(shards, mesh=fine, in_specs=in_specs, out_specs=out_specs, check_vma=False)
```

```python
import functools
import math

import jax
import jax.numpy as jnp
from jax import lax
from jax.experimental import pallas as pl
from jax.experimental.pallas import tpu as pltpu
from jax.sharding import Mesh
from jax.sharding import PartitionSpec as P

HEAD = 64
SEQ_LEN = 2048
BLOCK = 256
F32 = jnp.float32
BF = jnp.bfloat16

epsilon = 1e-05
masked = -1e30
highest = lax.Precision.HIGHEST

LIMIT = 32 << 20
COST = pl.CostEstimate(flops=10**5, bytes_accessed=10**5, transcendentals=0)


def dot(left, right):
    return jnp.dot(left, right, preferred_element_type=F32)


def dot_t(left, right):
    return lax.dot_general(left, right, (((1,), (1,)), ((), ())), preferred_element_type=F32)


def t_dot(left, right):
    return lax.dot_general(left, right, (((0,), (0,)), ((), ())), preferred_element_type=F32)


def params(*semantics, limit=LIMIT):
    return pltpu.CompilerParams(dimension_semantics=semantics, vmem_limit_bytes=limit)


def whole(shape):
    rank = len(shape)
    return pl.BlockSpec(shape, lambda *_: (0,) * rank)


def stage(sources, buffers, sems):
    going = [pltpu.make_async_copy(s, b, sems.at[k]) for k, (s, b) in enumerate(zip(sources, buffers, strict=True))]
    for copy in going:
        copy.start()
    return going


def buffers_of(values):
    return [pltpu.VMEM(v.shape, v.dtype) for v in values] + [pltpu.SemaphoreType.DMA((len(values),))]


def sinusoid(timesteps, features):
    half_width = features // 2
    frequency = jnp.exp(-math.log(10000.0) * jnp.arange(half_width, dtype=F32) / half_width)
    angles = timesteps.astype(F32)[:, None] * frequency[None, :]
    return jnp.concatenate([jnp.cos(angles), jnp.sin(angles)], axis=1)


def swap(value, axis):
    return lax.ppermute(value, axis, [(0, 1), (1, 0)])


def shift(value, axis, size, by):
    return lax.ppermute(value, axis, [(i, (i + by) % size) for i in range(size)])


def gather_near(value):
    far = swap(value, "t1")
    return [value, swap(value, "t0"), far, swap(far, "t0")]


def to_core(values):
    return [swap(v, "t0") for v in values]


def loader(pieces, rows, arrays):
    plan = []
    for value, lead, slot in pieces:
        for n, known in enumerate(arrays):
            if known is value:
                break
        else:
            n = len(arrays)
            arrays.append(value)
        plan.append((n, lead, slot))
    return plan


def copies(plan, rows, refs, target, base, table, sems):
    out = []
    for k, (n, lead, slot) in enumerate(plan):
        source = refs[n] if lead is None else refs[n].at[lead[0], pl.ds(lead[1] * rows, rows), :]
        if table is None:
            start = slot * rows
        else:
            start = pl.multiple_of(table[base + slot], rows)
        out.append(pltpu.make_async_copy(source, target.at[pl.ds(start, rows), :], sems.at[k]))
    return out


def norm(values):
    average = jnp.mean(values, axis=-1, keepdims=True)
    centered = values - average
    variance = jnp.mean(centered * centered, axis=-1, keepdims=True)
    scale = lax.rsqrt(variance + epsilon)
    return centered * scale, scale


def norm_back(gradient, unit, scale):
    one = jnp.mean(gradient, axis=-1, keepdims=True)
    two = jnp.mean(gradient * unit, axis=-1, keepdims=True)
    return scale * (gradient - one - unit * two)


def pack_columns(query, key, value):
    zeros = jnp.zeros_like(key[..., 128:])
    return jnp.concatenate(
        [query[..., :128], key[..., :128], value[..., :128], query[..., 128:], value[..., 128:], key[..., 128:], zeros],
        axis=-1,
    )


def pack_outer(out):
    return jnp.concatenate([jnp.zeros_like(out[..., 128:]), out[..., 128:], out[..., :128]], axis=-1)


def unpack_columns(pack):
    query = jnp.concatenate([pack[..., 0:128], pack[..., 384:448]], axis=-1)
    key = jnp.concatenate([pack[..., 128:256], pack[..., 512:576]], axis=-1)
    value = jnp.concatenate([pack[..., 256:384], pack[..., 448:512]], axis=-1)
    out = jnp.concatenate([pack[..., 640:768], pack[..., 576:640]], axis=-1)
    return query, key, value, out


VMEM = pl.BlockSpec(memory_space=pltpu.VMEM)
SMEM = pl.BlockSpec(memory_space=pltpu.SMEM)
HBM = pl.BlockSpec(memory_space=pltpu.HBM)


def put_turned(table, base, rows, value, target):
    for k in range(value.shape[0] // rows):
        here = pl.ds(pl.multiple_of(table[base + k], rows), rows)
        target[here, :] = value[k * rows : (k + 1) * rows]


def cotangent_kernel(rows, base, table, d_ref, keep_ref, grad_ref, turned_ref):
    value = d_ref[0]
    grad = jnp.where(keep_ref[...] > 0, value, jnp.zeros_like(value))
    grad_ref[...] = grad
    put_turned(table, base, rows, grad.T, turned_ref)


def cotangent(table, d_out, keep, rows, base):
    _, n, d = d_out.shape
    return pl.pallas_call(
        functools.partial(cotangent_kernel, rows, base),
        in_specs=[SMEM, VMEM, VMEM],
        out_specs=[VMEM, VMEM],
        out_shape=[jax.ShapeDtypeStruct((n, d), BF), jax.ShapeDtypeStruct((d, n), BF)],
        compiler_params=pltpu.CompilerParams(vmem_limit_bytes=LIMIT),
        cost_estimate=COST,
        name="cotangent",
    )(table, d_out, keep)


def project_kernel(plan, rows, turn_rows, base, table, *refs):
    sources, (times, add, gain, low_shift, bias, scale), refs = refs[:6], refs[6:12], refs[12:]
    count = len({n for n, _, _ in plan})
    pieces, (made_ref, turned_ref, stream_ref, w_out_ref, outer_ref, w_ref, embed_ref, sems, x_all, stage_sems) = refs[:count], refs[count:]
    near = pl.program_id(0)
    part = x_all.shape[1] // 2

    @pl.when(near == 0)
    def _():
        todo = copies(plan, rows, pieces, w_ref, 1, table, sems)
        for copy in todo:
            copy.start()
        targets = [x_all.at[0], x_all.at[1], x_all.at[2, :part], x_all.at[2, part:], x_all.at[3, :part], x_all.at[3, part:]]
        for copy in todo + stage(sources, targets, stage_sems):
            copy.wait()
        w_out_ref[...] = w_ref[:, 0:640]
        outer_ref[...] = w_ref[:, 768:1024]
        embed_ref[...] = dot_t(times[...], w_ref[:, 640:768]) + add[...]

    stream = x_all[near].astype(F32) + embed_ref[0:1]

    @pl.when(near == 0)
    def _():
        stream_ref[...] = stream

    unit, _ = norm(stream)
    low = (unit * gain[...] + low_shift[...]).astype(BF)
    made_ref[...] = ((dot(low, w_ref[:, :640]) + bias[...]) * scale[...]).astype(BF)
    put_turned(table, base, turn_rows, low.T, turned_ref)


def project(x_near, times, add, gain, low_shift, bias, scale, pieces, rows, table, turn_rows, base):
    n, d = x_near[0].shape
    arrays = []
    plan = loader(pieces, rows, arrays)
    small = (times, add, gain, low_shift, bias, scale)
    grid_spec = pltpu.PrefetchScalarGridSpec(
        num_scalar_prefetch=1,
        grid=(4,),
        in_specs=[HBM] * 6 + [whole(v.shape) for v in small] + [pl.BlockSpec(memory_space=pl.ANY)] * len(arrays),
        out_specs=[
            pl.BlockSpec((n, 640), lambda i, t: (t[0] ^ i, 0)),
            pl.BlockSpec((d, n), lambda i, t: (0, t[0] ^ i)),
            whole((n, d)),
            whole((d, 640)),
            whole((d, 256)),
        ],
        scratch_shapes=[
            pltpu.VMEM((d, 1024), BF),
            pltpu.VMEM((8, d), F32),
            pltpu.SemaphoreType.DMA((len(plan),)),
            pltpu.VMEM((4, n, d), BF),
            pltpu.SemaphoreType.DMA((6,)),
        ],
    )
    return pl.pallas_call(
        functools.partial(project_kernel, plan, rows, turn_rows, base),
        grid_spec=grid_spec,
        out_shape=[
            jax.ShapeDtypeStruct((4 * n, 640), BF),
            jax.ShapeDtypeStruct((d, 4 * n), BF),
            jax.ShapeDtypeStruct((n, d), F32),
            jax.ShapeDtypeStruct((d, 640), BF),
            jax.ShapeDtypeStruct((d, 256), BF),
        ],
        compiler_params=params("arbitrary", limit=60 << 20),
        cost_estimate=COST,
        name="project",
    )(table, *x_near, *small, *arrays)


def low_half(shape):
    return lax.broadcasted_iota(jnp.int32, shape, 1) < HEAD


def key_columns(key_ref, columns_ref):
    for j in range(key_ref.shape[0]):
        row = jnp.broadcast_to(key_ref[j : j + 1, :], (128, BLOCK))
        columns_ref[j * BLOCK : (j + 1) * BLOCK, :] = row.T


def pair_bias(columns_ref, row, own, start):
    key = columns_ref[pl.ds(start, BLOCK), :]
    gap = lax.broadcasted_iota(jnp.int32, key.shape, 0) - lax.broadcasted_iota(jnp.int32, key.shape, 1)
    sides = []
    for side in range(BLOCK // 128):
        same = (key == row[:, side * 128 : (side + 1) * 128]) | (gap == own - start + side * 128)
        sides.append(jnp.where(same, 0.0, masked))
    return jnp.concatenate(sides, axis=1)


def block_places(table, first_near, step, blocks):
    number = (table[0] ^ (first_near + step // blocks)) * blocks + step % blocks
    return number, pl.multiple_of(number * BLOCK, BLOCK), table[1 + 2 * number], table[2 + 2 * number]


def split_heads(pair, third, third_low):
    half = low_half(pair.shape)
    zero = jnp.zeros_like(pair)
    last = jnp.where(half, third, zero) if third_low else jnp.where(half, zero, third)
    return jnp.where(half, pair, zero), jnp.where(half, zero, pair), last


def attend_kernel(first_near, blocks, table, made_ref, key_ref, row_ref, context_ref, total_ref, score_ref, columns_ref):
    key_columns(key_ref, columns_ref)

    @pl.loop(0, 2 * blocks)
    def _(step):
        here = pl.ds(pl.multiple_of(step * BLOCK, BLOCK), BLOCK)
        number, own, first, last = block_places(table, first_near, step, blocks)
        rows = pl.ds(own, BLOCK)
        q_all = split_heads(made_ref[rows, 0:128], made_ref[rows, 384:512], True)
        row = row_ref[pl.ds(number, 1), :]

        def score(j, tops):
            start = pl.multiple_of(j * BLOCK, BLOCK)
            spot = pl.ds(start, BLOCK)
            bias = pair_bias(columns_ref, row, own, start)
            out = []
            for h in range(3):
                keys = made_ref[spot, 128:256] if h < 2 else made_ref[spot, 512:640]
                s = dot_t(keys, q_all[h]) + bias
                score_ref[h, j] = s
                out.append(jnp.maximum(tops[h], jnp.max(s.reshape(BLOCK // 8, 8, BLOCK), axis=0)))
            return tuple(out)

        begin = jnp.full((8, BLOCK), masked, F32)
        tops = lax.fori_loop(first, last, score, (begin,) * 3)
        tops = [jnp.max(t, axis=0, keepdims=True) for t in tops]

        def weigh(j, carry):
            spot = pl.ds(pl.multiple_of(j * BLOCK, BLOCK), BLOCK)
            pair_t = made_ref[spot, 256:384].T
            third_t = made_ref[spot, 384:512].T
            values = (pair_t[:HEAD], pair_t[HEAD:], third_t[HEAD:])
            sums, totals = carry
            new_sums, new_totals = [], []
            for h in range(3):
                p = jnp.exp(score_ref[h, j] - tops[h])
                new_totals.append(totals[h] + jnp.sum(p.reshape(BLOCK // 8, 8, BLOCK), axis=0))
                new_sums.append(sums[h] + dot(values[h], p.astype(BF)))
            return tuple(new_sums), tuple(new_totals)

        zeros = (jnp.zeros((HEAD, BLOCK), F32),) * 3
        sums, totals = lax.fori_loop(first, last, weigh, (zeros, (jnp.zeros((8, BLOCK), F32),) * 3))
        done = []
        for h in range(3):
            total = jnp.sum(totals[h], axis=0, keepdims=True)
            done.append(sums[h] / total)
            total_ref[h : h + 1, here] = tops[h] + jnp.log(total)
        context_ref[here, 0:128] = jnp.concatenate([jnp.zeros_like(done[2]), done[2]], axis=0).T.astype(BF)
        context_ref[here, 128:256] = jnp.concatenate([done[0], done[1]], axis=0).T.astype(BF)


def attend(first_near, table, made, key, row):
    keys = made.shape[0]
    n = keys // 4
    blocks = n // BLOCK
    return pl.pallas_call(
        functools.partial(attend_kernel, first_near, blocks),
        in_specs=[SMEM] + [VMEM] * 3,
        out_specs=[VMEM] * 2,
        out_shape=[jax.ShapeDtypeStruct((2 * n, 256), BF), jax.ShapeDtypeStruct((8, 2 * n), F32)],
        scratch_shapes=[pltpu.VMEM((3, keys // BLOCK, BLOCK, BLOCK), F32), pltpu.VMEM((keys, 128), jnp.int32)],
        compiler_params=pltpu.CompilerParams(vmem_limit_bytes=LIMIT),
        cost_estimate=COST,
        name="attend",
    )(table, made, key, row)


def outer_kernel(table, *refs):
    sources, (gain, low_shift, add, mid_ref, unit_ref, *buffers, sems) = refs[:9], refs[9:]
    going = stage(sources, buffers, sems)
    contexts, stream_ref = buffers[:4], buffers[8]
    for copy in going:
        copy.wait()
    mid = stream_ref[...] + add[...]
    n = stream_ref.shape[0]
    contexts = [context.at[k % 2 * n : (k % 2 + 1) * n] for k, context in enumerate(contexts)]
    for near, context in enumerate(contexts):
        mid = mid + dot_t(context[...], buffers[4 + near][...])
    mid_ref[...] = mid
    unit, _ = norm(mid)
    unit_ref[...] = (unit * gain[...] + low_shift[...]).astype(BF)


def outer(table, contexts, weights, stream, gain, low_shift, add):
    n, d = stream.shape
    staged = [*contexts, *weights, stream]
    return pl.pallas_call(
        outer_kernel,
        in_specs=[SMEM] + [HBM] * 9 + [VMEM] * 3,
        out_specs=[VMEM, VMEM],
        out_shape=[jax.ShapeDtypeStruct((n, d), F32), jax.ShapeDtypeStruct((n, d), BF)],
        scratch_shapes=buffers_of(staged),
        compiler_params=pltpu.CompilerParams(vmem_limit_bytes=60 << 20),
        cost_estimate=COST,
        name="outer",
    )(table, *staged, gain, low_shift, add)


CHUNK = 256


def feed_kernel(plans, rows, turn_rows, base, first_slot, table, unit_ref, grad_ref, bias, *refs):
    if plans is None:
        (w_up, w_down), refs = refs[:2], refs[2:]
        hidden_ref, pre_ref, out_ref, back_ref, turned_ref = refs
    else:
        hidden_ref, pre_ref, out_ref, back_ref, turned_ref, w_up, w_down, sems = refs[-8:]
        pieces = refs[:-8]
        todo = []
        for group in range(2):
            batch = []
            for k, target in enumerate((w_up, w_down)):
                batch += copies(plans[group][k], rows, pieces, target.at[group], first_slot, table, sems.at[group, k])
            for copy in batch:
                copy.start()
            todo.append(batch)
    width = w_up.shape[2]
    each = width // CHUNK
    put_turned(table, base, turn_rows, unit_ref[...].T, turned_ref)

    @pl.loop(0, 2 * each)
    def _(step):
        if plans is not None:
            for group in range(2):

                @pl.when(step == group * each)
                def _(group=group):
                    for copy in todo[group]:
                        copy.wait()

        group = step // each
        here = pl.ds(pl.multiple_of(step % each * CHUNK, CHUNK), CHUNK)
        there = pl.ds(pl.multiple_of(step * CHUNK, CHUNK), CHUNK)
        pre = dot(unit_ref[...], w_up[group, :, here]) + bias[:, there]
        d_hidden = dot(grad_ref[...], w_down[group, :, here])
        share = 0.5 + 0.5 * lax.erf(pre * math.sqrt(0.5))
        hidden_ref[:, there] = (pre * share).astype(BF)
        slope = share + pre * (jnp.exp(-0.5 * pre * pre) * (1.0 / math.sqrt(2.0 * math.pi)))
        pre_ref[:, there] = (d_hidden * slope).astype(BF)

    for target, values, weights in ((out_ref, hidden_ref, w_down), (back_ref, pre_ref, w_up)):
        made = dot_t(values[:, :width], weights[0]) + dot_t(values[:, width:], weights[1])
        target[...] = made.astype(target.dtype)


def feed(table, unit, grad, bias, weights, rows, turn_rows, base, first_slot, dtype):
    n, d = unit.shape
    width = bias.shape[-1] // 2
    made = [
        jax.ShapeDtypeStruct((n, 2 * width), BF),
        jax.ShapeDtypeStruct((n, 2 * width), BF),
        jax.ShapeDtypeStruct((n, d), dtype),
        jax.ShapeDtypeStruct((n, d), dtype),
        jax.ShapeDtypeStruct((d, n), BF),
    ]
    if isinstance(weights[0], tuple):
        arrays = []
        plans = [[loader(pieces, rows, arrays) for pieces in group] for group in weights]
        specs = [pl.BlockSpec(memory_space=pl.ANY)] * len(arrays)
        made += [jax.ShapeDtypeStruct((2, d, width), BF)] * 2
        scratch = [pltpu.SemaphoreType.DMA((2, 2, len(plans[0][0])))]
    else:
        arrays, plans, specs, scratch = list(weights), None, [VMEM, VMEM], []
    return pl.pallas_call(
        functools.partial(feed_kernel, plans, rows, turn_rows, base, first_slot),
        in_specs=[SMEM] + [VMEM] * 3 + specs,
        out_specs=[VMEM] * len(made),
        out_shape=made,
        scratch_shapes=scratch,
        compiler_params=pltpu.CompilerParams(vmem_limit_bytes=LIMIT),
        cost_estimate=COST,
        name="feed",
    )(table, unit, grad, bias, *arrays)


def weights_kernel(last, block, turned, grad, hidden, pre, *refs):
    before, refs = (refs[:6], refs[6:]) if last else (None, refs)
    half = refs[0].shape[0] // 2
    width = refs[0].shape[1]
    for group in (1, 0):
        outs = refs[3 * group : 3 * group + 3]
        olds = before[3 * group : 3 * group + 3] if last else None

        @pl.loop(0, width // CHUNK)
        def _(step, group=group, outs=outs, olds=olds):
            here = pl.ds(pl.multiple_of(step * CHUNK, CHUNK), CHUNK)
            there = pl.ds(pl.multiple_of(group * width + step * CHUNK, CHUNK), CHUNK)
            made = (dot(turned[...], pre[:, there]), dot(grad[...], hidden[:, there]))
            for side in range(2):
                for k in range(2 * half // block):
                    rows = slice(k * block, (k + 1) * block)
                    start = side * half + k // 2 * block
                    part = made[k % 2][start : start + block]
                    if last:
                        part = part + olds[side][rows, here].astype(F32)
                    outs[side][rows, here] = part.astype(BF)
            column = jnp.sum(pre[:, there].astype(F32), axis=0, keepdims=True)
            outs[2][:, here] = column + olds[2][:, here] if last else column


def weights_grad(turned, grad_turned, hidden, pre, before, block):
    d = turned.shape[0]
    width = hidden.shape[1] // 2
    made = [jax.ShapeDtypeStruct((d, width), BF)] * 2 + [jax.ShapeDtypeStruct((1, width), F32)]
    return pl.pallas_call(
        functools.partial(weights_kernel, bool(before), block),
        in_specs=[VMEM] * (4 + len(before)),
        out_specs=[VMEM] * 6,
        out_shape=made * 2,
        input_output_aliases={4 + k: k for k in range(len(before))},
        compiler_params=pltpu.CompilerParams(vmem_limit_bytes=LIMIT),
        cost_estimate=COST,
        name="weights_grad",
    )(turned, grad_turned, hidden, pre, *before)


def middle_kernel(back_a, back_b, mid_ref, grad_ref, gain, full_ref, short_ref, sums_ref):
    unit, scale = norm(mid_ref[...])
    back = back_a[...] + back_b[...].astype(F32)
    grad = grad_ref[...].astype(F32)
    full = grad + norm_back(back * gain[...], unit, scale)
    full_ref[...] = full
    short_ref[...] = full.astype(BF)
    sums_ref[...] = jnp.zeros_like(sums_ref)
    sums_ref[0:1] = jnp.sum(back * unit, axis=0, keepdims=True)
    sums_ref[1:2] = jnp.sum(back, axis=0, keepdims=True)
    sums_ref[2:3] = jnp.sum(full, axis=0, keepdims=True)
    sums_ref[3:4] = jnp.sum(grad, axis=0, keepdims=True)


def middle(back_a, back_b, mid, grad, gain):
    n, d = mid.shape
    return pl.pallas_call(
        middle_kernel,
        in_specs=[VMEM] * 5,
        out_specs=[VMEM] * 3,
        out_shape=[
            jax.ShapeDtypeStruct((n, d), F32),
            jax.ShapeDtypeStruct((n, d), BF),
            jax.ShapeDtypeStruct((8, d), F32),
        ],
        compiler_params=pltpu.CompilerParams(vmem_limit_bytes=LIMIT),
        cost_estimate=COST,
        name="middle",
    )(back_a, back_b, mid, grad, gain)


def back_kernel(first_near, blocks, last_call, table, made_ref, key_ref, row_ref, total_ref, w_ref, short_a, short_b, *refs):
    if last_call:
        before_ref, dq_ref, out_ref, d_ref, p_ref, dp_ref, columns_ref, sum_ref = refs
        sum_ref[...] = before_ref[...]
    else:
        dq_ref, sum_ref, d_ref, p_ref, dp_ref, columns_ref = refs
        sum_ref[...] = jnp.zeros_like(sum_ref)
    key_columns(key_ref, columns_ref)
    scale = HEAD ** (-0.5)
    n = blocks * BLOCK
    for slot, short in enumerate((short_a, short_b)):
        d_ref[slot * n : (slot + 1) * n] = dot(short[...], w_ref[...]).astype(BF)

    @pl.loop(0, 2 * blocks)
    def _(step):
        here = pl.ds(pl.multiple_of(step * BLOCK, BLOCK), BLOCK)
        number, own, first, last = block_places(table, first_near, step, blocks)
        rows = pl.ds(own, BLOCK)
        q_all = split_heads(made_ref[rows, 0:128], made_ref[rows, 384:512], True)
        d_all = split_heads(d_ref[here, 128:256], d_ref[here, 0:128], False)
        row = row_ref[pl.ds(number, 1), :]
        totals = [total_ref[h : h + 1, here] for h in range(3)]

        def weigh(j, inners):
            start = pl.multiple_of(j * BLOCK, BLOCK)
            spot = pl.ds(start, BLOCK)
            bias = pair_bias(columns_ref, row, own, start)
            new, add_v = [], []
            for h in range(3):
                keys = made_ref[spot, 128:256] if h < 2 else made_ref[spot, 512:640]
                values = made_ref[spot, 256:384] if h < 2 else made_ref[spot, 384:512]
                p = jnp.exp(dot_t(keys, q_all[h]) + bias - totals[h])
                d_p = dot_t(values, d_all[h])
                p_ref[h, j] = p
                dp_ref[h, j] = d_p
                new.append(inners[h] + jnp.sum((p * d_p).reshape(BLOCK // 8, 8, BLOCK), axis=0))
                add_v.append(dot(p.astype(BF), d_all[h]))
            sum_ref[spot, 128:256] += add_v[0] + add_v[1]
            sum_ref[spot, 256:384] += add_v[2]
            return tuple(new)

        inners = lax.fori_loop(first, last, weigh, (jnp.zeros((8, BLOCK), F32),) * 3)
        inners = [jnp.sum(v, axis=0, keepdims=True) for v in inners]

        def turn(j, sums):
            spot = pl.ds(pl.multiple_of(j * BLOCK, BLOCK), BLOCK)
            pair_t, third_t = made_ref[spot, 128:256].T, made_ref[spot, 512:640].T
            turned = (pair_t[:HEAD], pair_t[HEAD:], third_t[:HEAD])
            new, add_k = [], []
            for h in range(3):
                d_s = (p_ref[h, j] * (dp_ref[h, j] - inners[h])).astype(BF)
                add_k.append(dot(d_s, q_all[h]))
                new.append(sums[h] + dot(turned[h], d_s))
            sum_ref[spot, 0:128] += add_k[0] + add_k[1]
            sum_ref[spot, 384:512] += add_k[2]
            return tuple(new)

        sums = lax.fori_loop(first, last, turn, (jnp.zeros((HEAD, BLOCK), F32),) * 3)
        two = jnp.concatenate([sums[0], sums[1]], axis=0).T.astype(BF) * jnp.asarray(scale, BF)
        one = jnp.concatenate([sums[2], jnp.zeros_like(sums[2])], axis=0).T.astype(BF) * jnp.asarray(scale, BF)
        dq_ref[here, :] = two
        sum_ref[rows, 256:384] += one.astype(F32)

    if last_call:
        out_ref[...] = sum_ref[...].astype(BF)


def attend_back(first_near, table, made, key, row, total, w, shorts, before):
    keys = made.shape[0]
    n = keys // 4
    last_call = before is not None
    operands = [table, made, key, row, total, w, *shorts] + ([before] if last_call else [])
    scores = pltpu.VMEM((3, keys // BLOCK, BLOCK, BLOCK), F32)
    scratch = [pltpu.VMEM((2 * n, 256), BF), scores, scores, pltpu.VMEM((keys, 128), jnp.int32)]
    if last_call:
        scratch.append(pltpu.VMEM((keys, 512), F32))
    return pl.pallas_call(
        functools.partial(back_kernel, first_near, n // BLOCK, last_call),
        in_specs=[SMEM] + [VMEM] * (len(operands) - 1),
        out_specs=[VMEM] * 2,
        out_shape=[
            jax.ShapeDtypeStruct((2 * n, 128), BF),
            jax.ShapeDtypeStruct((keys, 512), BF if last_call else F32),
        ],
        scratch_shapes=scratch,
        compiler_params=pltpu.CompilerParams(vmem_limit_bytes=LIMIT),
        cost_estimate=COST,
        name="attend_back",
    )(*operands)


def unit_back_kernel(table, dkv_ref, dq_a, dq_b, w_hbm, out_a, out_b, out_c, out_d, w_ref, sems):
    (going,) = stage([w_hbm], [w_ref], sems)
    going.wait()
    n = out_a.shape[0]
    for near, out in enumerate((out_a, out_b, out_c, out_d)):
        here = pl.ds(pl.multiple_of((table[0] ^ near) * n, n), n)
        dq = (dq_a, dq_b)[near // 2][near % 2 * n : (near % 2 + 1) * n]
        out[...] = (dot_t(dkv_ref[here, :], w_ref[:, 128:640]) + dot_t(dq, w_ref[:, 0:128])).astype(BF)


def unit_back(table, w, dqs, dkv):
    n, d = dqs[0].shape[0] // 2, w.shape[0]
    return pl.pallas_call(
        unit_back_kernel,
        in_specs=[SMEM] + [VMEM] * 3 + [HBM],
        out_specs=[VMEM] * 4,
        out_shape=[jax.ShapeDtypeStruct((n, d), BF)] * 4,
        scratch_shapes=buffers_of([w]),
        compiler_params=pltpu.CompilerParams(vmem_limit_bytes=LIMIT),
        cost_estimate=COST,
        name="unit_back",
    )(table, dkv, *dqs, w)


def grads_kernel(rows, base, table, dkv_ref, dq_a, dq_b, *refs):
    sources, refs = refs[:7], refs[7:]
    keep_ref, send_ref, column_ref, sum_ref, turned_ref, shorts, contexts, dqs, sems = refs
    n = shorts.shape[1]
    half = keep_ref.shape[0]
    targets = [dqs.at[: 2 * n], dqs.at[2 * n :], turned_ref, *[shorts.at[k] for k in range(4)]]
    targets += [contexts.at[: 2 * n], contexts.at[2 * n :]]
    for copy in stage((dq_a, dq_b, *sources), targets, sems):
        copy.wait()
    sum_ref[:, 128:640] = dot(turned_ref[...], dkv_ref[...])
    column_ref[:, 128:640] = jnp.sum(dkv_ref[...].astype(F32), axis=0, keepdims=True)
    column_ref[:, 0:128] = jnp.sum(dqs[...].astype(F32), axis=0, keepdims=True)
    sum_ref[:, 0:128] = jnp.zeros_like(sum_ref[:, 0:128])
    sum_ref[:, 640:768] = jnp.zeros_like(sum_ref[:, 640:768])

    @pl.loop(0, 4)
    def _(near):
        here = pl.ds(pl.multiple_of((table[0] ^ near) * n, n), n)
        own = pl.ds(pl.multiple_of(near * n, n), n)
        sum_ref[:, 0:128] += dot(turned_ref[:, here], dqs[own, :])
        out = t_dot(shorts[near], contexts[own, :])
        for k in range(out.shape[0] // rows):
            spot = pl.ds(pl.multiple_of(table[base + k], rows), rows)
            sum_ref[spot, 512:768] += out[k * rows : (k + 1) * rows]

    keep_ref[...] = sum_ref[:half, :].astype(BF)
    send_ref[...] = sum_ref[half:, :].astype(BF)


def grads(table, turned, dqs, dkv, shorts, contexts, rows, base):
    d = turned.shape[0]
    n = shorts[0].shape[0]
    return pl.pallas_call(
        functools.partial(grads_kernel, rows, base),
        in_specs=[SMEM] + [VMEM] * 3 + [HBM] * 7,
        out_specs=[VMEM] * 3,
        out_shape=[jax.ShapeDtypeStruct((d // 2, 768), BF)] * 2 + [jax.ShapeDtypeStruct((1, 640), F32)],
        scratch_shapes=[
            pltpu.VMEM((d, 768), F32),
            pltpu.VMEM(turned.shape, BF),
            pltpu.VMEM((4, n, d), BF),
            pltpu.VMEM((4 * n, 256), BF),
            pltpu.VMEM((4 * n, 128), BF),
            pltpu.SemaphoreType.DMA((9,)),
        ],
        compiler_params=pltpu.CompilerParams(vmem_limit_bytes=60 << 20),
        cost_estimate=COST,
        name="grads",
    )(table, dkv, *dqs, turned, *shorts, *contexts)


def final_kernel(one_ref, core_ref, two_ref, stream_ref, full_ref, gain, early_ref, col_a, col_b, col_one, grad_ref, sums_ref):
    step = pl.program_id(0)

    @pl.when(step == 0)
    def _():
        sums_ref[...] = jnp.zeros_like(sums_ref)
        sums_ref[3:7] = early_ref[0:4]
        sums_ref[7:8] = col_b[...]
        sums_ref[8:9] = col_a[...]
        sums_ref[9:10, : col_one.shape[1]] = col_one[...]

    back = one_ref[...].astype(F32) + core_ref[...].astype(F32) + two_ref[...].astype(F32)
    unit, scale = norm(stream_ref[...])
    grad = full_ref[...] + norm_back(back * gain[...], unit, scale)
    grad_ref[...] = grad
    sums_ref[0:1] += jnp.sum(back * unit, axis=0, keepdims=True)
    sums_ref[1:2] += jnp.sum(back, axis=0, keepdims=True)
    sums_ref[2:3] += jnp.sum(grad, axis=0, keepdims=True)


def small_call(kernel, shapes, limit=LIMIT):
    def call(*operands):
        return pl.pallas_call(
            kernel,
            in_specs=[VMEM] * len(operands),
            out_specs=[VMEM] * len(shapes),
            out_shape=[jax.ShapeDtypeStruct(shape, F32) for shape in shapes],
            compiler_params=pltpu.CompilerParams(vmem_limit_bytes=limit),
            cost_estimate=COST,
            name=getattr(kernel, "__name__", "finish"),
        )(*operands)

    return call


def core_sums(own, there, out):
    out[0:7] = own[0:7] + there[0:7]
    out[7:8] = own[8:9] + there[7:8]
    out[8:9] = own[9:10]
    out[9:16] = jnp.zeros_like(own[9:16])


def row_sums(own, there, seat, spread, out):
    dp = seat.shape[0]
    both = own[0:7] + there[0:7]
    out[0:2] = both[0:2]
    out[2:6] = both[3:7]
    out[6:8] = own[7:9]
    out[8 : 8 + dp] = seat[...] * both[2:3]
    out[8 + dp : 8 + dp + spread.shape[0]] = spread[...]


def finish_kernel(dp, features, columns, count, *refs):
    parts, (pick, gain_ref, bias_ref, query_ref, value_ref, up_ref, time_ref) = refs[:count], refs[count:]
    total = parts[0][...]
    for part in parts[1:]:
        total = total + part[...]
    by_sequence = total[8 : 8 + dp]
    gain_ref[0:1] = total[0:1]
    gain_ref[1:2] = total[2:3]
    bias_ref[0:1] = total[1:2]
    bias_ref[1:4] = total[3:6]
    bias_ref[4:5] = jnp.sum(by_sequence, axis=0, keepdims=True)
    up_ref[...] = total[6:7]
    query_ref[...] = jnp.concatenate([total[7:8, 0:128], total[7:8, 384:448]], axis=1)
    value_ref[...] = jnp.concatenate([total[7:8, 256:384], total[7:8, 448:512]], axis=1)
    wide = total.shape[1] // features
    rows = [total[8 + dp + k // wide : 9 + dp + k // wide, k % wide * features : (k % wide + 1) * features] for k in range(dp)]
    share = jnp.dot(by_sequence, pick[...], precision=highest, preferred_element_type=F32)
    time_ref[...] = lax.dot_general(
        jnp.concatenate(rows, axis=0), share, (((0,), (0,)), ((), ())), precision=highest, preferred_element_type=F32
    )


def final(one, core, two, stream, full, gain, early, cols, col_one):
    n, d = stream.shape
    rows = pl.BlockSpec((n // 4, d), lambda i: (i, 0))
    small = (gain, early, *cols, col_one)
    return pl.pallas_call(
        final_kernel,
        grid=(4,),
        in_specs=[rows] * 5 + [whole(v.shape) for v in small],
        out_specs=[rows, whole((16, d))],
        out_shape=[jax.ShapeDtypeStruct((n, d), F32), jax.ShapeDtypeStruct((16, d), F32)],
        compiler_params=params("arbitrary", limit=60 << 20),
        cost_estimate=COST,
        name="final",
    )(one, core, two, stream, full, *small)


def add_kernel(*refs):
    total = refs[0][...].astype(F32)
    for ref in refs[1:-1]:
        total = total + ref[...].astype(F32)
    refs[-1][...] = total.astype(refs[-1].dtype)


def low_sum(*terms, rows=None, dtype=BF):
    terms = [v if isinstance(v, tuple) else (v, 0) for v in terms]
    rows = rows or min(v.shape[0] for v, _ in terms)
    block = rows // (4 if rows % 64 == 0 else 1)
    width = terms[0][0].shape[1]
    return pl.pallas_call(
        add_kernel,
        grid=(rows // block,),
        in_specs=[
            pl.BlockSpec((block, width), functools.partial(lambda first, i: (i + first, 0), start // block))
            for _, start in terms
        ],
        out_specs=pl.BlockSpec((block, width), lambda i: (i, 0)),
        out_shape=jax.ShapeDtypeStruct((rows, width), dtype),
        compiler_params=params("arbitrary"),
        cost_estimate=COST,
        name="low_sum",
    )(*[v for v, _ in terms])


def stack_kernel(*refs):
    for k, ref in enumerate(refs[:-1]):
        refs[-1][k] = ref[...]


def stack(values):
    return pl.pallas_call(
        stack_kernel,
        in_specs=[VMEM] * len(values),
        out_specs=VMEM,
        out_shape=jax.ShapeDtypeStruct((len(values),) + values[0].shape, values[0].dtype),
        compiler_params=pltpu.CompilerParams(vmem_limit_bytes=LIMIT),
        cost_estimate=COST,
        name="stack",
    )(*values)


def tie(values, after):
    return lax.optimization_barrier((values, after))[0]


def line_sums(terms, starts, size, rows):
    found = [[(v, start + by * rows) for v, start in zip(terms, starts, strict=True)] for by in range(size)]
    return low_sum(*found[0], rows=rows, dtype=F32), [low_sum(*pairs, rows=rows) for pairs in found[1:]]


def along_line(sent, size):
    return [shift(v, "d1", size, by + 1) for by, v in enumerate(sent)]


def scatter_dp(value):
    return lax.psum_scatter(value, ("d1", "d0"), scatter_dimension=0, tiled=True).astype(F32)


def shards(
    inputs,
    segment_ids,
    keep_mask,
    timestep,
    w_qkv,
    b_query,
    b_value,
    w_out,
    w_up,
    b_up,
    w_down,
    time_weight,
    gains,
    row_biases,
    d_out,
):
    size = lax.axis_size("d1")
    long = size > 4
    z, x = lax.axis_index("d1"), lax.axis_index("d0")
    own = lax.axis_index("t1") * 2 + lax.axis_index("t0")
    n, d = inputs.shape
    dp = 2 * size
    place = z * 2 + x
    features = time_weight.shape[0]
    columns = time_weight.shape[1]

    rows = w_up.shape[0]
    blocks = 4 * n // BLOCK
    ids = segment_ids.reshape(blocks, BLOCK)
    first = jnp.sum(segment_ids[None, :] < ids[:, :1], axis=1, dtype=jnp.int32)
    last = jnp.sum(segment_ids[None, :] <= ids[:, -1:], axis=1, dtype=jnp.int32)
    span = jnp.stack([first // BLOCK, (last + BLOCK - 1) // BLOCK], axis=1).reshape(-1)
    slots = [(lax.rem(z - s + size, size) * 2 + (x ^ a)) * rows for a in range(2) for s in range(size)]
    places = [((k % 2 ^ x) * size + k // 2) * rows for k in range(dp)]
    slots_two = [(s * 2 + (x ^ a)) * rows for a in range(2) for s in range(size)]
    if long:
        nothing = [jnp.zeros_like(own)]
        slots, places, slots_two, turn_rows = nothing, nothing, nothing, d
    else:
        turn_rows = rows
    base = 1 + len(slots)
    slot_two = base + len(places)
    table_one = jnp.stack([own, *slots, *places, *slots_two]).astype(jnp.int32)
    table_two = jnp.concatenate([jnp.stack([own]), span]).astype(jnp.int32)
    key = jnp.where(keep_mask > 0, segment_ids, -1).reshape(blocks, BLOCK)
    own_keep = lax.dynamic_slice_in_dim(keep_mask, own * n, n, 0)[:, None]
    up_core = swap(b_up[None], "t0")
    grad_two, grad_turned = cotangent(table_one, d_out[None], own_keep, turn_rows, base)

    pack_one = jnp.concatenate(
        [pack_columns(w_qkv[0], w_qkv[1], w_qkv[2]), time_weight.T, pack_outer(w_out.T)], axis=1
    )
    rows = pack_one.shape[0]
    if long:
        half = lax.all_gather(pack_one, ("d1", "d0"), axis=0, tiled=True)
        pieces_one = [(half, None, 0)]
    else:
        line = [pack_one] + [shift(pack_one, "d1", size, by) for by in range(1, size)]
    x_core = swap(inputs, "t0")
    x_far_a = swap(inputs[: n // 2], "t1")
    if not long:
        half = stack(tie(line, (x_core, grad_two, grad_turned, key, x_far_a)))
        other_half = swap(half, "d0")
        pieces_one = [(half, (s, 0), s) for s in range(size)] + [(other_half, (s, 0), size + s) for s in range(size)]
    x_far_b = tie(swap(inputs[n // 2 :], "t1"), half)
    x_near = [inputs, x_core, x_far_a, x_far_b, swap(x_far_a, "t0"), swap(x_far_b, "t0")]
    time_rows = sinusoid(timestep, features).astype(BF)
    times = jnp.pad(time_rows, ((0, 7), (0, 0)))
    seat = (jnp.arange(dp) == place).astype(F32)[:, None]
    spread = (seat * time_rows.astype(F32)).reshape(1, -1)
    spread = jnp.pad(spread, ((0, 0), (0, -spread.shape[1] % d))).reshape(-1, d)
    bias_one = pack_columns(b_query, jnp.zeros_like(b_query), b_value)[None, :]

    scale = jnp.where(
        (jnp.arange(640) < 128) | ((jnp.arange(640) >= 384) & (jnp.arange(640) < 448)), HEAD ** (-0.5), 1.0
    ).astype(F32)[None, :]

    far_keep = lax.dynamic_slice_in_dim(keep_mask, (own ^ 2) * n, n, 0)[:, None]
    d_far = swap(tie(d_out, x_far_b), "t1")
    d_far = swap(tie(d_out, x_far_b), "t1")

    if long:
        gathered = lax.all_gather(jnp.stack([w_up, w_down.T]), ("d1", "d0"), axis=1, tiled=True)
        other = swap(gathered, "t0")
        feed_weights = [tuple([(v[k], None, 0)] for k in range(2)) for v in (gathered, other)]
        rows_two = d
    else:
        gathered = lax.all_gather(tie(jnp.concatenate([w_up, w_down.T]), half), "d1")
        x_near = tie(x_near, up_core)
    made, turned_one, stream_in, w_one, outer_own = project(
        x_near, times, row_biases[4:5], gains[0:1], row_biases[0:1], bias_one, scale, pieces_one, d if long else rows,
        table_one, turn_rows, base,
    )
    outer_near = gather_near(outer_own)
    made_near = made_far = made
    if not long:
        gathered = tie(gathered, made)
        gathered_side, gathered_core = swap(gathered, "d0"), swap(gathered, "t0")
    context_far, total_far = attend(2, table_two, made_far, key, ids)
    context_over = swap(context_far, "t1")
    if not long:
        made_near = tie(made, (d_far, gathered_core))
    context_near, total_near = attend(0, table_two, made_near, key, ids)
    grad_far, grad_turned_far = cotangent(table_one, tie(d_far, context_near)[None], far_keep, turn_rows, base)
    context_over = tie(context_over, grad_far if long else (grad_far, gathered_side))
    contexts = [context_near, swap(context_near, "t0"), context_over, swap(context_over, "t0")]
    if not long:
        def pieces_of(near, other, part):
            return [(v, (s, part), a * size + s) for a, v in enumerate((near, other)) for s in range(size)]

        pairs = ((gathered, gathered_side), (gathered_core, swap(gathered_side, "t0")))
        feed_weights = [tuple(pieces_of(*pair, part) for part in range(2)) for pair in pairs]
        rows_two = rows
    stream_mid, unit_two = outer(
        table_one, contexts, outer_near, stream_in, gains[1:2], row_biases[1:2], row_biases[2:3]
    )

    biases = jnp.concatenate([b_up[None], up_core], axis=1)
    block = d // 2 if long else rows
    unit_far = swap(unit_two, "t1")
    hidden, pre, out, back, turned_two, *feed_arrays = feed(
        table_one, unit_two, grad_two, biases, feed_weights, rows_two, turn_rows, base, slot_two, F32
    )
    own_grads = weights_grad(turned_two, grad_turned, hidden, pre, [], block)
    hidden_far, pre_far, out_far, back_far, turned_far = feed(
        table_one, tie(unit_far, own_grads), grad_far, biases, feed_arrays, rows_two, turn_rows, base, slot_two, BF
    )
    back_over = swap(back_far, "t1")
    part = d // 2
    keep_a, send_a, column_a, keep_b, send_b, column_b = weights_grad(turned_far, grad_turned_far, hidden_far, pre_far, own_grads, block)
    keep_b, send_b = to_core((keep_b, send_b))
    full, short, sums_two = middle(back, back_over, stream_mid, grad_two, gains[1:2])
    short_core, short_over = swap(short, "t0"), swap(short, "t1")
    send_b = tie(send_b, short)
    sent = low_sum(send_a, send_b)
    over = sent if long else swap(sent, "d0")
    shorts = tie([short, short_core], sent)
    dq_near, sum_near = attend_back(0, table_two, made, key, ids, total_near, outer_own, shorts, None)
    short_over = tie(short_over, sum_near)
    shorts = [short_over, swap(short_over, "t0")]
    short_near = [short, short_core] + shorts
    if long:
        kept = low_sum(keep_a, keep_b)
        up_share = scatter_dp(jnp.concatenate([kept[:part], sent[:part]]))
        down_share = scatter_dp(jnp.concatenate([kept[part:], sent[part:]]))
    dq_far, dkv = attend_back(2, table_two, made, key, ids, total_far, outer_own, shorts, sum_near)
    if not long:
        kept = low_sum(keep_a, keep_b, tie(over, dkv))
        both_share = lax.psum_scatter(kept, "d1", scatter_dimension=0, tiled=True)
        dkv = tie(dkv, kept)
    out_over, dkv = tie((swap(tie(out_far, short_over), "t1"), dkv), dkv)
    back_a, back_b, back_c, back_d = unit_back(table_one, w_one, [dq_near, dq_far], dkv)
    back_d, back_b = swap(back_d, "t0"), swap(back_b, "t0")
    back_far = low_sum(back_c, tie(back_d, back_b))
    other = swap(back_far, "t1")
    grad_keep, grad_send, column_one = grads(
        table_one, turned_one, tie([dq_near, dq_far], back_far), dkv, short_near, [context_near, context_far], turn_rows, base
    )
    if long:
        one_share = scatter_dp(jnp.concatenate([grad_keep, grad_send]))
    else:
        grad_over = swap(grad_send, "d0")
    grad_input, small = final(
        back_a, back_b, other, stream_in, full, gains[0:1], sums_two, (column_a, column_b), column_one
    )

    out_over = tie(out_over, small)
    output = (stream_mid + out + out_over.astype(F32) + row_biases[3]).astype(BF)

    if not long:
        one_sum = (grad_keep.astype(F32) + tie(grad_over, small).astype(F32)).astype(BF)
        one_share = lax.psum_scatter(one_sum, "d1", scatter_dimension=0, tiled=True).astype(F32)

    (small,) = small_call(core_sums, [(16, d)])(small, swap(small, "t0"))
    height = 8 + dp + spread.shape[0]
    (small,) = small_call(row_sums, [(height, d)])(small, swap(small, "t1"), seat, spread)
    small = small + swap(small, "d0")
    parts = [lax.psum(small, "d1")] if long else [small] + [shift(small, "d1", size, by) for by in range(1, size)]
    pick = (jnp.arange(d)[:, None] == place * columns + jnp.arange(columns)[None, :]).astype(F32)
    width = b_query.shape[0]
    gain_total, bias_total, column_query, column_value, up_bias, grad_time = small_call(
        functools.partial(finish_kernel, dp, features, columns, len(parts)),
        [(2, d), (5, d), (1, width), (1, width), (1, d), (features, columns)],
    )(*parts, pick)
    if not long:
        up_share, down_share = both_share[:rows].astype(F32), both_share[rows:].astype(F32)
    d_query, d_key, d_value, d_outer = unpack_columns(one_share)
    return (
        output,
        grad_input,
        jnp.stack([d_query, d_key, d_value]),
        column_query[0],
        column_value[0],
        d_outer.T,
        up_share,
        up_bias[0],
        down_share.T,
        grad_time,
        gain_total,
        bias_total,
    )


def solution(mesh):
    dp, tensor = mesh.shape["dp"], mesh.shape["tensor"]
    fine = Mesh(mesh.devices.reshape(dp // 2, 2, tensor // 2, 2), ("d1", "d0", "t1", "t0"))
    rows, cols = ("d1", "d0"), ("t1", "t0")
    every = rows + cols
    in_specs = (
        P(every, None),
        P(rows),
        P(rows),
        P(rows),
        P(None, rows, cols),
        P(cols),
        P(cols),
        P(cols, rows),
        P(rows, cols),
        P(cols),
        P(cols, rows),
        P(None, rows),
        P(),
        P(),
        P(every, None),
    )
    out_specs = (
        P(every, None),
        P(every, None),
        P(None, rows, cols),
        P(cols),
        P(cols),
        P(cols, rows),
        P(rows, cols),
        P(cols),
        P(cols, rows),
        P(None, rows),
        P(),
        P(),
    )
    return jax.shard_map(shards, mesh=fine, in_specs=in_specs, out_specs=out_specs, check_vma=False)
```

```python
import functools
import math

import jax
import jax.numpy as jnp
from jax import lax
from jax.experimental import pallas as pl
from jax.experimental.pallas import tpu as pltpu
from jax.sharding import Mesh
from jax.sharding import PartitionSpec as P

HEAD = 64
SEQ_LEN = 2048
BLOCK = 256
F32 = jnp.float32
BF = jnp.bfloat16

epsilon = 1e-05
masked = -1e30
highest = lax.Precision.HIGHEST

LIMIT = 32 << 20
COST = pl.CostEstimate(flops=10**5, bytes_accessed=10**5, transcendentals=0)


def dot(left, right):
    return jnp.dot(left, right, preferred_element_type=F32)


def dot_t(left, right):
    return lax.dot_general(left, right, (((1,), (1,)), ((), ())), preferred_element_type=F32)


def t_dot(left, right):
    return lax.dot_general(left, right, (((0,), (0,)), ((), ())), preferred_element_type=F32)


def params(*semantics, limit=LIMIT):
    return pltpu.CompilerParams(dimension_semantics=semantics, vmem_limit_bytes=limit)


def whole(shape):
    rank = len(shape)
    return pl.BlockSpec(shape, lambda *_: (0,) * rank)


def stage(sources, buffers, sems):
    going = [pltpu.make_async_copy(s, b, sems.at[k]) for k, (s, b) in enumerate(zip(sources, buffers, strict=True))]
    for copy in going:
        copy.start()
    return going


def buffers_of(values):
    return [pltpu.VMEM(v.shape, v.dtype) for v in values] + [pltpu.SemaphoreType.DMA((len(values),))]


def sinusoid(timesteps, features):
    half_width = features // 2
    frequency = jnp.exp(-math.log(10000.0) * jnp.arange(half_width, dtype=F32) / half_width)
    angles = timesteps.astype(F32)[:, None] * frequency[None, :]
    return jnp.concatenate([jnp.cos(angles), jnp.sin(angles)], axis=1)


def swap(value, axis):
    return lax.ppermute(value, axis, [(0, 1), (1, 0)])


def shift(value, axis, size, by):
    return lax.ppermute(value, axis, [(i, (i + by) % size) for i in range(size)])


def gather_near(value):
    far = swap(value, "t1")
    return [value, swap(value, "t0"), far, swap(far, "t0")]


def to_core(values):
    return [swap(v, "t0") for v in values]


def loader(pieces, rows, arrays):
    plan = []
    for value, lead, slot in pieces:
        for n, known in enumerate(arrays):
            if known is value:
                break
        else:
            n = len(arrays)
            arrays.append(value)
        plan.append((n, lead, slot))
    return plan


def copies(plan, rows, refs, target, base, table, sems):
    out = []
    for k, (n, lead, slot) in enumerate(plan):
        source = refs[n] if lead is None else refs[n].at[lead[0], pl.ds(lead[1] * rows, rows), :]
        if table is None:
            start = slot * rows
        else:
            start = pl.multiple_of(table[base + slot], rows)
        out.append(pltpu.make_async_copy(source, target.at[pl.ds(start, rows), :], sems.at[k]))
    return out


def norm(values):
    average = jnp.mean(values, axis=-1, keepdims=True)
    centered = values - average
    variance = jnp.mean(centered * centered, axis=-1, keepdims=True)
    scale = lax.rsqrt(variance + epsilon)
    return centered * scale, scale


def norm_back(gradient, unit, scale):
    one = jnp.mean(gradient, axis=-1, keepdims=True)
    two = jnp.mean(gradient * unit, axis=-1, keepdims=True)
    return scale * (gradient - one - unit * two)


def pack_columns(query, key, value):
    zeros = jnp.zeros_like(key[..., 128:])
    return jnp.concatenate(
        [query[..., :128], key[..., :128], value[..., :128], query[..., 128:], value[..., 128:], key[..., 128:], zeros],
        axis=-1,
    )


def pack_outer(out):
    return jnp.concatenate([jnp.zeros_like(out[..., 128:]), out[..., 128:], out[..., :128]], axis=-1)


def unpack_columns(pack):
    query = jnp.concatenate([pack[..., 0:128], pack[..., 384:448]], axis=-1)
    key = jnp.concatenate([pack[..., 128:256], pack[..., 512:576]], axis=-1)
    value = jnp.concatenate([pack[..., 256:384], pack[..., 448:512]], axis=-1)
    out = jnp.concatenate([pack[..., 640:768], pack[..., 576:640]], axis=-1)
    return query, key, value, out


VMEM = pl.BlockSpec(memory_space=pltpu.VMEM)
SMEM = pl.BlockSpec(memory_space=pltpu.SMEM)
HBM = pl.BlockSpec(memory_space=pltpu.HBM)


def put_turned(table, base, rows, value, target):
    for k in range(value.shape[0] // rows):
        here = pl.ds(pl.multiple_of(table[base + k], rows), rows)
        target[here, :] = value[k * rows : (k + 1) * rows]


def cotangent_kernel(rows, base, table, d_ref, keep_ref, grad_ref, turned_ref):
    value = d_ref[0]
    grad = jnp.where(keep_ref[...] > 0, value, jnp.zeros_like(value))
    grad_ref[...] = grad
    put_turned(table, base, rows, grad.T, turned_ref)


def cotangent(table, d_out, keep, rows, base):
    _, n, d = d_out.shape
    return pl.pallas_call(
        functools.partial(cotangent_kernel, rows, base),
        in_specs=[SMEM, VMEM, VMEM],
        out_specs=[VMEM, VMEM],
        out_shape=[jax.ShapeDtypeStruct((n, d), BF), jax.ShapeDtypeStruct((d, n), BF)],
        compiler_params=pltpu.CompilerParams(vmem_limit_bytes=LIMIT),
        cost_estimate=COST,
        name="cotangent",
    )(table, d_out, keep)


def project_kernel(plan, rows, turn_rows, base, table, *refs):
    sources, (times, add, gain, low_shift, bias, scale), refs = refs[:6], refs[6:12], refs[12:]
    count = len({n for n, _, _ in plan})
    pieces, (made_ref, turned_ref, stream_ref, w_out_ref, outer_ref, w_ref, embed_ref, sems, x_all, stage_sems) = refs[:count], refs[count:]
    near = pl.program_id(0)
    part = x_all.shape[1] // 2

    @pl.when(near == 0)
    def _():
        todo = copies(plan, rows, pieces, w_ref, 1, table, sems)
        for copy in todo:
            copy.start()
        targets = [x_all.at[0], x_all.at[1], x_all.at[2, :part], x_all.at[2, part:], x_all.at[3, :part], x_all.at[3, part:]]
        for copy in todo + stage(sources, targets, stage_sems):
            copy.wait()
        w_out_ref[...] = w_ref[:, 0:640]
        outer_ref[...] = w_ref[:, 768:1024]
        embed_ref[...] = dot_t(times[...], w_ref[:, 640:768]) + add[...]

    stream = x_all[near].astype(F32) + embed_ref[0:1]

    @pl.when(near == 0)
    def _():
        stream_ref[...] = stream

    unit, _ = norm(stream)
    low = (unit * gain[...] + low_shift[...]).astype(BF)
    made_ref[...] = ((dot(low, w_ref[:, :640]) + bias[...]) * scale[...]).astype(BF)
    put_turned(table, base, turn_rows, low.T, turned_ref)


def project(x_near, times, add, gain, low_shift, bias, scale, pieces, rows, table, turn_rows, base):
    n, d = x_near[0].shape
    arrays = []
    plan = loader(pieces, rows, arrays)
    small = (times, add, gain, low_shift, bias, scale)
    grid_spec = pltpu.PrefetchScalarGridSpec(
        num_scalar_prefetch=1,
        grid=(4,),
        in_specs=[HBM] * 6 + [whole(v.shape) for v in small] + [pl.BlockSpec(memory_space=pl.ANY)] * len(arrays),
        out_specs=[
            pl.BlockSpec((n, 640), lambda i, t: (t[0] ^ i, 0)),
            pl.BlockSpec((d, n), lambda i, t: (0, t[0] ^ i)),
            whole((n, d)),
            whole((d, 640)),
            whole((d, 256)),
        ],
        scratch_shapes=[
            pltpu.VMEM((d, 1024), BF),
            pltpu.VMEM((8, d), F32),
            pltpu.SemaphoreType.DMA((len(plan),)),
            pltpu.VMEM((4, n, d), BF),
            pltpu.SemaphoreType.DMA((6,)),
        ],
    )
    return pl.pallas_call(
        functools.partial(project_kernel, plan, rows, turn_rows, base),
        grid_spec=grid_spec,
        out_shape=[
            jax.ShapeDtypeStruct((4 * n, 640), BF),
            jax.ShapeDtypeStruct((d, 4 * n), BF),
            jax.ShapeDtypeStruct((n, d), F32),
            jax.ShapeDtypeStruct((d, 640), BF),
            jax.ShapeDtypeStruct((d, 256), BF),
        ],
        compiler_params=params("arbitrary", limit=60 << 20),
        cost_estimate=COST,
        name="project",
    )(table, *x_near, *small, *arrays)


def low_half(shape):
    return lax.broadcasted_iota(jnp.int32, shape, 1) < HEAD


def key_columns(key_ref, columns_ref):
    for j in range(key_ref.shape[0]):
        row = jnp.broadcast_to(key_ref[j : j + 1, :], (128, BLOCK))
        columns_ref[j * BLOCK : (j + 1) * BLOCK, :] = row.T


def pair_bias(columns_ref, row, own, start):
    key = columns_ref[pl.ds(start, BLOCK), :]
    gap = lax.broadcasted_iota(jnp.int32, key.shape, 0) - lax.broadcasted_iota(jnp.int32, key.shape, 1)
    sides = []
    for side in range(BLOCK // 128):
        same = (key == row[:, side * 128 : (side + 1) * 128]) | (gap == own - start + side * 128)
        sides.append(jnp.where(same, 0.0, masked))
    return jnp.concatenate(sides, axis=1)


def block_places(table, first_near, step, blocks):
    number = (table[0] ^ (first_near + step // blocks)) * blocks + step % blocks
    return number, pl.multiple_of(number * BLOCK, BLOCK), table[1 + 2 * number], table[2 + 2 * number]


def split_heads(pair, third, third_low):
    half = low_half(pair.shape)
    zero = jnp.zeros_like(pair)
    last = jnp.where(half, third, zero) if third_low else jnp.where(half, zero, third)
    return jnp.where(half, pair, zero), jnp.where(half, zero, pair), last


def attend_kernel(first_near, blocks, table, made_ref, key_ref, row_ref, context_ref, total_ref, score_ref, columns_ref):
    key_columns(key_ref, columns_ref)

    @pl.loop(0, 2 * blocks)
    def _(step):
        here = pl.ds(pl.multiple_of(step * BLOCK, BLOCK), BLOCK)
        number, own, first, last = block_places(table, first_near, step, blocks)
        rows = pl.ds(own, BLOCK)
        q_all = split_heads(made_ref[rows, 0:128], made_ref[rows, 384:512], True)
        row = row_ref[pl.ds(number, 1), :]

        def score(j, tops):
            start = pl.multiple_of(j * BLOCK, BLOCK)
            spot = pl.ds(start, BLOCK)
            bias = pair_bias(columns_ref, row, own, start)
            out = []
            for h in range(3):
                keys = made_ref[spot, 128:256] if h < 2 else made_ref[spot, 512:640]
                s = dot_t(keys, q_all[h]) + bias
                score_ref[h, j] = s
                out.append(jnp.maximum(tops[h], jnp.max(s.reshape(BLOCK // 8, 8, BLOCK), axis=0)))
            return tuple(out)

        begin = jnp.full((8, BLOCK), masked, F32)
        tops = lax.fori_loop(first, last, score, (begin,) * 3)
        tops = [jnp.max(t, axis=0, keepdims=True) for t in tops]

        def weigh(j, carry):
            spot = pl.ds(pl.multiple_of(j * BLOCK, BLOCK), BLOCK)
            pair_t = made_ref[spot, 256:384].T
            third_t = made_ref[spot, 384:512].T
            values = (pair_t[:HEAD], pair_t[HEAD:], third_t[HEAD:])
            sums, totals = carry
            new_sums, new_totals = [], []
            for h in range(3):
                p = jnp.exp(score_ref[h, j] - tops[h])
                new_totals.append(totals[h] + jnp.sum(p.reshape(BLOCK // 8, 8, BLOCK), axis=0))
                new_sums.append(sums[h] + dot(values[h], p.astype(BF)))
            return tuple(new_sums), tuple(new_totals)

        zeros = (jnp.zeros((HEAD, BLOCK), F32),) * 3
        sums, totals = lax.fori_loop(first, last, weigh, (zeros, (jnp.zeros((8, BLOCK), F32),) * 3))
        done = []
        for h in range(3):
            total = jnp.sum(totals[h], axis=0, keepdims=True)
            done.append(sums[h] / total)
            total_ref[h : h + 1, here] = tops[h] + jnp.log(total)
        context_ref[here, 0:128] = jnp.concatenate([jnp.zeros_like(done[2]), done[2]], axis=0).T.astype(BF)
        context_ref[here, 128:256] = jnp.concatenate([done[0], done[1]], axis=0).T.astype(BF)


def attend(first_near, table, made, key, row):
    keys = made.shape[0]
    n = keys // 4
    blocks = n // BLOCK
    return pl.pallas_call(
        functools.partial(attend_kernel, first_near, blocks),
        in_specs=[SMEM] + [VMEM] * 3,
        out_specs=[VMEM] * 2,
        out_shape=[jax.ShapeDtypeStruct((2 * n, 256), BF), jax.ShapeDtypeStruct((8, 2 * n), F32)],
        scratch_shapes=[pltpu.VMEM((3, keys // BLOCK, BLOCK, BLOCK), F32), pltpu.VMEM((keys, 128), jnp.int32)],
        compiler_params=pltpu.CompilerParams(vmem_limit_bytes=LIMIT),
        cost_estimate=COST,
        name="attend",
    )(table, made, key, row)


def outer_kernel(table, *refs):
    sources, (gain, low_shift, add, mid_ref, unit_ref, *buffers, sems) = refs[:9], refs[9:]
    going = stage(sources, buffers, sems)
    contexts, stream_ref = buffers[:4], buffers[8]
    for copy in going:
        copy.wait()
    mid = stream_ref[...] + add[...]
    n = stream_ref.shape[0]
    contexts = [context.at[k % 2 * n : (k % 2 + 1) * n] for k, context in enumerate(contexts)]
    for near, context in enumerate(contexts):
        mid = mid + dot_t(context[...], buffers[4 + near][...])
    mid_ref[...] = mid
    unit, _ = norm(mid)
    unit_ref[...] = (unit * gain[...] + low_shift[...]).astype(BF)


def outer(table, contexts, weights, stream, gain, low_shift, add):
    n, d = stream.shape
    staged = [*contexts, *weights, stream]
    return pl.pallas_call(
        outer_kernel,
        in_specs=[SMEM] + [HBM] * 9 + [VMEM] * 3,
        out_specs=[VMEM, VMEM],
        out_shape=[jax.ShapeDtypeStruct((n, d), F32), jax.ShapeDtypeStruct((n, d), BF)],
        scratch_shapes=buffers_of(staged),
        compiler_params=pltpu.CompilerParams(vmem_limit_bytes=60 << 20),
        cost_estimate=COST,
        name="outer",
    )(table, *staged, gain, low_shift, add)


CHUNK = 256


def feed_kernel(plans, rows, turn_rows, base, first_slot, table, unit_ref, grad_ref, bias, *refs):
    if plans is None:
        (w_up, w_down), refs = refs[:2], refs[2:]
        hidden_ref, pre_ref, out_ref, back_ref, turned_ref = refs
    else:
        hidden_ref, pre_ref, out_ref, back_ref, turned_ref, w_up, w_down, sems = refs[-8:]
        pieces = refs[:-8]
        todo = []
        for group in range(2):
            batch = []
            for k, target in enumerate((w_up, w_down)):
                batch += copies(plans[group][k], rows, pieces, target.at[group], first_slot, table, sems.at[group, k])
            for copy in batch:
                copy.start()
            todo.append(batch)
    width = w_up.shape[2]
    each = width // CHUNK
    put_turned(table, base, turn_rows, unit_ref[...].T, turned_ref)

    for step in range(2 * each):
        group = step // each
        if plans is not None and step % each == 0:
            for copy in todo[group]:
                copy.wait()
        here = slice(step % each * CHUNK, (step % each + 1) * CHUNK)
        there = slice(step * CHUNK, (step + 1) * CHUNK)
        pre = dot(unit_ref[...], w_up[group, :, here]) + bias[:, there]
        d_hidden = dot(grad_ref[...], w_down[group, :, here])
        share = 0.5 + 0.5 * lax.erf(pre * math.sqrt(0.5))
        hidden_ref[:, there] = (pre * share).astype(BF)
        slope = share + pre * (jnp.exp(-0.5 * pre * pre) * (1.0 / math.sqrt(2.0 * math.pi)))
        pre_ref[:, there] = (d_hidden * slope).astype(BF)

    for target, values, weights in ((out_ref, hidden_ref, w_down), (back_ref, pre_ref, w_up)):
        made = dot_t(values[:, :width], weights[0]) + dot_t(values[:, width:], weights[1])
        target[...] = made.astype(target.dtype)


def feed(table, unit, grad, bias, weights, rows, turn_rows, base, first_slot, dtype):
    n, d = unit.shape
    width = bias.shape[-1] // 2
    made = [
        jax.ShapeDtypeStruct((n, 2 * width), BF),
        jax.ShapeDtypeStruct((n, 2 * width), BF),
        jax.ShapeDtypeStruct((n, d), dtype),
        jax.ShapeDtypeStruct((n, d), dtype),
        jax.ShapeDtypeStruct((d, n), BF),
    ]
    if isinstance(weights[0], tuple):
        arrays = []
        plans = [[loader(pieces, rows, arrays) for pieces in group] for group in weights]
        specs = [pl.BlockSpec(memory_space=pl.ANY)] * len(arrays)
        made += [jax.ShapeDtypeStruct((2, d, width), BF)] * 2
        scratch = [pltpu.SemaphoreType.DMA((2, 2, len(plans[0][0])))]
    else:
        arrays, plans, specs, scratch = list(weights), None, [VMEM, VMEM], []
    return pl.pallas_call(
        functools.partial(feed_kernel, plans, rows, turn_rows, base, first_slot),
        in_specs=[SMEM] + [VMEM] * 3 + specs,
        out_specs=[VMEM] * len(made),
        out_shape=made,
        scratch_shapes=scratch,
        compiler_params=pltpu.CompilerParams(vmem_limit_bytes=LIMIT),
        cost_estimate=COST,
        name="feed",
    )(table, unit, grad, bias, *arrays)


def weights_kernel(last, block, turned, grad, hidden, pre, *refs):
    before, refs = (refs[:6], refs[6:]) if last else (None, refs)
    half = refs[0].shape[0] // 2
    width = refs[0].shape[1]
    for group in (1, 0):
        outs = refs[3 * group : 3 * group + 3]
        olds = before[3 * group : 3 * group + 3] if last else None

        @pl.loop(0, width // CHUNK)
        def _(step, group=group, outs=outs, olds=olds):
            here = pl.ds(pl.multiple_of(step * CHUNK, CHUNK), CHUNK)
            there = pl.ds(pl.multiple_of(group * width + step * CHUNK, CHUNK), CHUNK)
            made = (dot(turned[...], pre[:, there]), dot(grad[...], hidden[:, there]))
            for side in range(2):
                for k in range(2 * half // block):
                    rows = slice(k * block, (k + 1) * block)
                    start = side * half + k // 2 * block
                    part = made[k % 2][start : start + block]
                    if last:
                        part = part + olds[side][rows, here].astype(F32)
                    outs[side][rows, here] = part.astype(BF)
            column = jnp.sum(pre[:, there].astype(F32), axis=0, keepdims=True)
            outs[2][:, here] = column + olds[2][:, here] if last else column


def weights_grad(turned, grad_turned, hidden, pre, before, block):
    d = turned.shape[0]
    width = hidden.shape[1] // 2
    made = [jax.ShapeDtypeStruct((d, width), BF)] * 2 + [jax.ShapeDtypeStruct((1, width), F32)]
    return pl.pallas_call(
        functools.partial(weights_kernel, bool(before), block),
        in_specs=[VMEM] * (4 + len(before)),
        out_specs=[VMEM] * 6,
        out_shape=made * 2,
        input_output_aliases={4 + k: k for k in range(len(before))},
        compiler_params=pltpu.CompilerParams(vmem_limit_bytes=LIMIT),
        cost_estimate=COST,
        name="weights_grad",
    )(turned, grad_turned, hidden, pre, *before)


def middle_kernel(back_a, back_b, mid_ref, grad_ref, gain, full_ref, short_ref, sums_ref):
    unit, scale = norm(mid_ref[...])
    back = back_a[...] + back_b[...].astype(F32)
    grad = grad_ref[...].astype(F32)
    full = grad + norm_back(back * gain[...], unit, scale)
    full_ref[...] = full
    short_ref[...] = full.astype(BF)
    sums_ref[...] = jnp.zeros_like(sums_ref)
    sums_ref[0:1] = jnp.sum(back * unit, axis=0, keepdims=True)
    sums_ref[1:2] = jnp.sum(back, axis=0, keepdims=True)
    sums_ref[2:3] = jnp.sum(full, axis=0, keepdims=True)
    sums_ref[3:4] = jnp.sum(grad, axis=0, keepdims=True)


def middle(back_a, back_b, mid, grad, gain):
    n, d = mid.shape
    return pl.pallas_call(
        middle_kernel,
        in_specs=[VMEM] * 5,
        out_specs=[VMEM] * 3,
        out_shape=[
            jax.ShapeDtypeStruct((n, d), F32),
            jax.ShapeDtypeStruct((n, d), BF),
            jax.ShapeDtypeStruct((8, d), F32),
        ],
        compiler_params=pltpu.CompilerParams(vmem_limit_bytes=LIMIT),
        cost_estimate=COST,
        name="middle",
    )(back_a, back_b, mid, grad, gain)


def back_kernel(first_near, blocks, last_call, table, made_ref, key_ref, row_ref, total_ref, w_ref, short_a, short_b, *refs):
    if last_call:
        before_ref, dq_ref, out_ref, d_ref, p_ref, dp_ref, columns_ref, sum_ref = refs
        sum_ref[...] = before_ref[...]
    else:
        dq_ref, sum_ref, d_ref, p_ref, dp_ref, columns_ref = refs
        sum_ref[...] = jnp.zeros_like(sum_ref)
    key_columns(key_ref, columns_ref)
    scale = HEAD ** (-0.5)
    n = blocks * BLOCK
    for slot, short in enumerate((short_a, short_b)):
        d_ref[slot * n : (slot + 1) * n] = dot(short[...], w_ref[...]).astype(BF)

    @pl.loop(0, 2 * blocks)
    def _(step):
        here = pl.ds(pl.multiple_of(step * BLOCK, BLOCK), BLOCK)
        number, own, first, last = block_places(table, first_near, step, blocks)
        rows = pl.ds(own, BLOCK)
        q_all = split_heads(made_ref[rows, 0:128], made_ref[rows, 384:512], True)
        d_all = split_heads(d_ref[here, 128:256], d_ref[here, 0:128], False)
        row = row_ref[pl.ds(number, 1), :]
        totals = [total_ref[h : h + 1, here] for h in range(3)]

        def weigh(j, inners):
            start = pl.multiple_of(j * BLOCK, BLOCK)
            spot = pl.ds(start, BLOCK)
            bias = pair_bias(columns_ref, row, own, start)
            new, add_v = [], []
            for h in range(3):
                keys = made_ref[spot, 128:256] if h < 2 else made_ref[spot, 512:640]
                values = made_ref[spot, 256:384] if h < 2 else made_ref[spot, 384:512]
                p = jnp.exp(dot_t(keys, q_all[h]) + bias - totals[h])
                d_p = dot_t(values, d_all[h])
                p_ref[h, j] = p
                dp_ref[h, j] = d_p
                new.append(inners[h] + jnp.sum((p * d_p).reshape(BLOCK // 8, 8, BLOCK), axis=0))
                add_v.append(dot(p.astype(BF), d_all[h]))
            sum_ref[spot, 128:256] += add_v[0] + add_v[1]
            sum_ref[spot, 256:384] += add_v[2]
            return tuple(new)

        inners = lax.fori_loop(first, last, weigh, (jnp.zeros((8, BLOCK), F32),) * 3)
        inners = [jnp.sum(v, axis=0, keepdims=True) for v in inners]

        def turn(j, sums):
            spot = pl.ds(pl.multiple_of(j * BLOCK, BLOCK), BLOCK)
            pair_t, third_t = made_ref[spot, 128:256].T, made_ref[spot, 512:640].T
            turned = (pair_t[:HEAD], pair_t[HEAD:], third_t[:HEAD])
            new, add_k = [], []
            for h in range(3):
                d_s = (p_ref[h, j] * (dp_ref[h, j] - inners[h])).astype(BF)
                add_k.append(dot(d_s, q_all[h]))
                new.append(sums[h] + dot(turned[h], d_s))
            sum_ref[spot, 0:128] += add_k[0] + add_k[1]
            sum_ref[spot, 384:512] += add_k[2]
            return tuple(new)

        sums = lax.fori_loop(first, last, turn, (jnp.zeros((HEAD, BLOCK), F32),) * 3)
        two = jnp.concatenate([sums[0], sums[1]], axis=0).T.astype(BF) * jnp.asarray(scale, BF)
        one = jnp.concatenate([sums[2], jnp.zeros_like(sums[2])], axis=0).T.astype(BF) * jnp.asarray(scale, BF)
        dq_ref[here, :] = two
        sum_ref[rows, 256:384] += one.astype(F32)

    if last_call:
        out_ref[...] = sum_ref[...].astype(BF)


def attend_back(first_near, table, made, key, row, total, w, shorts, before):
    keys = made.shape[0]
    n = keys // 4
    last_call = before is not None
    operands = [table, made, key, row, total, w, *shorts] + ([before] if last_call else [])
    scores = pltpu.VMEM((3, keys // BLOCK, BLOCK, BLOCK), F32)
    scratch = [pltpu.VMEM((2 * n, 256), BF), scores, scores, pltpu.VMEM((keys, 128), jnp.int32)]
    if last_call:
        scratch.append(pltpu.VMEM((keys, 512), F32))
    return pl.pallas_call(
        functools.partial(back_kernel, first_near, n // BLOCK, last_call),
        in_specs=[SMEM] + [VMEM] * (len(operands) - 1),
        out_specs=[VMEM] * 2,
        out_shape=[
            jax.ShapeDtypeStruct((2 * n, 128), BF),
            jax.ShapeDtypeStruct((keys, 512), BF if last_call else F32),
        ],
        scratch_shapes=scratch,
        compiler_params=pltpu.CompilerParams(vmem_limit_bytes=LIMIT),
        cost_estimate=COST,
        name="attend_back",
    )(*operands)


def unit_back_kernel(table, dkv_ref, dq_a, dq_b, w_hbm, out_a, out_b, out_c, out_d, w_ref, sems):
    (going,) = stage([w_hbm], [w_ref], sems)
    going.wait()
    n = out_a.shape[0]
    for near, out in enumerate((out_a, out_b, out_c, out_d)):
        here = pl.ds(pl.multiple_of((table[0] ^ near) * n, n), n)
        dq = (dq_a, dq_b)[near // 2][near % 2 * n : (near % 2 + 1) * n]
        out[...] = (dot_t(dkv_ref[here, :], w_ref[:, 128:640]) + dot_t(dq, w_ref[:, 0:128])).astype(BF)


def unit_back(table, w, dqs, dkv):
    n, d = dqs[0].shape[0] // 2, w.shape[0]
    return pl.pallas_call(
        unit_back_kernel,
        in_specs=[SMEM] + [VMEM] * 3 + [HBM],
        out_specs=[VMEM] * 4,
        out_shape=[jax.ShapeDtypeStruct((n, d), BF)] * 4,
        scratch_shapes=buffers_of([w]),
        compiler_params=pltpu.CompilerParams(vmem_limit_bytes=LIMIT),
        cost_estimate=COST,
        name="unit_back",
    )(table, dkv, *dqs, w)


def grads_kernel(rows, base, table, dkv_ref, dq_a, dq_b, *refs):
    sources, refs = refs[:7], refs[7:]
    keep_ref, send_ref, column_ref, sum_ref, turned_ref, shorts, contexts, dqs, sems = refs
    n = shorts.shape[1]
    half = keep_ref.shape[0]
    targets = [dqs.at[: 2 * n], dqs.at[2 * n :], turned_ref, *[shorts.at[k] for k in range(4)]]
    targets += [contexts.at[: 2 * n], contexts.at[2 * n :]]
    for copy in stage((dq_a, dq_b, *sources), targets, sems):
        copy.wait()
    sum_ref[:, 128:640] = dot(turned_ref[...], dkv_ref[...])
    column_ref[:, 128:640] = jnp.sum(dkv_ref[...].astype(F32), axis=0, keepdims=True)
    column_ref[:, 0:128] = jnp.sum(dqs[...].astype(F32), axis=0, keepdims=True)
    sum_ref[:, 0:128] = jnp.zeros_like(sum_ref[:, 0:128])
    sum_ref[:, 640:768] = jnp.zeros_like(sum_ref[:, 640:768])

    @pl.loop(0, 4)
    def _(near):
        here = pl.ds(pl.multiple_of((table[0] ^ near) * n, n), n)
        own = pl.ds(pl.multiple_of(near * n, n), n)
        sum_ref[:, 0:128] += dot(turned_ref[:, here], dqs[own, :])
        out = t_dot(shorts[near], contexts[own, :])
        for k in range(out.shape[0] // rows):
            spot = pl.ds(pl.multiple_of(table[base + k], rows), rows)
            sum_ref[spot, 512:768] += out[k * rows : (k + 1) * rows]

    keep_ref[...] = sum_ref[:half, :].astype(BF)
    send_ref[...] = sum_ref[half:, :].astype(BF)


def grads(table, turned, dqs, dkv, shorts, contexts, rows, base):
    d = turned.shape[0]
    n = shorts[0].shape[0]
    return pl.pallas_call(
        functools.partial(grads_kernel, rows, base),
        in_specs=[SMEM] + [VMEM] * 3 + [HBM] * 7,
        out_specs=[VMEM] * 3,
        out_shape=[jax.ShapeDtypeStruct((d // 2, 768), BF)] * 2 + [jax.ShapeDtypeStruct((1, 640), F32)],
        scratch_shapes=[
            pltpu.VMEM((d, 768), F32),
            pltpu.VMEM(turned.shape, BF),
            pltpu.VMEM((4, n, d), BF),
            pltpu.VMEM((4 * n, 256), BF),
            pltpu.VMEM((4 * n, 128), BF),
            pltpu.SemaphoreType.DMA((9,)),
        ],
        compiler_params=pltpu.CompilerParams(vmem_limit_bytes=60 << 20),
        cost_estimate=COST,
        name="grads",
    )(table, dkv, *dqs, turned, *shorts, *contexts)


def final_kernel(one_ref, core_ref, two_ref, stream_ref, full_ref, gain, early_ref, col_a, col_b, col_one, grad_ref, sums_ref):
    step = pl.program_id(0)

    @pl.when(step == 0)
    def _():
        sums_ref[...] = jnp.zeros_like(sums_ref)
        sums_ref[3:7] = early_ref[0:4]
        sums_ref[7:8] = col_b[...]
        sums_ref[8:9] = col_a[...]
        sums_ref[9:10, : col_one.shape[1]] = col_one[...]

    back = one_ref[...].astype(F32) + core_ref[...].astype(F32) + two_ref[...].astype(F32)
    unit, scale = norm(stream_ref[...])
    grad = full_ref[...] + norm_back(back * gain[...], unit, scale)
    grad_ref[...] = grad
    sums_ref[0:1] += jnp.sum(back * unit, axis=0, keepdims=True)
    sums_ref[1:2] += jnp.sum(back, axis=0, keepdims=True)
    sums_ref[2:3] += jnp.sum(grad, axis=0, keepdims=True)


def small_call(kernel, shapes, limit=LIMIT):
    def call(*operands):
        return pl.pallas_call(
            kernel,
            in_specs=[VMEM] * len(operands),
            out_specs=[VMEM] * len(shapes),
            out_shape=[jax.ShapeDtypeStruct(shape, F32) for shape in shapes],
            compiler_params=pltpu.CompilerParams(vmem_limit_bytes=limit),
            cost_estimate=COST,
            name=getattr(kernel, "__name__", "finish"),
        )(*operands)

    return call


def core_sums(own, there, out):
    out[0:7] = own[0:7] + there[0:7]
    out[7:8] = own[8:9] + there[7:8]
    out[8:9] = own[9:10]
    out[9:16] = jnp.zeros_like(own[9:16])


def row_sums(own, there, seat, spread, out):
    dp = seat.shape[0]
    both = own[0:7] + there[0:7]
    out[0:2] = both[0:2]
    out[2:6] = both[3:7]
    out[6:8] = own[7:9]
    out[8 : 8 + dp] = seat[...] * both[2:3]
    out[8 + dp : 8 + dp + spread.shape[0]] = spread[...]


def finish_kernel(dp, features, columns, count, *refs):
    parts, (pick, gain_ref, bias_ref, query_ref, value_ref, up_ref, time_ref) = refs[:count], refs[count:]
    total = parts[0][...]
    for part in parts[1:]:
        total = total + part[...]
    by_sequence = total[8 : 8 + dp]
    gain_ref[0:1] = total[0:1]
    gain_ref[1:2] = total[2:3]
    bias_ref[0:1] = total[1:2]
    bias_ref[1:4] = total[3:6]
    bias_ref[4:5] = jnp.sum(by_sequence, axis=0, keepdims=True)
    up_ref[...] = total[6:7]
    query_ref[...] = jnp.concatenate([total[7:8, 0:128], total[7:8, 384:448]], axis=1)
    value_ref[...] = jnp.concatenate([total[7:8, 256:384], total[7:8, 448:512]], axis=1)
    wide = total.shape[1] // features
    rows = [total[8 + dp + k // wide : 9 + dp + k // wide, k % wide * features : (k % wide + 1) * features] for k in range(dp)]
    share = jnp.dot(by_sequence, pick[...], precision=highest, preferred_element_type=F32)
    time_ref[...] = lax.dot_general(
        jnp.concatenate(rows, axis=0), share, (((0,), (0,)), ((), ())), precision=highest, preferred_element_type=F32
    )


def final(one, core, two, stream, full, gain, early, cols, col_one):
    n, d = stream.shape
    rows = pl.BlockSpec((n // 4, d), lambda i: (i, 0))
    small = (gain, early, *cols, col_one)
    return pl.pallas_call(
        final_kernel,
        grid=(4,),
        in_specs=[rows] * 5 + [whole(v.shape) for v in small],
        out_specs=[rows, whole((16, d))],
        out_shape=[jax.ShapeDtypeStruct((n, d), F32), jax.ShapeDtypeStruct((16, d), F32)],
        compiler_params=params("arbitrary", limit=60 << 20),
        cost_estimate=COST,
        name="final",
    )(one, core, two, stream, full, *small)


def add_kernel(*refs):
    total = refs[0][...].astype(F32)
    for ref in refs[1:-1]:
        total = total + ref[...].astype(F32)
    refs[-1][...] = total.astype(refs[-1].dtype)


def low_sum(*terms, rows=None, dtype=BF):
    terms = [v if isinstance(v, tuple) else (v, 0) for v in terms]
    rows = rows or min(v.shape[0] for v, _ in terms)
    block = rows // (4 if rows % 64 == 0 else 1)
    width = terms[0][0].shape[1]
    return pl.pallas_call(
        add_kernel,
        grid=(rows // block,),
        in_specs=[
            pl.BlockSpec((block, width), functools.partial(lambda first, i: (i + first, 0), start // block))
            for _, start in terms
        ],
        out_specs=pl.BlockSpec((block, width), lambda i: (i, 0)),
        out_shape=jax.ShapeDtypeStruct((rows, width), dtype),
        compiler_params=params("arbitrary"),
        cost_estimate=COST,
        name="low_sum",
    )(*[v for v, _ in terms])


def stack_kernel(*refs):
    for k, ref in enumerate(refs[:-1]):
        refs[-1][k] = ref[...]


def stack(values):
    return pl.pallas_call(
        stack_kernel,
        in_specs=[VMEM] * len(values),
        out_specs=VMEM,
        out_shape=jax.ShapeDtypeStruct((len(values),) + values[0].shape, values[0].dtype),
        compiler_params=pltpu.CompilerParams(vmem_limit_bytes=LIMIT),
        cost_estimate=COST,
        name="stack",
    )(*values)


def tie(values, after):
    return lax.optimization_barrier((values, after))[0]


def line_sums(terms, starts, size, rows):
    found = [[(v, start + by * rows) for v, start in zip(terms, starts, strict=True)] for by in range(size)]
    return low_sum(*found[0], rows=rows, dtype=F32), [low_sum(*pairs, rows=rows) for pairs in found[1:]]


def along_line(sent, size):
    return [shift(v, "d1", size, by + 1) for by, v in enumerate(sent)]


def scatter_dp(value):
    return lax.psum_scatter(value, ("d1", "d0"), scatter_dimension=0, tiled=True).astype(F32)


def shards(
    inputs,
    segment_ids,
    keep_mask,
    timestep,
    w_qkv,
    b_query,
    b_value,
    w_out,
    w_up,
    b_up,
    w_down,
    time_weight,
    gains,
    row_biases,
    d_out,
):
    size = lax.axis_size("d1")
    long = size > 4
    z, x = lax.axis_index("d1"), lax.axis_index("d0")
    own = lax.axis_index("t1") * 2 + lax.axis_index("t0")
    n, d = inputs.shape
    dp = 2 * size
    place = z * 2 + x
    features = time_weight.shape[0]
    columns = time_weight.shape[1]

    rows = w_up.shape[0]
    blocks = 4 * n // BLOCK
    ids = segment_ids.reshape(blocks, BLOCK)
    first = jnp.sum(segment_ids[None, :] < ids[:, :1], axis=1, dtype=jnp.int32)
    last = jnp.sum(segment_ids[None, :] <= ids[:, -1:], axis=1, dtype=jnp.int32)
    span = jnp.stack([first // BLOCK, (last + BLOCK - 1) // BLOCK], axis=1).reshape(-1)
    slots = [(lax.rem(z - s + size, size) * 2 + (x ^ a)) * rows for a in range(2) for s in range(size)]
    places = [((k % 2 ^ x) * size + k // 2) * rows for k in range(dp)]
    slots_two = [(s * 2 + (x ^ a)) * rows for a in range(2) for s in range(size)]
    if long:
        nothing = [jnp.zeros_like(own)]
        slots, places, slots_two, turn_rows = nothing, nothing, nothing, d
    else:
        turn_rows = rows
    base = 1 + len(slots)
    slot_two = base + len(places)
    table_one = jnp.stack([own, *slots, *places, *slots_two]).astype(jnp.int32)
    table_two = jnp.concatenate([jnp.stack([own]), span]).astype(jnp.int32)
    key = jnp.where(keep_mask > 0, segment_ids, -1).reshape(blocks, BLOCK)
    own_keep = lax.dynamic_slice_in_dim(keep_mask, own * n, n, 0)[:, None]
    up_core = swap(b_up[None], "t0")
    grad_two, grad_turned = cotangent(table_one, d_out[None], own_keep, turn_rows, base)

    pack_one = jnp.concatenate(
        [pack_columns(w_qkv[0], w_qkv[1], w_qkv[2]), time_weight.T, pack_outer(w_out.T)], axis=1
    )
    rows = pack_one.shape[0]
    if long:
        half = lax.all_gather(pack_one, ("d1", "d0"), axis=0, tiled=True)
        pieces_one = [(half, None, 0)]
    else:
        line = [pack_one] + [shift(pack_one, "d1", size, by) for by in range(1, size)]
    x_core = swap(inputs, "t0")
    x_far_a = swap(inputs[: n // 2], "t1")
    if not long:
        half = stack(tie(line, (x_core, grad_two, grad_turned, key, x_far_a)))
        other_half = swap(half, "d0")
        pieces_one = [(half, (s, 0), s) for s in range(size)] + [(other_half, (s, 0), size + s) for s in range(size)]
    x_far_b = tie(swap(inputs[n // 2 :], "t1"), half)
    x_near = [inputs, x_core, x_far_a, x_far_b, swap(x_far_a, "t0"), swap(x_far_b, "t0")]
    time_rows = sinusoid(timestep, features).astype(BF)
    times = jnp.pad(time_rows, ((0, 7), (0, 0)))
    seat = (jnp.arange(dp) == place).astype(F32)[:, None]
    spread = (seat * time_rows.astype(F32)).reshape(1, -1)
    spread = jnp.pad(spread, ((0, 0), (0, -spread.shape[1] % d))).reshape(-1, d)
    bias_one = pack_columns(b_query, jnp.zeros_like(b_query), b_value)[None, :]

    scale = jnp.where(
        (jnp.arange(640) < 128) | ((jnp.arange(640) >= 384) & (jnp.arange(640) < 448)), HEAD ** (-0.5), 1.0
    ).astype(F32)[None, :]

    far_keep = lax.dynamic_slice_in_dim(keep_mask, (own ^ 2) * n, n, 0)[:, None]
    d_far = swap(tie(d_out, x_far_b), "t1")
    d_far = swap(tie(d_out, x_far_b), "t1")

    if long:
        gathered = lax.all_gather(jnp.stack([w_up, w_down.T]), ("d1", "d0"), axis=1, tiled=True)
        other = swap(gathered, "t0")
        feed_weights = [tuple([(v[k], None, 0)] for k in range(2)) for v in (gathered, other)]
        rows_two = d
    else:
        gathered = lax.all_gather(tie(jnp.concatenate([w_up, w_down.T]), half), "d1")
        x_near = tie(x_near, up_core)
    made, turned_one, stream_in, w_one, outer_own = project(
        x_near, times, row_biases[4:5], gains[0:1], row_biases[0:1], bias_one, scale, pieces_one, d if long else rows,
        table_one, turn_rows, base,
    )
    outer_near = gather_near(outer_own)
    made_near = made_far = made
    if not long:
        gathered = tie(gathered, made)
        gathered_side, gathered_core = swap(gathered, "d0"), swap(gathered, "t0")
    context_far, total_far = attend(2, table_two, made_far, key, ids)
    context_over = swap(context_far, "t1")
    if not long:
        made_near = tie(made, (d_far, gathered_core))
    context_near, total_near = attend(0, table_two, made_near, key, ids)
    grad_far, grad_turned_far = cotangent(table_one, tie(d_far, context_near)[None], far_keep, turn_rows, base)
    context_over = tie(context_over, grad_far if long else (grad_far, gathered_side))
    contexts = [context_near, swap(context_near, "t0"), context_over, swap(context_over, "t0")]
    if not long:
        def pieces_of(near, other, part):
            return [(v, (s, part), a * size + s) for a, v in enumerate((near, other)) for s in range(size)]

        pairs = ((gathered, gathered_side), (gathered_core, swap(gathered_side, "t0")))
        feed_weights = [tuple(pieces_of(*pair, part) for part in range(2)) for pair in pairs]
        rows_two = rows
    stream_mid, unit_two = outer(
        table_one, contexts, outer_near, stream_in, gains[1:2], row_biases[1:2], row_biases[2:3]
    )

    biases = jnp.concatenate([b_up[None], up_core], axis=1)
    block = d // 2 if long else rows
    unit_far = swap(unit_two, "t1")
    hidden, pre, out, back, turned_two, *feed_arrays = feed(
        table_one, unit_two, grad_two, biases, feed_weights, rows_two, turn_rows, base, slot_two, F32
    )
    own_grads = weights_grad(turned_two, grad_turned, hidden, pre, [], block)
    hidden_far, pre_far, out_far, back_far, turned_far = feed(
        table_one, tie(unit_far, own_grads), grad_far, biases, feed_arrays, rows_two, turn_rows, base, slot_two, BF
    )
    back_over = swap(back_far, "t1")
    part = d // 2
    keep_a, send_a, column_a, keep_b, send_b, column_b = weights_grad(turned_far, grad_turned_far, hidden_far, pre_far, own_grads, block)
    keep_b, send_b = to_core((keep_b, send_b))
    full, short, sums_two = middle(back, back_over, stream_mid, grad_two, gains[1:2])
    short_core, short_over = swap(short, "t0"), swap(short, "t1")
    send_b = tie(send_b, short)
    sent = low_sum(send_a, send_b)
    over = sent if long else swap(sent, "d0")
    shorts = tie([short, short_core], sent)
    dq_near, sum_near = attend_back(0, table_two, made, key, ids, total_near, outer_own, shorts, None)
    short_over = tie(short_over, sum_near)
    shorts = [short_over, swap(short_over, "t0")]
    short_near = [short, short_core] + shorts
    if long:
        kept = low_sum(keep_a, keep_b)
        up_share = scatter_dp(jnp.concatenate([kept[:part], sent[:part]]))
        down_share = scatter_dp(jnp.concatenate([kept[part:], sent[part:]]))
    dq_far, dkv = attend_back(2, table_two, made, key, ids, total_far, outer_own, shorts, sum_near)
    if not long:
        kept = low_sum(keep_a, keep_b, tie(over, dkv))
        both_share = lax.psum_scatter(kept, "d1", scatter_dimension=0, tiled=True)
        dkv = tie(dkv, kept)
    out_over, dkv = tie((swap(tie(out_far, short_over), "t1"), dkv), dkv)
    back_a, back_b, back_c, back_d = unit_back(table_one, w_one, [dq_near, dq_far], dkv)
    back_d, back_b = swap(back_d, "t0"), swap(back_b, "t0")
    back_far = low_sum(back_c, back_d)
    other = swap(back_far, "t1")
    grad_keep, grad_send, column_one = grads(
        table_one, turned_one, tie([dq_near, dq_far], back_far), dkv, short_near, [context_near, context_far], turn_rows, base
    )
    if long:
        one_share = scatter_dp(jnp.concatenate([grad_keep, grad_send]))
    else:
        grad_over = swap(grad_send, "d0")
    grad_input, small = final(
        back_a, back_b, other, stream_in, full, gains[0:1], sums_two, (column_a, column_b), column_one
    )

    out_over = tie(out_over, small)
    output = (stream_mid + out + out_over.astype(F32) + row_biases[3]).astype(BF)

    if not long:
        one_sum = (grad_keep.astype(F32) + tie(grad_over, small).astype(F32)).astype(BF)
        one_share = lax.psum_scatter(one_sum, "d1", scatter_dimension=0, tiled=True).astype(F32)

    (small,) = small_call(core_sums, [(16, d)])(small, swap(small, "t0"))
    height = 8 + dp + spread.shape[0]
    (small,) = small_call(row_sums, [(height, d)])(small, swap(small, "t1"), seat, spread)
    small = small + swap(small, "d0")
    parts = [lax.psum(small, "d1")] if long else [small] + [shift(small, "d1", size, by) for by in range(1, size)]
    pick = (jnp.arange(d)[:, None] == place * columns + jnp.arange(columns)[None, :]).astype(F32)
    width = b_query.shape[0]
    gain_total, bias_total, column_query, column_value, up_bias, grad_time = small_call(
        functools.partial(finish_kernel, dp, features, columns, len(parts)),
        [(2, d), (5, d), (1, width), (1, width), (1, d), (features, columns)],
    )(*parts, pick)
    if not long:
        up_share, down_share = both_share[:rows].astype(F32), both_share[rows:].astype(F32)
    d_query, d_key, d_value, d_outer = unpack_columns(one_share)
    return (
        output,
        grad_input,
        jnp.stack([d_query, d_key, d_value]),
        column_query[0],
        column_value[0],
        d_outer.T,
        up_share,
        up_bias[0],
        down_share.T,
        grad_time,
        gain_total,
        bias_total,
    )


def solution(mesh):
    dp, tensor = mesh.shape["dp"], mesh.shape["tensor"]
    fine = Mesh(mesh.devices.reshape(dp // 2, 2, tensor // 2, 2), ("d1", "d0", "t1", "t0"))
    rows, cols = ("d1", "d0"), ("t1", "t0")
    every = rows + cols
    in_specs = (
        P(every, None),
        P(rows),
        P(rows),
        P(rows),
        P(None, rows, cols),
        P(cols),
        P(cols),
        P(cols, rows),
        P(rows, cols),
        P(cols),
        P(cols, rows),
        P(None, rows),
        P(),
        P(),
        P(every, None),
    )
    out_specs = (
        P(every, None),
        P(every, None),
        P(None, rows, cols),
        P(cols),
        P(cols),
        P(cols, rows),
        P(rows, cols),
        P(cols),
        P(cols, rows),
        P(None, rows),
        P(),
        P(),
    )
    return jax.shard_map(shards, mesh=fine, in_specs=in_specs, out_specs=out_specs, check_vma=False)
```

```python
import functools
import math

import jax
import jax.numpy as jnp
from jax import lax
from jax.experimental import pallas as pl
from jax.experimental.pallas import tpu as pltpu
from jax.sharding import Mesh
from jax.sharding import PartitionSpec as P

HEAD = 64
SEQ_LEN = 2048
BLOCK = 256
F32 = jnp.float32
BF = jnp.bfloat16

epsilon = 1e-05
masked = -1e30
highest = lax.Precision.HIGHEST

LIMIT = 32 << 20
COST = pl.CostEstimate(flops=10**5, bytes_accessed=10**5, transcendentals=0)


def dot(left, right):
    return jnp.dot(left, right, preferred_element_type=F32)


def dot_t(left, right):
    return lax.dot_general(left, right, (((1,), (1,)), ((), ())), preferred_element_type=F32)


def t_dot(left, right):
    return lax.dot_general(left, right, (((0,), (0,)), ((), ())), preferred_element_type=F32)


def params(*semantics, limit=LIMIT):
    return pltpu.CompilerParams(dimension_semantics=semantics, vmem_limit_bytes=limit)


def whole(shape):
    rank = len(shape)
    return pl.BlockSpec(shape, lambda *_: (0,) * rank)


def stage(sources, buffers, sems):
    going = [pltpu.make_async_copy(s, b, sems.at[k]) for k, (s, b) in enumerate(zip(sources, buffers, strict=True))]
    for copy in going:
        copy.start()
    return going


def buffers_of(values):
    return [pltpu.VMEM(v.shape, v.dtype) for v in values] + [pltpu.SemaphoreType.DMA((len(values),))]


def sinusoid(timesteps, features):
    half_width = features // 2
    frequency = jnp.exp(-math.log(10000.0) * jnp.arange(half_width, dtype=F32) / half_width)
    angles = timesteps.astype(F32)[:, None] * frequency[None, :]
    return jnp.concatenate([jnp.cos(angles), jnp.sin(angles)], axis=1)


def swap(value, axis):
    return lax.ppermute(value, axis, [(0, 1), (1, 0)])


def shift(value, axis, size, by):
    return lax.ppermute(value, axis, [(i, (i + by) % size) for i in range(size)])


def gather_near(value):
    far = swap(value, "t1")
    return [value, swap(value, "t0"), far, swap(far, "t0")]


def to_core(values):
    return [swap(v, "t0") for v in values]


def loader(pieces, rows, arrays):
    plan = []
    for value, lead, slot in pieces:
        for n, known in enumerate(arrays):
            if known is value:
                break
        else:
            n = len(arrays)
            arrays.append(value)
        plan.append((n, lead, slot))
    return plan


def copies(plan, rows, refs, target, base, table, sems):
    out = []
    for k, (n, lead, slot) in enumerate(plan):
        source = refs[n] if lead is None else refs[n].at[lead[0], pl.ds(lead[1] * rows, rows), :]
        if table is None:
            start = slot * rows
        else:
            start = pl.multiple_of(table[base + slot], rows)
        out.append(pltpu.make_async_copy(source, target.at[pl.ds(start, rows), :], sems.at[k]))
    return out


def norm(values):
    average = jnp.mean(values, axis=-1, keepdims=True)
    centered = values - average
    variance = jnp.mean(centered * centered, axis=-1, keepdims=True)
    scale = lax.rsqrt(variance + epsilon)
    return centered * scale, scale


def norm_back(gradient, unit, scale):
    one = jnp.mean(gradient, axis=-1, keepdims=True)
    two = jnp.mean(gradient * unit, axis=-1, keepdims=True)
    return scale * (gradient - one - unit * two)


def pack_columns(query, key, value):
    zeros = jnp.zeros_like(key[..., 128:])
    return jnp.concatenate(
        [query[..., :128], key[..., :128], value[..., :128], query[..., 128:], value[..., 128:], key[..., 128:], zeros],
        axis=-1,
    )


def pack_outer(out):
    return jnp.concatenate([jnp.zeros_like(out[..., 128:]), out[..., 128:], out[..., :128]], axis=-1)


def unpack_columns(pack):
    query = jnp.concatenate([pack[..., 0:128], pack[..., 384:448]], axis=-1)
    key = jnp.concatenate([pack[..., 128:256], pack[..., 512:576]], axis=-1)
    value = jnp.concatenate([pack[..., 256:384], pack[..., 448:512]], axis=-1)
    out = jnp.concatenate([pack[..., 640:768], pack[..., 576:640]], axis=-1)
    return query, key, value, out


VMEM = pl.BlockSpec(memory_space=pltpu.VMEM)
SMEM = pl.BlockSpec(memory_space=pltpu.SMEM)
HBM = pl.BlockSpec(memory_space=pltpu.HBM)


def put_turned(table, base, rows, value, target):
    for k in range(value.shape[0] // rows):
        here = pl.ds(pl.multiple_of(table[base + k], rows), rows)
        target[here, :] = value[k * rows : (k + 1) * rows]


def cotangent_kernel(rows, base, table, d_ref, keep_ref, grad_ref, turned_ref):
    value = d_ref[0]
    grad = jnp.where(keep_ref[...] > 0, value, jnp.zeros_like(value))
    grad_ref[...] = grad
    put_turned(table, base, rows, grad.T, turned_ref)


def cotangent(table, d_out, keep, rows, base):
    _, n, d = d_out.shape
    return pl.pallas_call(
        functools.partial(cotangent_kernel, rows, base),
        in_specs=[SMEM, VMEM, VMEM],
        out_specs=[VMEM, VMEM],
        out_shape=[jax.ShapeDtypeStruct((n, d), BF), jax.ShapeDtypeStruct((d, n), BF)],
        compiler_params=pltpu.CompilerParams(vmem_limit_bytes=LIMIT),
        cost_estimate=COST,
        name="cotangent",
    )(table, d_out, keep)


def project_kernel(plan, rows, turn_rows, base, table, *refs):
    sources, (times, add, gain, low_shift, bias, scale), refs = refs[:6], refs[6:12], refs[12:]
    count = len({n for n, _, _ in plan})
    pieces, (made_ref, turned_ref, stream_ref, w_out_ref, outer_ref, w_ref, embed_ref, sems, x_all, stage_sems) = refs[:count], refs[count:]
    near = pl.program_id(0)
    part = x_all.shape[1] // 2

    @pl.when(near == 0)
    def _():
        todo = copies(plan, rows, pieces, w_ref, 1, table, sems)
        for copy in todo:
            copy.start()
        targets = [x_all.at[0], x_all.at[1], x_all.at[2, :part], x_all.at[2, part:], x_all.at[3, :part], x_all.at[3, part:]]
        for copy in todo + stage(sources, targets, stage_sems):
            copy.wait()
        w_out_ref[...] = w_ref[:, 0:640]
        outer_ref[...] = w_ref[:, 768:1024]
        embed_ref[...] = dot_t(times[...], w_ref[:, 640:768]) + add[...]

    stream = x_all[near].astype(F32) + embed_ref[0:1]

    @pl.when(near == 0)
    def _():
        stream_ref[...] = stream

    unit, _ = norm(stream)
    low = (unit * gain[...] + low_shift[...]).astype(BF)
    made_ref[...] = ((dot(low, w_ref[:, :640]) + bias[...]) * scale[...]).astype(BF)
    put_turned(table, base, turn_rows, low.T, turned_ref)


def project(x_near, times, add, gain, low_shift, bias, scale, pieces, rows, table, turn_rows, base):
    n, d = x_near[0].shape
    arrays = []
    plan = loader(pieces, rows, arrays)
    small = (times, add, gain, low_shift, bias, scale)
    grid_spec = pltpu.PrefetchScalarGridSpec(
        num_scalar_prefetch=1,
        grid=(4,),
        in_specs=[HBM] * 6 + [whole(v.shape) for v in small] + [pl.BlockSpec(memory_space=pl.ANY)] * len(arrays),
        out_specs=[
            pl.BlockSpec((n, 640), lambda i, t: (t[0] ^ i, 0)),
            pl.BlockSpec((d, n), lambda i, t: (0, t[0] ^ i)),
            whole((n, d)),
            whole((d, 640)),
            whole((d, 256)),
        ],
        scratch_shapes=[
            pltpu.VMEM((d, 1024), BF),
            pltpu.VMEM((8, d), F32),
            pltpu.SemaphoreType.DMA((len(plan),)),
            pltpu.VMEM((4, n, d), BF),
            pltpu.SemaphoreType.DMA((6,)),
        ],
    )
    return pl.pallas_call(
        functools.partial(project_kernel, plan, rows, turn_rows, base),
        grid_spec=grid_spec,
        out_shape=[
            jax.ShapeDtypeStruct((4 * n, 640), BF),
            jax.ShapeDtypeStruct((d, 4 * n), BF),
            jax.ShapeDtypeStruct((n, d), F32),
            jax.ShapeDtypeStruct((d, 640), BF),
            jax.ShapeDtypeStruct((d, 256), BF),
        ],
        compiler_params=params("arbitrary", limit=60 << 20),
        cost_estimate=COST,
        name="project",
    )(table, *x_near, *small, *arrays)


def low_half(shape):
    return lax.broadcasted_iota(jnp.int32, shape, 1) < HEAD


def key_columns(key_ref, columns_ref):
    for j in range(key_ref.shape[0]):
        row = jnp.broadcast_to(key_ref[j : j + 1, :], (128, BLOCK))
        columns_ref[j * BLOCK : (j + 1) * BLOCK, :] = row.T


def pair_bias(columns_ref, row, own, start):
    key = columns_ref[pl.ds(start, BLOCK), :]
    gap = lax.broadcasted_iota(jnp.int32, key.shape, 0) - lax.broadcasted_iota(jnp.int32, key.shape, 1)
    sides = []
    for side in range(BLOCK // 128):
        same = (key == row[:, side * 128 : (side + 1) * 128]) | (gap == own - start + side * 128)
        sides.append(jnp.where(same, 0.0, masked))
    return jnp.concatenate(sides, axis=1)


def block_places(table, first_near, step, blocks):
    number = (table[0] ^ (first_near + step // blocks)) * blocks + step % blocks
    return number, pl.multiple_of(number * BLOCK, BLOCK), table[1 + 2 * number], table[2 + 2 * number]


def split_heads(pair, third, third_low):
    half = low_half(pair.shape)
    zero = jnp.zeros_like(pair)
    last = jnp.where(half, third, zero) if third_low else jnp.where(half, zero, third)
    return jnp.where(half, pair, zero), jnp.where(half, zero, pair), last


def attend_kernel(first_near, blocks, table, made_ref, key_ref, row_ref, context_ref, total_ref, score_ref, columns_ref):
    key_columns(key_ref, columns_ref)

    @pl.loop(0, 2 * blocks)
    def _(step):
        here = pl.ds(pl.multiple_of(step * BLOCK, BLOCK), BLOCK)
        number, own, first, last = block_places(table, first_near, step, blocks)
        rows = pl.ds(own, BLOCK)
        q_all = split_heads(made_ref[rows, 0:128], made_ref[rows, 384:512], True)
        row = row_ref[pl.ds(number, 1), :]

        def score(j, tops):
            start = pl.multiple_of(j * BLOCK, BLOCK)
            spot = pl.ds(start, BLOCK)
            bias = pair_bias(columns_ref, row, own, start)
            out = []
            for h in range(3):
                keys = made_ref[spot, 128:256] if h < 2 else made_ref[spot, 512:640]
                s = dot_t(keys, q_all[h]) + bias
                score_ref[h, j] = s
                out.append(jnp.maximum(tops[h], jnp.max(s.reshape(BLOCK // 8, 8, BLOCK), axis=0)))
            return tuple(out)

        begin = jnp.full((8, BLOCK), masked, F32)
        tops = lax.fori_loop(first, last, score, (begin,) * 3)
        tops = [jnp.max(t, axis=0, keepdims=True) for t in tops]

        def weigh(j, carry):
            spot = pl.ds(pl.multiple_of(j * BLOCK, BLOCK), BLOCK)
            pair_t = made_ref[spot, 256:384].T
            third_t = made_ref[spot, 384:512].T
            values = (pair_t[:HEAD], pair_t[HEAD:], third_t[HEAD:])
            sums, totals = carry
            new_sums, new_totals = [], []
            for h in range(3):
                p = jnp.exp(score_ref[h, j] - tops[h])
                new_totals.append(totals[h] + jnp.sum(p.reshape(BLOCK // 8, 8, BLOCK), axis=0))
                new_sums.append(sums[h] + dot(values[h], p.astype(BF)))
            return tuple(new_sums), tuple(new_totals)

        zeros = (jnp.zeros((HEAD, BLOCK), F32),) * 3
        sums, totals = lax.fori_loop(first, last, weigh, (zeros, (jnp.zeros((8, BLOCK), F32),) * 3))
        done = []
        for h in range(3):
            total = jnp.sum(totals[h], axis=0, keepdims=True)
            done.append(sums[h] / total)
            total_ref[h : h + 1, here] = tops[h] + jnp.log(total)
        context_ref[here, 0:128] = jnp.concatenate([jnp.zeros_like(done[2]), done[2]], axis=0).T.astype(BF)
        context_ref[here, 128:256] = jnp.concatenate([done[0], done[1]], axis=0).T.astype(BF)


def attend(first_near, table, made, key, row):
    keys = made.shape[0]
    n = keys // 4
    blocks = n // BLOCK
    return pl.pallas_call(
        functools.partial(attend_kernel, first_near, blocks),
        in_specs=[SMEM] + [VMEM] * 3,
        out_specs=[VMEM] * 2,
        out_shape=[jax.ShapeDtypeStruct((2 * n, 256), BF), jax.ShapeDtypeStruct((8, 2 * n), F32)],
        scratch_shapes=[pltpu.VMEM((3, keys // BLOCK, BLOCK, BLOCK), F32), pltpu.VMEM((keys, 128), jnp.int32)],
        compiler_params=pltpu.CompilerParams(vmem_limit_bytes=LIMIT),
        cost_estimate=COST,
        name="attend",
    )(table, made, key, row)


def outer_kernel(table, *refs):
    sources, (gain, low_shift, add, mid_ref, unit_ref, *buffers, sems) = refs[:9], refs[9:]
    going = stage(sources, buffers, sems)
    contexts, stream_ref = buffers[:4], buffers[8]
    for copy in going:
        copy.wait()
    mid = stream_ref[...] + add[...]
    n = stream_ref.shape[0]
    contexts = [context.at[k % 2 * n : (k % 2 + 1) * n] for k, context in enumerate(contexts)]
    for near, context in enumerate(contexts):
        mid = mid + dot_t(context[...], buffers[4 + near][...])
    mid_ref[...] = mid
    unit, _ = norm(mid)
    unit_ref[...] = (unit * gain[...] + low_shift[...]).astype(BF)


def outer(table, contexts, weights, stream, gain, low_shift, add):
    n, d = stream.shape
    staged = [*contexts, *weights, stream]
    return pl.pallas_call(
        outer_kernel,
        in_specs=[SMEM] + [HBM] * 9 + [VMEM] * 3,
        out_specs=[VMEM, VMEM],
        out_shape=[jax.ShapeDtypeStruct((n, d), F32), jax.ShapeDtypeStruct((n, d), BF)],
        scratch_shapes=buffers_of(staged),
        compiler_params=pltpu.CompilerParams(vmem_limit_bytes=60 << 20),
        cost_estimate=COST,
        name="outer",
    )(table, *staged, gain, low_shift, add)


CHUNK = 256


def feed_kernel(plans, rows, turn_rows, base, first_slot, table, unit_ref, grad_ref, bias, *refs):
    if plans is None:
        (w_up, w_down), refs = refs[:2], refs[2:]
        hidden_ref, pre_ref, out_ref, back_ref, turned_ref = refs
    else:
        hidden_ref, pre_ref, out_ref, back_ref, turned_ref, w_up, w_down, sems = refs[-8:]
        pieces = refs[:-8]
        todo = []
        for group in range(2):
            batch = []
            for k, target in enumerate((w_up, w_down)):
                batch += copies(plans[group][k], rows, pieces, target.at[group], first_slot, table, sems.at[group, k])
            for copy in batch:
                copy.start()
            todo.append(batch)
    width = w_up.shape[2]
    each = width // CHUNK
    put_turned(table, base, turn_rows, unit_ref[...].T, turned_ref)

    for step in range(2 * each):
        group = step // each
        if plans is not None and step % each == 0:
            for copy in todo[group]:
                copy.wait()
        here = slice(step % each * CHUNK, (step % each + 1) * CHUNK)
        there = slice(step * CHUNK, (step + 1) * CHUNK)
        pre = dot(unit_ref[...], w_up[group, :, here]) + bias[:, there]
        d_hidden = dot(grad_ref[...], w_down[group, :, here])
        share = 0.5 + 0.5 * lax.erf(pre * math.sqrt(0.5))
        hidden_ref[:, there] = (pre * share).astype(BF)
        slope = share + pre * (jnp.exp(-0.5 * pre * pre) * (1.0 / math.sqrt(2.0 * math.pi)))
        pre_ref[:, there] = (d_hidden * slope).astype(BF)

    for target, values, weights in ((out_ref, hidden_ref, w_down), (back_ref, pre_ref, w_up)):
        made = dot_t(values[:, :width], weights[0]) + dot_t(values[:, width:], weights[1])
        target[...] = made.astype(target.dtype)


def feed(table, unit, grad, bias, weights, rows, turn_rows, base, first_slot, dtype):
    n, d = unit.shape
    width = bias.shape[-1] // 2
    made = [
        jax.ShapeDtypeStruct((n, 2 * width), BF),
        jax.ShapeDtypeStruct((n, 2 * width), BF),
        jax.ShapeDtypeStruct((n, d), dtype),
        jax.ShapeDtypeStruct((n, d), dtype),
        jax.ShapeDtypeStruct((d, n), BF),
    ]
    if isinstance(weights[0], tuple):
        arrays = []
        plans = [[loader(pieces, rows, arrays) for pieces in group] for group in weights]
        specs = [pl.BlockSpec(memory_space=pl.ANY)] * len(arrays)
        made += [jax.ShapeDtypeStruct((2, d, width), BF)] * 2
        scratch = [pltpu.SemaphoreType.DMA((2, 2, len(plans[0][0])))]
    else:
        arrays, plans, specs, scratch = list(weights), None, [VMEM, VMEM], []
    return pl.pallas_call(
        functools.partial(feed_kernel, plans, rows, turn_rows, base, first_slot),
        in_specs=[SMEM] + [VMEM] * 3 + specs,
        out_specs=[VMEM] * len(made),
        out_shape=made,
        scratch_shapes=scratch,
        compiler_params=pltpu.CompilerParams(vmem_limit_bytes=LIMIT),
        cost_estimate=COST,
        name="feed",
    )(table, unit, grad, bias, *arrays)


def weights_kernel(last, block, turned, grad, hidden, pre, *refs):
    before, refs = (refs[:6], refs[6:]) if last else (None, refs)
    half = refs[0].shape[0] // 2
    width = refs[0].shape[1]
    for group in (1, 0):
        outs = refs[3 * group : 3 * group + 3]
        olds = before[3 * group : 3 * group + 3] if last else None

        @pl.loop(0, width // CHUNK)
        def _(step, group=group, outs=outs, olds=olds):
            here = pl.ds(pl.multiple_of(step * CHUNK, CHUNK), CHUNK)
            there = pl.ds(pl.multiple_of(group * width + step * CHUNK, CHUNK), CHUNK)
            made = (dot(turned[...], pre[:, there]), dot(grad[...], hidden[:, there]))
            for side in range(2):
                for k in range(2 * half // block):
                    rows = slice(k * block, (k + 1) * block)
                    start = side * half + k // 2 * block
                    part = made[k % 2][start : start + block]
                    if last:
                        part = part + olds[side][rows, here].astype(F32)
                    outs[side][rows, here] = part.astype(BF)
            column = jnp.sum(pre[:, there].astype(F32), axis=0, keepdims=True)
            outs[2][:, here] = column + olds[2][:, here] if last else column


def weights_grad(turned, grad_turned, hidden, pre, before, block):
    d = turned.shape[0]
    width = hidden.shape[1] // 2
    made = [jax.ShapeDtypeStruct((d, width), BF)] * 2 + [jax.ShapeDtypeStruct((1, width), F32)]
    return pl.pallas_call(
        functools.partial(weights_kernel, bool(before), block),
        in_specs=[VMEM] * (4 + len(before)),
        out_specs=[VMEM] * 6,
        out_shape=made * 2,
        input_output_aliases={4 + k: k for k in range(len(before))},
        compiler_params=pltpu.CompilerParams(vmem_limit_bytes=LIMIT),
        cost_estimate=COST,
        name="weights_grad",
    )(turned, grad_turned, hidden, pre, *before)


def middle_kernel(back_a, back_b, mid_ref, grad_ref, gain, full_ref, short_ref, sums_ref):
    unit, scale = norm(mid_ref[...])
    back = back_a[...] + back_b[...].astype(F32)
    grad = grad_ref[...].astype(F32)
    full = grad + norm_back(back * gain[...], unit, scale)
    full_ref[...] = full
    short_ref[...] = full.astype(BF)
    sums_ref[...] = jnp.zeros_like(sums_ref)
    sums_ref[0:1] = jnp.sum(back * unit, axis=0, keepdims=True)
    sums_ref[1:2] = jnp.sum(back, axis=0, keepdims=True)
    sums_ref[2:3] = jnp.sum(full, axis=0, keepdims=True)
    sums_ref[3:4] = jnp.sum(grad, axis=0, keepdims=True)


def middle(back_a, back_b, mid, grad, gain):
    n, d = mid.shape
    return pl.pallas_call(
        middle_kernel,
        in_specs=[VMEM] * 5,
        out_specs=[VMEM] * 3,
        out_shape=[
            jax.ShapeDtypeStruct((n, d), F32),
            jax.ShapeDtypeStruct((n, d), BF),
            jax.ShapeDtypeStruct((8, d), F32),
        ],
        compiler_params=pltpu.CompilerParams(vmem_limit_bytes=LIMIT),
        cost_estimate=COST,
        name="middle",
    )(back_a, back_b, mid, grad, gain)


def back_kernel(first_near, blocks, last_call, table, made_ref, key_ref, row_ref, total_ref, w_ref, short_a, short_b, *refs):
    if last_call:
        before_ref, dq_ref, out_ref, d_ref, p_ref, dp_ref, columns_ref, sum_ref = refs
        sum_ref[...] = before_ref[...]
    else:
        dq_ref, sum_ref, d_ref, p_ref, dp_ref, columns_ref = refs
        sum_ref[...] = jnp.zeros_like(sum_ref)
    key_columns(key_ref, columns_ref)
    scale = HEAD ** (-0.5)
    n = blocks * BLOCK
    for slot, short in enumerate((short_a, short_b)):
        d_ref[slot * n : (slot + 1) * n] = dot(short[...], w_ref[...]).astype(BF)

    @pl.loop(0, 2 * blocks)
    def _(step):
        here = pl.ds(pl.multiple_of(step * BLOCK, BLOCK), BLOCK)
        number, own, first, last = block_places(table, first_near, step, blocks)
        rows = pl.ds(own, BLOCK)
        q_all = split_heads(made_ref[rows, 0:128], made_ref[rows, 384:512], True)
        d_all = split_heads(d_ref[here, 128:256], d_ref[here, 0:128], False)
        row = row_ref[pl.ds(number, 1), :]
        totals = [total_ref[h : h + 1, here] for h in range(3)]

        def weigh(j, inners):
            start = pl.multiple_of(j * BLOCK, BLOCK)
            spot = pl.ds(start, BLOCK)
            bias = pair_bias(columns_ref, row, own, start)
            new, add_v = [], []
            for h in range(3):
                keys = made_ref[spot, 128:256] if h < 2 else made_ref[spot, 512:640]
                values = made_ref[spot, 256:384] if h < 2 else made_ref[spot, 384:512]
                p = jnp.exp(dot_t(keys, q_all[h]) + bias - totals[h])
                d_p = dot_t(values, d_all[h])
                p_ref[h, j] = p
                dp_ref[h, j] = d_p
                new.append(inners[h] + jnp.sum((p * d_p).reshape(BLOCK // 8, 8, BLOCK), axis=0))
                add_v.append(dot(p.astype(BF), d_all[h]))
            sum_ref[spot, 128:256] += add_v[0] + add_v[1]
            sum_ref[spot, 256:384] += add_v[2]
            return tuple(new)

        inners = lax.fori_loop(first, last, weigh, (jnp.zeros((8, BLOCK), F32),) * 3)
        inners = [jnp.sum(v, axis=0, keepdims=True) for v in inners]

        def turn(j, sums):
            spot = pl.ds(pl.multiple_of(j * BLOCK, BLOCK), BLOCK)
            pair_t, third_t = made_ref[spot, 128:256].T, made_ref[spot, 512:640].T
            turned = (pair_t[:HEAD], pair_t[HEAD:], third_t[:HEAD])
            new, add_k = [], []
            for h in range(3):
                d_s = (p_ref[h, j] * (dp_ref[h, j] - inners[h])).astype(BF)
                add_k.append(dot(d_s, q_all[h]))
                new.append(sums[h] + dot(turned[h], d_s))
            sum_ref[spot, 0:128] += add_k[0] + add_k[1]
            sum_ref[spot, 384:512] += add_k[2]
            return tuple(new)

        sums = lax.fori_loop(first, last, turn, (jnp.zeros((HEAD, BLOCK), F32),) * 3)
        two = jnp.concatenate([sums[0], sums[1]], axis=0).T.astype(BF) * jnp.asarray(scale, BF)
        one = jnp.concatenate([sums[2], jnp.zeros_like(sums[2])], axis=0).T.astype(BF) * jnp.asarray(scale, BF)
        dq_ref[here, :] = two
        sum_ref[rows, 256:384] += one.astype(F32)

    if last_call:
        out_ref[...] = sum_ref[...].astype(BF)


def attend_back(first_near, table, made, key, row, total, w, shorts, before):
    keys = made.shape[0]
    n = keys // 4
    last_call = before is not None
    operands = [table, made, key, row, total, w, *shorts] + ([before] if last_call else [])
    scores = pltpu.VMEM((3, keys // BLOCK, BLOCK, BLOCK), F32)
    scratch = [pltpu.VMEM((2 * n, 256), BF), scores, scores, pltpu.VMEM((keys, 128), jnp.int32)]
    if last_call:
        scratch.append(pltpu.VMEM((keys, 512), F32))
    return pl.pallas_call(
        functools.partial(back_kernel, first_near, n // BLOCK, last_call),
        in_specs=[SMEM] + [VMEM] * (len(operands) - 1),
        out_specs=[VMEM] * 2,
        out_shape=[
            jax.ShapeDtypeStruct((2 * n, 128), BF),
            jax.ShapeDtypeStruct((keys, 512), BF if last_call else F32),
        ],
        scratch_shapes=scratch,
        compiler_params=pltpu.CompilerParams(vmem_limit_bytes=LIMIT),
        cost_estimate=COST,
        name="attend_back",
    )(*operands)


def unit_back_kernel(table, dkv_ref, dq_a, dq_b, w_hbm, out_a, out_b, out_c, out_d, w_ref, sems):
    (going,) = stage([w_hbm], [w_ref], sems)
    going.wait()
    n = out_a.shape[0]
    for near, out in enumerate((out_a, out_b, out_c, out_d)):
        here = pl.ds(pl.multiple_of((table[0] ^ near) * n, n), n)
        dq = (dq_a, dq_b)[near // 2][near % 2 * n : (near % 2 + 1) * n]
        out[...] = (dot_t(dkv_ref[here, :], w_ref[:, 128:640]) + dot_t(dq, w_ref[:, 0:128])).astype(BF)


def unit_back(table, w, dqs, dkv):
    n, d = dqs[0].shape[0] // 2, w.shape[0]
    return pl.pallas_call(
        unit_back_kernel,
        in_specs=[SMEM] + [VMEM] * 3 + [HBM],
        out_specs=[VMEM] * 4,
        out_shape=[jax.ShapeDtypeStruct((n, d), BF)] * 4,
        scratch_shapes=buffers_of([w]),
        compiler_params=pltpu.CompilerParams(vmem_limit_bytes=LIMIT),
        cost_estimate=COST,
        name="unit_back",
    )(table, dkv, *dqs, w)


def grads_kernel(rows, base, table, dkv_ref, dq_a, dq_b, *refs):
    sources, refs = refs[:7], refs[7:]
    keep_ref, send_ref, column_ref, sum_ref, turned_ref, shorts, contexts, dqs, sems = refs
    n = shorts.shape[1]
    half = keep_ref.shape[0]
    targets = [dqs.at[: 2 * n], dqs.at[2 * n :], turned_ref, *[shorts.at[k] for k in range(4)]]
    targets += [contexts.at[: 2 * n], contexts.at[2 * n :]]
    for copy in stage((dq_a, dq_b, *sources), targets, sems):
        copy.wait()
    sum_ref[:, 128:640] = dot(turned_ref[...], dkv_ref[...])
    column_ref[:, 128:640] = jnp.sum(dkv_ref[...].astype(F32), axis=0, keepdims=True)
    column_ref[:, 0:128] = jnp.sum(dqs[...].astype(F32), axis=0, keepdims=True)
    sum_ref[:, 0:128] = jnp.zeros_like(sum_ref[:, 0:128])
    sum_ref[:, 640:768] = jnp.zeros_like(sum_ref[:, 640:768])

    @pl.loop(0, 4)
    def _(near):
        here = pl.ds(pl.multiple_of((table[0] ^ near) * n, n), n)
        own = pl.ds(pl.multiple_of(near * n, n), n)
        sum_ref[:, 0:128] += dot(turned_ref[:, here], dqs[own, :])
        out = t_dot(shorts[near], contexts[own, :])
        for k in range(out.shape[0] // rows):
            spot = pl.ds(pl.multiple_of(table[base + k], rows), rows)
            sum_ref[spot, 512:768] += out[k * rows : (k + 1) * rows]

    keep_ref[...] = sum_ref[:half, :].astype(BF)
    send_ref[...] = sum_ref[half:, :].astype(BF)


def grads(table, turned, dqs, dkv, shorts, contexts, rows, base):
    d = turned.shape[0]
    n = shorts[0].shape[0]
    return pl.pallas_call(
        functools.partial(grads_kernel, rows, base),
        in_specs=[SMEM] + [VMEM] * 3 + [HBM] * 7,
        out_specs=[VMEM] * 3,
        out_shape=[jax.ShapeDtypeStruct((d // 2, 768), BF)] * 2 + [jax.ShapeDtypeStruct((1, 640), F32)],
        scratch_shapes=[
            pltpu.VMEM((d, 768), F32),
            pltpu.VMEM(turned.shape, BF),
            pltpu.VMEM((4, n, d), BF),
            pltpu.VMEM((4 * n, 256), BF),
            pltpu.VMEM((4 * n, 128), BF),
            pltpu.SemaphoreType.DMA((9,)),
        ],
        compiler_params=pltpu.CompilerParams(vmem_limit_bytes=60 << 20),
        cost_estimate=COST,
        name="grads",
    )(table, dkv, *dqs, turned, *shorts, *contexts)


def final_kernel(one_ref, core_ref, two_ref, stream_ref, full_ref, gain, early_ref, col_a, col_b, col_one, grad_ref, sums_ref):
    step = pl.program_id(0)

    @pl.when(step == 0)
    def _():
        sums_ref[...] = jnp.zeros_like(sums_ref)
        sums_ref[3:7] = early_ref[0:4]
        sums_ref[7:8] = col_b[...]
        sums_ref[8:9] = col_a[...]
        sums_ref[9:10, : col_one.shape[1]] = col_one[...]

    back = one_ref[...].astype(F32) + core_ref[...].astype(F32) + two_ref[...].astype(F32)
    unit, scale = norm(stream_ref[...])
    grad = full_ref[...] + norm_back(back * gain[...], unit, scale)
    grad_ref[...] = grad
    sums_ref[0:1] += jnp.sum(back * unit, axis=0, keepdims=True)
    sums_ref[1:2] += jnp.sum(back, axis=0, keepdims=True)
    sums_ref[2:3] += jnp.sum(grad, axis=0, keepdims=True)


def small_call(kernel, shapes, limit=LIMIT):
    def call(*operands):
        return pl.pallas_call(
            kernel,
            in_specs=[VMEM] * len(operands),
            out_specs=[VMEM] * len(shapes),
            out_shape=[jax.ShapeDtypeStruct(shape, F32) for shape in shapes],
            compiler_params=pltpu.CompilerParams(vmem_limit_bytes=limit),
            cost_estimate=COST,
            name=getattr(kernel, "__name__", "finish"),
        )(*operands)

    return call


def core_sums(own, there, out):
    out[0:7] = own[0:7] + there[0:7]
    out[7:8] = own[8:9] + there[7:8]
    out[8:9] = own[9:10]
    out[9:16] = jnp.zeros_like(own[9:16])


def row_sums(own, there, seat, spread, out):
    dp = seat.shape[0]
    both = own[0:7] + there[0:7]
    out[0:2] = both[0:2]
    out[2:6] = both[3:7]
    out[6:8] = own[7:9]
    out[8 : 8 + dp] = seat[...] * both[2:3]
    out[8 + dp : 8 + dp + spread.shape[0]] = spread[...]


def finish_kernel(dp, features, columns, count, *refs):
    parts, (pick, gain_ref, bias_ref, query_ref, value_ref, up_ref, time_ref) = refs[:count], refs[count:]
    total = parts[0][...]
    for part in parts[1:]:
        total = total + part[...]
    by_sequence = total[8 : 8 + dp]
    gain_ref[0:1] = total[0:1]
    gain_ref[1:2] = total[2:3]
    bias_ref[0:1] = total[1:2]
    bias_ref[1:4] = total[3:6]
    bias_ref[4:5] = jnp.sum(by_sequence, axis=0, keepdims=True)
    up_ref[...] = total[6:7]
    query_ref[...] = jnp.concatenate([total[7:8, 0:128], total[7:8, 384:448]], axis=1)
    value_ref[...] = jnp.concatenate([total[7:8, 256:384], total[7:8, 448:512]], axis=1)
    wide = total.shape[1] // features
    rows = [total[8 + dp + k // wide : 9 + dp + k // wide, k % wide * features : (k % wide + 1) * features] for k in range(dp)]
    share = jnp.dot(by_sequence, pick[...], precision=highest, preferred_element_type=F32)
    time_ref[...] = lax.dot_general(
        jnp.concatenate(rows, axis=0), share, (((0,), (0,)), ((), ())), precision=highest, preferred_element_type=F32
    )


def final(one, core, two, stream, full, gain, early, cols, col_one):
    n, d = stream.shape
    rows = pl.BlockSpec((n // 4, d), lambda i: (i, 0))
    small = (gain, early, *cols, col_one)
    return pl.pallas_call(
        final_kernel,
        grid=(4,),
        in_specs=[rows] * 5 + [whole(v.shape) for v in small],
        out_specs=[rows, whole((16, d))],
        out_shape=[jax.ShapeDtypeStruct((n, d), F32), jax.ShapeDtypeStruct((16, d), F32)],
        compiler_params=params("arbitrary", limit=60 << 20),
        cost_estimate=COST,
        name="final",
    )(one, core, two, stream, full, *small)


def add_kernel(*refs):
    total = refs[0][...].astype(F32)
    for ref in refs[1:-1]:
        total = total + ref[...].astype(F32)
    refs[-1][...] = total.astype(refs[-1].dtype)


def low_sum(*terms, rows=None, dtype=BF):
    terms = [v if isinstance(v, tuple) else (v, 0) for v in terms]
    rows = rows or min(v.shape[0] for v, _ in terms)
    block = rows // (4 if rows % 64 == 0 else 1)
    width = terms[0][0].shape[1]
    return pl.pallas_call(
        add_kernel,
        grid=(rows // block,),
        in_specs=[
            pl.BlockSpec((block, width), functools.partial(lambda first, i: (i + first, 0), start // block))
            for _, start in terms
        ],
        out_specs=pl.BlockSpec((block, width), lambda i: (i, 0)),
        out_shape=jax.ShapeDtypeStruct((rows, width), dtype),
        compiler_params=params("arbitrary"),
        cost_estimate=COST,
        name="low_sum",
    )(*[v for v, _ in terms])


def stack_kernel(*refs):
    for k, ref in enumerate(refs[:-1]):
        refs[-1][k] = ref[...]


def stack(values):
    return pl.pallas_call(
        stack_kernel,
        in_specs=[VMEM] * len(values),
        out_specs=VMEM,
        out_shape=jax.ShapeDtypeStruct((len(values),) + values[0].shape, values[0].dtype),
        compiler_params=pltpu.CompilerParams(vmem_limit_bytes=LIMIT),
        cost_estimate=COST,
        name="stack",
    )(*values)


def tie(values, after):
    return lax.optimization_barrier((values, after))[0]


def line_sums(terms, starts, size, rows):
    found = [[(v, start + by * rows) for v, start in zip(terms, starts, strict=True)] for by in range(size)]
    return low_sum(*found[0], rows=rows, dtype=F32), [low_sum(*pairs, rows=rows) for pairs in found[1:]]


def along_line(sent, size):
    return [shift(v, "d1", size, by + 1) for by, v in enumerate(sent)]


def scatter_dp(value):
    return lax.psum_scatter(value, ("d1", "d0"), scatter_dimension=0, tiled=True).astype(F32)


def shards(
    inputs,
    segment_ids,
    keep_mask,
    timestep,
    w_qkv,
    b_query,
    b_value,
    w_out,
    w_up,
    b_up,
    w_down,
    time_weight,
    gains,
    row_biases,
    d_out,
):
    size = lax.axis_size("d1")
    long = size > 4
    z, x = lax.axis_index("d1"), lax.axis_index("d0")
    own = lax.axis_index("t1") * 2 + lax.axis_index("t0")
    n, d = inputs.shape
    dp = 2 * size
    place = z * 2 + x
    features = time_weight.shape[0]
    columns = time_weight.shape[1]

    rows = w_up.shape[0]
    blocks = 4 * n // BLOCK
    ids = segment_ids.reshape(blocks, BLOCK)
    first = jnp.sum(segment_ids[None, :] < ids[:, :1], axis=1, dtype=jnp.int32)
    last = jnp.sum(segment_ids[None, :] <= ids[:, -1:], axis=1, dtype=jnp.int32)
    span = jnp.stack([first // BLOCK, (last + BLOCK - 1) // BLOCK], axis=1).reshape(-1)
    slots = [(lax.rem(z - s + size, size) * 2 + (x ^ a)) * rows for a in range(2) for s in range(size)]
    places = [((k % 2 ^ x) * size + k // 2) * rows for k in range(dp)]
    slots_two = [(s * 2 + (x ^ a)) * rows for a in range(2) for s in range(size)]
    if long:
        nothing = [jnp.zeros_like(own)]
        slots, places, slots_two, turn_rows = nothing, nothing, nothing, d
    else:
        turn_rows = rows
    base = 1 + len(slots)
    slot_two = base + len(places)
    table_one = jnp.stack([own, *slots, *places, *slots_two]).astype(jnp.int32)
    table_two = jnp.concatenate([jnp.stack([own]), span]).astype(jnp.int32)
    key = jnp.where(keep_mask > 0, segment_ids, -1).reshape(blocks, BLOCK)
    own_keep = lax.dynamic_slice_in_dim(keep_mask, own * n, n, 0)[:, None]
    up_core = swap(b_up[None], "t0")
    grad_two, grad_turned = cotangent(table_one, d_out[None], own_keep, turn_rows, base)

    pack_one = jnp.concatenate(
        [pack_columns(w_qkv[0], w_qkv[1], w_qkv[2]), time_weight.T, pack_outer(w_out.T)], axis=1
    )
    rows = pack_one.shape[0]
    if long:
        half = lax.all_gather(pack_one, ("d1", "d0"), axis=0, tiled=True)
        pieces_one = [(half, None, 0)]
    else:
        line = [pack_one] + [shift(pack_one, "d1", size, by) for by in range(1, size)]
    x_core = swap(inputs, "t0")
    x_far_a = swap(inputs[: n // 2], "t1")
    if not long:
        half = stack(tie(line, (x_core, grad_two, grad_turned, key, x_far_a)))
        other_half = swap(half, "d0")
        pieces_one = [(half, (s, 0), s) for s in range(size)] + [(other_half, (s, 0), size + s) for s in range(size)]
    x_far_b = tie(swap(inputs[n // 2 :], "t1"), half)
    x_near = [inputs, x_core, x_far_a, x_far_b, swap(x_far_a, "t0"), swap(x_far_b, "t0")]
    time_rows = sinusoid(timestep, features).astype(BF)
    times = jnp.pad(time_rows, ((0, 7), (0, 0)))
    seat = (jnp.arange(dp) == place).astype(F32)[:, None]
    spread = (seat * time_rows.astype(F32)).reshape(1, -1)
    spread = jnp.pad(spread, ((0, 0), (0, -spread.shape[1] % d))).reshape(-1, d)
    bias_one = pack_columns(b_query, jnp.zeros_like(b_query), b_value)[None, :]

    scale = jnp.where(
        (jnp.arange(640) < 128) | ((jnp.arange(640) >= 384) & (jnp.arange(640) < 448)), HEAD ** (-0.5), 1.0
    ).astype(F32)[None, :]

    far_keep = lax.dynamic_slice_in_dim(keep_mask, (own ^ 2) * n, n, 0)[:, None]
    d_far = swap(tie(d_out, x_far_b), "t1")
    d_far = swap(tie(d_out, x_far_b), "t1")

    if long:
        gathered = lax.all_gather(jnp.stack([w_up, w_down.T]), ("d1", "d0"), axis=1, tiled=True)
        other = swap(gathered, "t0")
        feed_weights = [tuple([(v[k], None, 0)] for k in range(2)) for v in (gathered, other)]
        rows_two = d
    else:
        gathered = lax.all_gather(tie(jnp.concatenate([w_up, w_down.T]), half), "d1")
        x_near = tie(x_near, up_core)
    made, turned_one, stream_in, w_one, outer_own = project(
        x_near, times, row_biases[4:5], gains[0:1], row_biases[0:1], bias_one, scale, pieces_one, d if long else rows,
        table_one, turn_rows, base,
    )
    outer_near = gather_near(outer_own)
    made_near = made_far = made
    if not long:
        gathered = tie(gathered, made)
        gathered_side, gathered_core = swap(gathered, "d0"), swap(gathered, "t0")
    context_far, total_far = attend(2, table_two, made_far, key, ids)
    context_over = swap(context_far, "t1")
    if not long:
        made_near = tie(made, (d_far, gathered_core))
    context_near, total_near = attend(0, table_two, made_near, key, ids)
    grad_far, grad_turned_far = cotangent(table_one, tie(d_far, context_near)[None], far_keep, turn_rows, base)
    context_over = tie(context_over, grad_far if long else (grad_far, gathered_side))
    contexts = [context_near, swap(context_near, "t0"), context_over, swap(context_over, "t0")]
    if not long:
        def pieces_of(near, other, part):
            return [(v, (s, part), a * size + s) for a, v in enumerate((near, other)) for s in range(size)]

        pairs = ((gathered, gathered_side), (gathered_core, swap(gathered_side, "t0")))
        feed_weights = [tuple(pieces_of(*pair, part) for part in range(2)) for pair in pairs]
        rows_two = rows
    stream_mid, unit_two = outer(
        table_one, contexts, outer_near, stream_in, gains[1:2], row_biases[1:2], row_biases[2:3]
    )

    biases = jnp.concatenate([b_up[None], up_core], axis=1)
    block = d // 2 if long else rows
    unit_far = swap(unit_two, "t1")
    hidden, pre, out, back, turned_two, *feed_arrays = feed(
        table_one, unit_two, grad_two, biases, feed_weights, rows_two, turn_rows, base, slot_two, F32
    )
    own_grads = weights_grad(turned_two, grad_turned, hidden, pre, [], block)
    hidden_far, pre_far, out_far, back_far, turned_far = feed(
        table_one, tie(unit_far, own_grads), grad_far, biases, feed_arrays, rows_two, turn_rows, base, slot_two, BF
    )
    back_over = swap(back_far, "t1")
    part = d // 2
    keep_a, send_a, column_a, keep_b, send_b, column_b = weights_grad(turned_far, grad_turned_far, hidden_far, pre_far, own_grads, block)
    keep_b, send_b = to_core((keep_b, send_b))
    full, short, sums_two = middle(back, back_over, stream_mid, grad_two, gains[1:2])
    short_core, short_over = swap(short, "t0"), swap(short, "t1")
    send_b = tie(send_b, short)
    sent = low_sum(send_a, send_b)
    over = sent if long else swap(sent, "d0")
    shorts = tie([short, short_core], sent)
    dq_near, sum_near = attend_back(0, table_two, made, key, ids, total_near, outer_own, shorts, None)
    short_over = tie(short_over, sum_near)
    shorts = [short_over, swap(short_over, "t0")]
    short_near = [short, short_core] + shorts
    if long:
        kept = low_sum(keep_a, keep_b)
        up_share = scatter_dp(jnp.concatenate([kept[:part], sent[:part]]))
        down_share = scatter_dp(jnp.concatenate([kept[part:], sent[part:]]))
    dq_far, dkv = attend_back(2, table_two, made, key, ids, total_far, outer_own, shorts, sum_near)
    if not long:
        kept = low_sum(keep_a, keep_b, tie(over, dkv))
        both_share = lax.psum_scatter(kept, "d1", scatter_dimension=0, tiled=True)
        dkv = tie(dkv, kept)
    out_over, dkv = tie((swap(tie(out_far, short_over), "t1"), dkv), dkv)
    back_a, back_b, back_c, back_d = unit_back(table_one, w_one, [dq_near, dq_far], dkv)
    back_d, back_b = swap(back_d, "t0"), swap(back_b, "t0")
    back_far = low_sum(back_c, back_d)
    other = swap(back_far, "t1")
    grad_keep, grad_send, column_one = grads(
        table_one, turned_one, tie([dq_near, dq_far], back_far), dkv, short_near, [context_near, context_far], turn_rows, base
    )
    if long:
        one_share = scatter_dp(jnp.concatenate([grad_keep, grad_send]))
    else:
        grad_over = swap(grad_send, "d0")
    grad_input, small = final(
        back_a, back_b, other, stream_in, full, gains[0:1], sums_two, (column_a, column_b), column_one
    )

    out_over = tie(out_over, small)
    output = (stream_mid + out + out_over.astype(F32) + row_biases[3]).astype(BF)

    if not long:
        one_sum = (grad_keep.astype(F32) + tie(grad_over, small).astype(F32)).astype(BF)
        one_share = lax.psum_scatter(one_sum, "d1", scatter_dimension=0, tiled=True).astype(F32)

    (small,) = small_call(core_sums, [(16, d)])(small, swap(small, "t0"))
    height = 8 + dp + spread.shape[0]
    (small,) = small_call(row_sums, [(height, d)])(small, swap(small, "t1"), seat, spread)
    small = small + swap(small, "d0")
    parts = [lax.psum(small, "d1")] if long else [small] + [shift(small, "d1", size, by) for by in range(1, size)]
    if not long:
        up_share, down_share = both_share[:rows].astype(F32), both_share[rows:].astype(F32).T
        parts, up_share, down_share = lax.optimization_barrier((parts, up_share, down_share))
        down_share = down_share.T
    pick = (jnp.arange(d)[:, None] == place * columns + jnp.arange(columns)[None, :]).astype(F32)
    width = b_query.shape[0]
    gain_total, bias_total, column_query, column_value, up_bias, grad_time = small_call(
        functools.partial(finish_kernel, dp, features, columns, len(parts)),
        [(2, d), (5, d), (1, width), (1, width), (1, d), (features, columns)],
    )(*parts, pick)
    d_query, d_key, d_value, d_outer = unpack_columns(one_share)
    return (
        output,
        grad_input,
        jnp.stack([d_query, d_key, d_value]),
        column_query[0],
        column_value[0],
        d_outer.T,
        up_share,
        up_bias[0],
        down_share.T,
        grad_time,
        gain_total,
        bias_total,
    )


def solution(mesh):
    dp, tensor = mesh.shape["dp"], mesh.shape["tensor"]
    fine = Mesh(mesh.devices.reshape(dp // 2, 2, tensor // 2, 2), ("d1", "d0", "t1", "t0"))
    rows, cols = ("d1", "d0"), ("t1", "t0")
    every = rows + cols
    in_specs = (
        P(every, None),
        P(rows),
        P(rows),
        P(rows),
        P(None, rows, cols),
        P(cols),
        P(cols),
        P(cols, rows),
        P(rows, cols),
        P(cols),
        P(cols, rows),
        P(None, rows),
        P(),
        P(),
        P(every, None),
    )
    out_specs = (
        P(every, None),
        P(every, None),
        P(None, rows, cols),
        P(cols),
        P(cols),
        P(cols, rows),
        P(rows, cols),
        P(cols),
        P(cols, rows),
        P(None, rows),
        P(),
        P(),
    )
    return jax.shard_map(shards, mesh=fine, in_specs=in_specs, out_specs=out_specs, check_vma=False)
```
